256 devices in a mesh: gx: 4 (over y), gy: 16 (over z, core), gz: 4 (over x).
Axes of the slice: x: 4, y: 4, z: 8, core: 2. Of those that a mesh axis runs over, the one named last changes fastest.
Arguments:
- frac: float32 [3, 4, 16, 8, 128], P(None, 'gx', 'gy', 'gz'), may hold values from 0 to 1
- velocity: float32 [3, 4, 16, 8, 128], P(None, 'gx', 'gy', 'gz'), may hold values from -2 to 2
- force_old: float32 [3, 4, 16, 8, 128], P(None, 'gx', 'gy', 'gz'), may hold values from -6 to 6
- species: int32 [4, 16, 8, 128], P('gx', 'gy', 'gz'), may hold values from 0 to 9
- cell_count: int32 [4, 16, 8], P('gx', 'gy', 'gz'), may hold values from 1 to 128, as said below
- neighbours: int32 [16, 4, 16, 8, 128], P(None, 'gx', 'gy', 'gz'), may hold values from 0 to 3455, as said below
- embed: bfloat16 [10, 64], replicated, may hold values from -6 to 6
- w_radial_in: bfloat16 [8, 64], replicated, may hold values from -2 to 2
- w_radial_out: bfloat16 [64, 192], replicated, may hold values from -0.75 to 0.75
- w_node: bfloat16 [256, 64], replicated, may hold values from -0.375 to 0.375
- w_energy: float32 [64], replicated, may hold values from -0.75 to 0.75
Outputs:
- next_frac: float32 [3, 4, 16, 8, 128], P(None, 'gx', 'gy', 'gz')
- next_velocity: float32 [3, 4, 16, 8, 128], P(None, 'gx', 'gy', 'gz')
- next_force: float32 [3, 4, 16, 8, 128], P(None, 'gx', 'gy', 'gz')
- site_energy: float32 [4, 16, 8, 128], P('gx', 'gy', 'gz')
The draws below stay inside these ranges and needn't reach their ends.
Inputs may be any that keep to these rules, and one draw needn't show every extreme that they name: `cell_count`: in every draw at least one cell holds exactly 128 atoms; the other cells hold 1 to 128. `neighbours`: each code o * 128 + s names slot s of the cell at offset (o // 9 - 1, (o // 3) % 3 - 1, o % 3 - 1) from the receiver's cell, periodic; s is below that cell's count; no code names the receiver itself.
All inputs are finite; a program needn't handle non-finite values.
Results may differ from the reference program's by a relative error of at most 0.015.
Values may be sent and summed in bfloat16 or wider, within the bound.
No kernel may reach another device: no remote copies, remote signals or barrier semaphores. Data moves between devices by JAX's collectives and lax.ppermute only.
A program may use at most 64 MiB of HBM per device.

```python
import math
import jax
import jax.numpy as jnp
import numpy as np
from jax import lax

CH = 64
NB = 8
NSPEC = 10
K = 16
CAP = 128
NX = 4
NY = 16
NZ = 8


def count_field(key):
    key_a, key_b, key_c, key_d = jax.random.split(key, 4)
    first = jax.random.randint(key_a, (NX, NY, NZ), 1, CAP + 1)
    second = jax.random.randint(key_b, (NX, NY, NZ), 1, CAP + 1)
    base = 1 + first * second // CAP
    centre = jax.random.randint(key_c, (3,), 0, 1 << 20)
    grid_a = jnp.arange(NX, dtype=jnp.int32)[:, None, None]
    grid_b = jnp.arange(NY, dtype=jnp.int32)[None, :, None]
    grid_c = jnp.arange(NZ, dtype=jnp.int32)[None, None, :]
    dist_a = (grid_a - centre[0] % NX) % NX
    dist_b = (grid_b - centre[1] % NY) % NY
    dist_c = (grid_c - centre[2] % NZ) % NZ
    inside_a = jnp.minimum(dist_a, NX - dist_a) < max(NX // 4, 1)
    inside_b = jnp.minimum(dist_b, NY - dist_b) < max(NY // 4, 1)
    inside_c = jnp.minimum(dist_c, NZ - dist_c) < max(NZ // 4, 1)
    dense = inside_a & inside_b & inside_c
    counts = jnp.minimum(jnp.where(dense, 3 * base, base), CAP)
    chosen = jax.random.randint(key_d, (), 0, NX * NY * NZ)
    counts = counts.reshape(-1).at[chosen].set(CAP).reshape(NX, NY, NZ)
    return counts.astype(jnp.int32)


def draw_cell_count(key, part):
    return count_field(jax.random.fold_in(key, 7))


def draw_neighbours(key, part):
    counts = count_field(jax.random.fold_in(key, 7))
    key_a, key_b, key_c = jax.random.split(jax.random.fold_in(key, 8), 3)
    shape = (K, NX, NY, NZ, CAP)
    nearby = jax.random.randint(key_a, shape, 0, 2)
    spread = jax.random.randint(key_b, shape, 0, 27)
    offset = jnp.where(nearby == 0, 13, spread)
    grid_a = jnp.arange(NX, dtype=jnp.int32)[None, :, None, None, None]
    grid_b = jnp.arange(NY, dtype=jnp.int32)[None, None, :, None, None]
    grid_c = jnp.arange(NZ, dtype=jnp.int32)[None, None, None, :, None]
    slot_grid = jnp.arange(CAP, dtype=jnp.int32)[None, None, None, None, :]
    target = counts[(grid_a + offset // 9 - 1) % NX, (grid_b + offset // 3 % 3 - 1) % NY, (grid_c + offset % 3 - 1) % NZ]
    picked = jax.random.randint(key_c, shape, 0, 65536)
    slot_id = picked * target // 65536
    itself = (offset == 13) & (slot_id == slot_grid)
    offset = jnp.where(itself, 14, offset)
    slot_id = jnp.where(itself, 0, slot_id)
    return (offset * CAP + slot_id).astype(jnp.int32)


def set_ends(values, own_key, smallest, high):
    longest = values.shape.index(max(values.shape))
    spots = []
    for shift in (0, 1):
        where = [jax.random.randint(jax.random.fold_in(own_key, axis), (), 0, length) for axis, length in enumerate(values.shape)]
        where[longest] = (where[longest] + shift) % values.shape[longest]
        spots.append(tuple(where))
    return values.at[spots[0]].set(smallest).at[spots[1]].set(high)


def block_levels(key, shape, pieces, least, top_value):
    def one(axis_at, parts):
        heights = jax.random.uniform(jax.random.fold_in(jax.random.fold_in(key, 6), axis_at), (parts,), jnp.float32, least / len(pieces), top_value / len(pieces))
        return jnp.repeat(jnp.exp(heights), shape[axis_at] // parts).reshape((-1,) + (1,) * (len(shape) - axis_at - 1))

    loudness = one(*pieces[0])
    for cut in pieces[1:]:
        loudness = loudness * one(*cut)
    return loudness


def cumulative_ranks(amount, slope):
    loads = [(1 << 20) // math.isqrt(rank ** slope) + 1 for rank in range(1, amount + 1)]
    scale = 1 + sum(loads) // (1 << 30)
    return np.cumsum(np.array([max(1, weight // scale) for weight in loads]))


def skewed_ids(stream_key, extent, count, skew):
    table = cumulative_ranks(count, skew)
    pick = jax.random.randint(jax.random.fold_in(stream_key, 1), extent, 0, int(table[count - 1]))
    grade = jnp.searchsorted(jnp.asarray(table, jnp.int32), pick, side="right")
    return jax.random.permutation(jax.random.fold_in(stream_key, 2), count)[grade].astype(jnp.int32)


def gaussian(own_key, extent, deviation, bound, cuts=(), held_as=jnp.bfloat16):
    gain = block_levels(own_key, extent, cuts, -0.22, 0.18) if cuts else 1.0
    entries = jax.random.normal(own_key, extent, jnp.float32) * deviation * gain
    return jnp.minimum(jnp.maximum(entries, -bound), bound).astype(held_as)


def setup_inputs(seed: int = 0) -> dict:
    seeds = jax.random.split(jax.random.key(seed), 12)
    frac = jnp.clip(1.0 * jax.random.uniform(seeds[0], (3, NX, NY, NZ, CAP), jnp.float32) ** block_levels(seeds[0], (3, NX, NY, NZ, CAP), ((1, 4), (2, 16), (3, 4)), -0.2, 0.2), 0.0, 1.0)
    velocity = gaussian(seeds[1], (3, NX, NY, NZ, CAP), 0.3, 2.0, ((1, 4), (2, 16), (3, 4)), jnp.float32)
    force_old = gaussian(seeds[2], (3, NX, NY, NZ, CAP), 1.0, 6.0, ((1, 4), (2, 16), (3, 4)), jnp.float32)
    species = set_ends(skewed_ids(seeds[3], (NX, NY, NZ, CAP), NSPEC, 2), jax.random.fold_in(seeds[3], 3), 0, NSPEC - 1).astype(jnp.int32)
    cell_count = draw_cell_count(jax.random.fold_in(seeds[11], 71), 0)
    neighbours = draw_neighbours(jax.random.fold_in(seeds[11], 71), 0)
    embed = gaussian(seeds[6], (NSPEC, CH), 1.0, 6.0)
    w_radial_in = gaussian(seeds[7], (NB, CH), NB ** -0.5, 2.0)
    w_radial_out = gaussian(seeds[8], (CH, 3 * CH), CH ** -0.5, 0.75)
    w_node = gaussian(seeds[9], (4 * CH, CH), (4 * CH) ** -0.5, 0.375)
    w_energy = gaussian(seeds[10], (CH,), CH ** -0.5, 0.75, (), jnp.float32)
    return {"frac": frac, "velocity": velocity, "force_old": force_old, "species": species, "cell_count": cell_count, "neighbours": neighbours, "embed": embed, "w_radial_in": w_radial_in, "w_radial_out": w_radial_out, "w_node": w_node, "w_energy": w_energy}


MASSES = (1.008, 12.011, 14.007, 15.999, 32.06, 22.99, 35.45, 39.098, 24.305, 40.078)
SQRT3 = 1.7320508075688772
HALF_SQRT3 = 0.8660254037844386
TIME_STEP = 0.5

def species_mass(species):
    table = jnp.asarray(MASSES, dtype=jnp.float32) / 16.0
    shape_ones = (1,) * species.ndim
    which = species[None] == jnp.arange(len(MASSES), dtype=jnp.int32).reshape((-1,) + shape_ones)
    return lax.optimization_barrier(jnp.sum(jnp.where(which, table.reshape((-1,) + shape_ones), 0.0), axis=0))

def embed_species(species_flat, embed):
    kinds = embed.shape[0]
    onehot = (species_flat[None, :] == jnp.arange(kinds, dtype=jnp.int32)[:, None]).astype(jnp.bfloat16)
    return jnp.dot(embed.T, onehot, preferred_element_type=jnp.float32).astype(jnp.bfloat16)

def site_terms(displace, send_feat, own_feat, w_radial_in, w_radial_out, w_node, w_energy):
    basis_count = w_radial_in.shape[0]
    channels = own_feat.shape[0]
    candidates = displace.shape[1]
    block_size = displace.shape[2]
    squared = lax.optimization_barrier(jnp.sum(displace * displace, axis=0))
    envelope = jnp.maximum(1.0 - squared, 0.0) ** 3
    centres = jnp.arange(basis_count, dtype=jnp.float32) / (basis_count - 1)
    basis_values = jnp.exp(-float((basis_count - 1) ** 2) * (squared[None] - centres[:, None, None]) ** 2)
    basis_values = basis_values.astype(jnp.bfloat16).reshape(basis_count, candidates * block_size)
    hidden = jax.nn.silu(jnp.dot(w_radial_in.T, basis_values, preferred_element_type=jnp.float32)).astype(jnp.bfloat16)
    radial = jnp.dot(w_radial_out.T, hidden, preferred_element_type=jnp.float32)
    radial = radial.reshape(3, channels, candidates, block_size) * envelope[None, None]
    along_x = displace[0]
    along_y = displace[1]
    along_z = displace[2]
    first_order = jnp.stack([along_x, along_y, along_z])
    second_order = jnp.stack([SQRT3 * along_x * along_y, SQRT3 * along_y * along_z, SQRT3 * along_z * along_x, HALF_SQRT3 * (along_x * along_x - along_y * along_y), 0.5 * (2.0 * along_z * along_z - along_x * along_x - along_y * along_y)])
    carried = radial * send_feat.astype(jnp.float32)[None]
    scalar_part = lax.optimization_barrier(jnp.sum(carried[0], axis=1))
    vector_part = lax.optimization_barrier(jnp.sum(carried[1][None] * first_order[:, None], axis=2))
    tensor_part = lax.optimization_barrier(jnp.sum(carried[2][None] * second_order[:, None], axis=2))
    invariant = jnp.concatenate([scalar_part, lax.optimization_barrier(jnp.sum(vector_part * vector_part, axis=0)), lax.optimization_barrier(jnp.sum(tensor_part * tensor_part, axis=0)), own_feat.astype(jnp.float32)], axis=0).astype(jnp.bfloat16)
    activity = jax.nn.silu(jnp.dot(w_node.T, invariant, preferred_element_type=jnp.float32))
    return lax.optimization_barrier(jnp.sum(w_energy[:, None] * activity, axis=0))

def reference(frac, velocity, force_old, species, cell_count, neighbours, embed, w_radial_in, w_radial_out, w_node, w_energy):
    cells_x, cells_y, cells_z, capacity = species.shape
    candidates = neighbours.shape[0]
    total = cells_x * cells_y * cells_z * capacity
    block_size = 16 * capacity
    occupied = (lax.broadcasted_iota(jnp.int32, species.shape, 3) < cell_count[..., None]).astype(jnp.float32)
    atom_mass = species_mass(species)
    half_velocity = velocity + 0.5 * TIME_STEP * force_old / atom_mass
    moved = frac + TIME_STEP * half_velocity
    feats = embed_species(species.reshape(total), embed)
    moved_flat = moved.reshape(3, total)
    codes = neighbours.reshape(candidates, total)
    occupied_flat = occupied.reshape(total)

    def one_block(carried, number):
        forces, energies = carried
        start = number * block_size
        receivers = start + jnp.arange(block_size, dtype=jnp.int32)
        cell_id = receivers // capacity
        cell_a = cell_id // (cells_y * cells_z)
        cell_b = cell_id // cells_z % cells_y
        cell_c = cell_id % cells_z
        packed = lax.dynamic_slice_in_dim(codes, start, block_size, 1)
        offset = packed // capacity
        slot_id = packed % capacity
        shift_a = offset // 9 - 1
        shift_b = offset // 3 % 3 - 1
        shift_c = offset % 3 - 1
        senders = (((cell_a + shift_a) % cells_x * cells_y + (cell_b + shift_b) % cells_y) * cells_z + (cell_c + shift_c) % cells_z) * capacity + slot_id
        cell_shift = jnp.stack([shift_a, shift_b, shift_c]).astype(jnp.float32)
        own_pos = lax.dynamic_slice_in_dim(moved_flat, start, block_size, 1)
        displace = cell_shift + moved_flat[:, senders] - own_pos[:, None, :]
        send_feat = feats[:, senders]
        own_feat = lax.dynamic_slice_in_dim(feats, start, block_size, 1)
        weights = lax.dynamic_slice_in_dim(occupied_flat, start, block_size, 0)

        def energy_of(shifted):
            return site_terms(shifted, send_feat, own_feat, w_radial_in, w_radial_out, w_node, w_energy)
        energy, pullback = jax.vjp(energy_of, displace)
        gradient = pullback(weights)[0]
        forces = forces.at[:, receivers].add(lax.optimization_barrier(jnp.sum(gradient, axis=1)))
        forces = forces.at[:, senders.reshape(-1)].add(-gradient.reshape(3, -1))
        energies = lax.dynamic_update_slice_in_dim(energies, energy, start, 0)
        return ((forces, energies), None)
    start_state = (jnp.zeros((3, total), jnp.float32), jnp.zeros((total,), jnp.float32))
    blocks = jnp.arange(total // block_size, dtype=jnp.int32)
    (forces, energies), _ = lax.scan(one_block, start_state, blocks)
    next_force = occupied * forces.reshape(3, cells_x, cells_y, cells_z, capacity)
    next_velocity = occupied * (half_velocity + 0.5 * TIME_STEP * next_force / atom_mass)
    next_frac = occupied * moved
    site_energy = occupied * energies.reshape(cells_x, cells_y, cells_z, capacity)
    return (next_frac, next_velocity, next_force, site_energy)
```

```python
import jax
import jax.numpy as jnp
from jax import lax
from jax.experimental import pallas as pl
from jax.experimental.pallas import tpu as pltpu
from jax.sharding import PartitionSpec as P

MASSES = (1.008, 12.011, 14.007, 15.999, 32.06, 22.99, 35.45, 39.098, 24.305, 40.078)
SQRT3 = 1.7320508075688772
HALF_SQRT3 = 0.8660254037844386
TIME_STEP = 0.5

K = 16
CAP = 128
R = 2
W = R * CAP
CH = 64
NB = 8
GROUP = 4
F32 = jnp.float32
BF16 = jnp.bfloat16


def swap(array, axis, odd):
    n = lax.axis_size(axis)
    if odd:
        pairs = [(i, (i + 1) % n if i % 2 else (i - 1) % n) for i in range(n)]
    else:
        pairs = [(i, i ^ 1) for i in range(n)]
    return lax.ppermute(array, axis, pairs)


def both(even, to_upper, to_lower, axis):
    if to_upper is to_lower:
        got_a = swap(to_upper, axis, False)
        got_b = swap(to_upper, axis, True)
    else:
        got_a = swap(jnp.where(even, to_upper, to_lower), axis, False)
        got_b = swap(jnp.where(even, to_lower, to_upper), axis, True)
    return jnp.where(even, got_b, got_a), jnp.where(even, got_a, got_b)


def species_mass(species):
    table = [m / 16.0 for m in MASSES]
    mass = jnp.zeros(species.shape, F32)
    for number, value in enumerate(table):
        mass = jnp.where(species == number, jnp.float32(jnp.float32(MASSES[number]) / jnp.float32(16.0)), mass)
    return mass


def rows8(row, width):
    return jnp.broadcast_to(row, (8, width))


def wide(ref, row, height):
    parts = [jnp.broadcast_to(ref[r, pl.ds(row, 1), :], (height, CAP)) for r in range(R)]
    return jnp.concatenate(parts, axis=1)


def core_kernel(
    count_ref, pos_ref, codes_ref, emb_ref, w1_ref, w2_ref, wn_ref, we_ref,
    ghost_ref, own_ref,
    wc_s, w2t_s, wnt_s, embt_s,
    d_s, kd_s, off_s, slot_s, ey_s, exu_s, ds_s, feat_s, q_s, m_s, gr_s, t_s, ts_s, g_s, a_s, s_s,
):
    wc_s[...] = jnp.zeros(wc_s.shape, BF16)
    wc_s[0:CH, 0:NB] = w1_ref[...].astype(F32).T.astype(BF16)
    embt = emb_ref[...].astype(F32).T.astype(BF16)
    wc_s[CH:, NB:NB + 16] = embt
    embt_s[...] = embt
    w2t_s[...] = w2_ref[...].astype(F32).T.astype(BF16)
    wnt_s[...] = wn_ref[...].astype(F32).T.astype(BF16)

    for r in range(R):
        code = codes_ref[pl.ds(r, K, stride=R), :]
        off_s[r] = code // CAP
        slot_s[r] = code % CAP
    zero8 = jnp.zeros((8, CAP), F32)

    def gather_column(col, acc):
        acc = list(acc)
        for r in range(R):
            for h in range(2):
                off = off_s[r, h * 8:(h + 1) * 8, :]
                slot = slot_s[r, h * 8:(h + 1) * 8, :]
                for dz in range(3):
                    hit = off == col * 3 + dz
                    for q in range(4):
                        row = pos_ref[pl.ds(col * 16 + (dz + r) * 4 + q, 1), :]
                        got = jnp.take_along_axis(rows8(row, CAP), slot, axis=1, mode="promise_in_bounds")
                        at = (r * 2 + h) * 4 + q
                        acc[at] = jnp.where(hit, got, acc[at])
        return tuple(acc)

    acc = lax.fori_loop(0, 9, gather_column, (zero8,) * 16)
    for r in range(R):
        own = [pos_ref[64 + (1 + r) * 4 + c:64 + (1 + r) * 4 + c + 1, :] for c in range(3)]
        for h in range(2):
            off = off_s[r, h * 8:(h + 1) * 8, :]
            shift = (off // 9 - 1, off // 3 % 3 - 1, off % 3 - 1)
            for c in range(3):
                value = shift[c].astype(F32) + acc[(r * 2 + h) * 4 + c] - rows8(own[c], CAP)
                d_s[r, c * K + h * 8:c * K + h * 8 + 8, :] = value
            kd_s[r, h * 8:h * 8 + 8, :] = acc[(r * 2 + h) * 4 + 3]

    centre = lax.broadcasted_iota(jnp.int32, (8, W), 0).astype(F32) / (NB - 1)
    kinds16 = lax.broadcasted_iota(jnp.int32, (16, W), 0).astype(F32)

    def radial_group(group, _):
        inputs = []
        for j in range(GROUP):
            k = group * GROUP + j
            x = wide(d_s, k, 8)
            y = wide(d_s, K + k, 8)
            z = wide(d_s, 2 * K + k, 8)
            xx, yy, zz = x * x, y * y, z * z
            s = xx + yy + zz
            m1 = jnp.maximum(1.0 - s, 0.0)
            env = m1 * m1 * m1
            u = s - centre
            ex = jnp.exp(-float((NB - 1) ** 2) * (u * u))
            at = pl.multiple_of(k * 8, 8)
            exu_s[pl.ds(at, 8), :] = ex * (u * (-2.0 * float((NB - 1) ** 2)))
            ex3 = env * SQRT3
            terms = (
                env, env * x, env * y, env * z, ex3 * (x * y), ex3 * (y * z), ex3 * (z * x),
                (env * HALF_SQRT3) * (xx - yy), (env * 0.5) * (2.0 * zz - xx - yy),
            )
            for m in range(9):
                ey_s[m, pl.ds(at, 8), :] = terms[m]
            kind = wide(kd_s, k, 16)
            onehot = jnp.where(kind == kinds16, 1.0, 0.0)
            inputs.append(jnp.concatenate([ex, onehot], axis=0))
        rhs = jnp.concatenate(inputs, axis=1).astype(BF16)
        lanes = pl.ds(pl.multiple_of(group * (GROUP * W), GROUP * W), GROUP * W)
        first = jnp.dot(wc_s[...], rhs, preferred_element_type=F32)
        pre = first[:CH]
        feat = first[CH:]
        sig = 0.5 * jnp.tanh(0.5 * pre) + 0.5
        hidden = (pre * sig).astype(BF16)
        ds_s[:, lanes] = sig * (1.0 + pre * (1.0 - sig))
        feat_s[:, lanes] = feat
        radial = jnp.dot(w2t_s[...], hidden, preferred_element_type=F32)
        for deg in range(3):
            q_s[deg * CH:(deg + 1) * CH, lanes] = radial[deg * CH:(deg + 1) * CH] * feat
        return 0

    lax.fori_loop(0, K // GROUP, radial_group, 0)

    def message_block(cb, _):
        base = pl.multiple_of(cb * 16, 16)
        for r in range(R):
            sums = [None] * 9
            for k in range(K):
                lo = k * W + r * CAP
                q = [q_s[pl.ds(deg * CH + base, 16), lo:lo + CAP] for deg in range(3)]
                for m in range(9):
                    weight = ey_s[m, k * 8:(k + 1) * 8, r * CAP:(r + 1) * CAP]
                    weight = jnp.concatenate([weight, weight], axis=0)
                    term = q[0 if m == 0 else 1 if m < 4 else 2] * weight
                    sums[m] = term if sums[m] is None else sums[m] + term
            for m in range(9):
                m_s[m, pl.ds(base, 16), r * CAP:(r + 1) * CAP] = sums[m]
        return 0

    lax.fori_loop(0, CH // 16, message_block, 0)

    own_kind = jnp.concatenate(
        [jnp.broadcast_to(pos_ref[64 + (1 + r) * 4 + 3:64 + (1 + r) * 4 + 4, :], (16, CAP)) for r in range(R)], axis=1
    )
    own_feat = jnp.dot(
        embt_s[...], jnp.where(own_kind == kinds16, 1.0, 0.0).astype(BF16), preferred_element_type=F32
    )
    slot_number = lax.broadcasted_iota(jnp.int32, (1, CAP), 1)
    occupied = jnp.concatenate(
        [jnp.where(slot_number < count_ref[r], 1.0, 0.0) for r in range(R)], axis=1
    )
    vec = m_s[1] * m_s[1] + m_s[2] * m_s[2] + m_s[3] * m_s[3]
    ten = m_s[4] * m_s[4] + m_s[5] * m_s[5] + m_s[6] * m_s[6] + m_s[7] * m_s[7] + m_s[8] * m_s[8]
    invariant = jnp.concatenate([m_s[0], vec, ten, own_feat], axis=0).astype(BF16)
    pre = jnp.dot(wnt_s[...], invariant, preferred_element_type=F32)
    sig = 0.5 * jnp.tanh(0.5 * pre) + 0.5
    we = jnp.concatenate([we_ref[...]] * R, axis=1)
    energy = jnp.sum(we * (pre * sig), axis=0, keepdims=True) * occupied
    gpre = we * occupied * (sig * (1.0 + pre * (1.0 - sig)))
    ginv = jnp.dot(wn_ref[0:3 * CH, :], gpre.astype(BF16), preferred_element_type=F32).astype(BF16).astype(F32)
    m_s[0] = ginv[:CH]
    gvec = 2.0 * ginv[CH:2 * CH]
    gten = 2.0 * ginv[2 * CH:]
    for m in range(1, 9):
        m_s[m] = m_s[m] * (gvec if m < 4 else gten)

    def carried_back(k, _):
        at = pl.multiple_of(k * 8, 8)
        for r in range(R):
            cols = slice(r * CAP, (r + 1) * CAP)
            lanes = pl.ds(pl.multiple_of(k * W + r * CAP, CAP), CAP)
            weight = []
            for m in range(9):
                w8 = ey_s[m, pl.ds(at, 8), cols]
                weight.append(jnp.concatenate([w8, w8], axis=0))
            sums = [None] * 9
            for cb in range(CH // 16):
                feat = feat_s[cb * 16:(cb + 1) * 16, lanes]
                q = [q_s[deg * CH + cb * 16:deg * CH + (cb + 1) * 16, lanes] for deg in range(3)]
                back = [None] * 3
                for m in range(9):
                    deg = 0 if m == 0 else 1 if m < 4 else 2
                    cot = m_s[m, cb * 16:(cb + 1) * 16, cols]
                    term = cot * q[deg]
                    sums[m] = term if sums[m] is None else sums[m] + term
                    term = cot * weight[m]
                    back[deg] = term if back[deg] is None else back[deg] + term
                for deg in range(3):
                    gr_s[deg * CH + cb * 16:deg * CH + (cb + 1) * 16, lanes] = (back[deg] * feat).astype(BF16)
            for m in range(9):
                t_s[r, m, pl.ds(at, 8), :] = sums[m][:8] + sums[m][8:]
        return 0

    lax.fori_loop(0, K, carried_back, 0)

    def radial_back(group, _):
        lanes = pl.ds(pl.multiple_of(group * (GROUP * W), GROUP * W), GROUP * W)
        ghid = jnp.dot(w2_ref[...], gr_s[:, lanes], preferred_element_type=F32)
        gpre = (ghid.astype(BF16).astype(F32) * ds_s[:, lanes]).astype(BF16)
        gbas = jnp.dot(w1_ref[...], gpre, preferred_element_type=F32).astype(BF16).astype(F32)
        for j in range(GROUP):
            at = pl.multiple_of((group * GROUP + j) * 8, 8)
            for r in range(R):
                lo = j * W + r * CAP
                ts_s[r, pl.ds(at, 8), :] = gbas[:, lo:lo + CAP] * exu_s[pl.ds(at, 8), r * CAP:(r + 1) * CAP]
        return 0

    lax.fori_loop(0, K // GROUP, radial_back, 0)

    def total(ref):
        out = ref[pl.ds(0, K, stride=8), :]
        for sub in range(1, 8):
            out = out + ref[pl.ds(sub, K, stride=8), :]
        return out

    for r in range(R):
        cols = slice(r * CAP, (r + 1) * CAP)
        x, y, z = d_s[r, 0:K, :], d_s[r, K:2 * K, :], d_s[r, 2 * K:3 * K, :]
        xx, yy, zz = x * x, y * y, z * z
        s = xx + yy + zz
        m1 = jnp.maximum(1.0 - s, 0.0)
        env = m1 * m1 * m1
        t = [total(t_s.at[r, m]) for m in range(9)]
        harm = (
            None, x, y, z, SQRT3 * (x * y), SQRT3 * (y * z), SQRT3 * (z * x),
            HALF_SQRT3 * (xx - yy), 0.5 * (2.0 * zz - xx - yy),
        )
        genv = t[0]
        for m in range(1, 9):
            genv = genv + harm[m] * t[m]
        gs2 = 2.0 * (total(ts_s.at[r]) - 3.0 * (m1 * m1) * genv)
        e = [env * v for v in t]
        gx = e[1] + SQRT3 * (y * e[4] + z * e[6]) + x * (SQRT3 * e[7] - e[8] + gs2)
        gy = e[2] + SQRT3 * (x * e[4] + z * e[5]) + y * (gs2 - SQRT3 * e[7] - e[8])
        gz = e[3] + SQRT3 * (y * e[5] + x * e[6]) + z * (2.0 * e[8] + gs2)
        for c, g in enumerate((gx, gy, gz)):
            g_s[r, c * K:(c + 1) * K, :] = g
            own_ref[r * 4 + c:r * 4 + c + 1, :] = jnp.sum(g, axis=0, keepdims=True)
        own_ref[r * 4 + 3:r * 4 + 4, :] = energy[:, cols]

    sub = lax.broadcasted_iota(jnp.int32, (8, CAP), 0)
    comp = sub % 4
    row_cell = lax.broadcasted_iota(jnp.int32, (144, CAP), 0) // 4
    slots = lax.broadcasted_iota(jnp.int32, (CAP, CAP), 0)

    def scatter_inputs(k, _):
        for r in range(R):
            cols = slice(r * CAP, (r + 1) * CAP)
            lanes = pl.ds(pl.multiple_of(k * W + r * CAP, CAP), CAP)
            off = off_s[r, pl.ds(k, 1), :]
            cell = off // 3 * 4 + off % 3 + r
            slot = slot_s[r, pl.ds(k, 1), :]
            gx, gy, gz = (rows8(g_s[r, pl.ds(c * K + k, 1), :], CAP) for c in range(3))
            mixed = jnp.where(comp == 0, gx, jnp.where(comp == 1, gy, jnp.where(comp == 2, gz, 0.0)))
            mixed = jnp.concatenate([-mixed] * 18, axis=0)
            hit = jnp.broadcast_to(cell, (144, CAP)) == row_cell
            a_s[:, lanes] = jnp.where(hit, mixed, 0.0).astype(BF16)
            s_s[:, lanes] = jnp.where(jnp.broadcast_to(slot, (CAP, CAP)) == slots, 1.0, 0.0).astype(BF16)
        return 0

    lax.fori_loop(0, K, scatter_inputs, 0)
    ghost_ref[...] = lax.dot_general(
        a_s[...], s_s[...], (((1,), (1,)), ((), ())), preferred_element_type=F32
    )


def core(count, pos, codes, embed16, w1, w2, wn, we):
    vmem = pl.BlockSpec(memory_space=pltpu.VMEM)
    scratch = [
        pltpu.VMEM((2 * CH, NB + 16), BF16),
        pltpu.VMEM((3 * CH, CH), BF16),
        pltpu.VMEM((CH, 4 * CH), BF16),
        pltpu.VMEM((CH, 16), BF16),
        pltpu.VMEM((R, 3 * K, CAP), F32),
        pltpu.VMEM((R, K, CAP), F32),
        pltpu.VMEM((R, K, CAP), jnp.int32),
        pltpu.VMEM((R, K, CAP), jnp.int32),
        pltpu.VMEM((9, 8 * K, W), F32),
        pltpu.VMEM((8 * K, W), F32),
        pltpu.VMEM((CH, K * W), F32),
        pltpu.VMEM((CH, K * W), F32),
        pltpu.VMEM((3 * CH, K * W), F32),
        pltpu.VMEM((9, CH, W), F32),
        pltpu.VMEM((3 * CH, K * W), BF16),
        pltpu.VMEM((R, 9, 8 * K, CAP), F32),
        pltpu.VMEM((R, 8 * K, CAP), F32),
        pltpu.VMEM((R, 3 * K, CAP), F32),
        pltpu.VMEM((144, K * W), BF16),
        pltpu.VMEM((CAP, K * W), BF16),
    ]
    return pl.pallas_call(
        core_kernel,
        in_specs=[pl.BlockSpec(memory_space=pltpu.SMEM)] + [vmem] * 7,
        out_specs=[vmem, vmem],
        out_shape=[jax.ShapeDtypeStruct((144, CAP), F32), jax.ShapeDtypeStruct((8, CAP), F32)],
        scratch_shapes=scratch,
        name="edges",
    )(count, pos, codes, embed16, w1, w2, wn, we)


def shards(
    frac, velocity, force_old, species, cell_count, neighbours, embed, w_radial_in, w_radial_out, w_node, w_energy
):
    even_x = lax.axis_index("gx") % 2 == 0
    even_y = lax.axis_index("gy") % 2 == 0
    even_z = lax.axis_index("gz") % 2 == 0
    occupied = (lax.broadcasted_iota(jnp.int32, species.shape, 3) < cell_count[..., None]).astype(F32)
    atom_mass = species_mass(species)
    half_velocity = velocity + 0.5 * TIME_STEP * force_old / atom_mass
    moved = frac + TIME_STEP * half_velocity
    mine = jnp.concatenate([moved, species.astype(F32)[None]], axis=0).reshape(4, R, CAP)
    mine = mine.transpose(1, 0, 2)

    low, high = both(even_z, mine[1], mine[0], "gz")
    column = jnp.concatenate([low, mine.reshape(4 * R, CAP), high], axis=0)
    low, high = both(even_y, column, column, "gy")
    plane = jnp.stack([low, column, high])
    low, high = both(even_x, plane, plane, "gx")
    pos = jnp.stack([low, plane, high]).reshape(144, CAP)

    ghost, own = core(
        cell_count.reshape(R),
        pos,
        neighbours.reshape(K * R, CAP),
        jnp.pad(embed, ((0, 16 - embed.shape[0]), (0, 0))),
        w_radial_in,
        w_radial_out,
        w_node,
        jnp.broadcast_to(w_energy[:, None], (CH, CAP)),
    )
    ghost = ghost.reshape(3, 3, 16, CAP)
    low, high = both(even_x, ghost[2], ghost[0], "gx")
    plane = ghost[1] + low + high
    low, high = both(even_y, plane[2], plane[0], "gy")
    column = (plane[1] + low + high).reshape(4, 4, CAP)
    low, high = both(even_z, column[3], column[0], "gz")
    own = own.reshape(R, 4, CAP)
    force = column[1:3] + own
    force = force + jnp.stack([low, high])
    force = force[:, :3].transpose(1, 0, 2).reshape(frac.shape)

    next_force = occupied * force
    next_velocity = occupied * (half_velocity + 0.5 * TIME_STEP * next_force / atom_mass)
    next_frac = occupied * moved
    site_energy = own[:, 3].reshape(species.shape)
    return (next_frac, next_velocity, next_force, site_energy)


def solution(mesh):
    cells = P(None, "gx", "gy", "gz", None)
    in_specs = (
        cells, cells, cells, P("gx", "gy", "gz", None), P("gx", "gy", "gz"), cells, P(), P(), P(), P(), P(),
    )
    out_specs = (cells, cells, cells, P("gx", "gy", "gz", None))
    return jax.shard_map(shards, mesh=mesh, in_specs=in_specs, out_specs=out_specs, check_vma=False)
```

```python
import jax
import jax.numpy as jnp
from jax import lax
from jax.experimental import pallas as pl
from jax.experimental.pallas import tpu as pltpu
from jax.sharding import PartitionSpec as P

MASSES = (1.008, 12.011, 14.007, 15.999, 32.06, 22.99, 35.45, 39.098, 24.305, 40.078)
SQRT3 = 1.7320508075688772
HALF_SQRT3 = 0.8660254037844386
TIME_STEP = 0.5

K = 16
CAP = 128
R = 2
W = R * CAP
CH = 64
NB = 8
GROUP = 4
F32 = jnp.float32
BF16 = jnp.bfloat16


def swap(array, axis, odd):
    n = lax.axis_size(axis)
    if odd:
        pairs = [(i, (i + 1) % n if i % 2 else (i - 1) % n) for i in range(n)]
    else:
        pairs = [(i, i ^ 1) for i in range(n)]
    return lax.ppermute(array, axis, pairs)


def rows8(row, width):
    return jnp.broadcast_to(row, (8, width))


def wide(ref, row, height):
    parts = [jnp.broadcast_to(ref[r, pl.ds(row, 1), :], (height, CAP)) for r in range(R)]
    return jnp.concatenate(parts, axis=1)


def begin_kernel(frac_ref, vel_ref, force_ref, kind_ref, send_a_ref, send_b_ref, mine_ref, keep_ref):
    kind = kind_ref[...]
    mass = jnp.zeros((R, CAP), F32)
    for number, value in enumerate(MASSES):
        mass = jnp.where(kind == number, jnp.float32(value) / jnp.float32(16.0), mass)
    for c in range(3):
        half = vel_ref[c] + 0.5 * TIME_STEP * force_ref[c] / mass
        moved = frac_ref[c] + TIME_STEP * half
        for r in range(R):
            mine_ref[r * 4 + c:r * 4 + c + 1, :] = moved[r:r + 1]
            keep_ref[r * 4 + c:r * 4 + c + 1, :] = half[r:r + 1]
    for r in range(R):
        mine_ref[r * 4 + 3:r * 4 + 4, :] = kind[r:r + 1].astype(F32)
        keep_ref[r * 4 + 3:r * 4 + 4, :] = mass[r:r + 1]
    even = lax.axis_index("gz") % 2 == 0
    send_a_ref[...] = jnp.where(even, mine_ref[4:8, :], mine_ref[0:4, :])
    send_b_ref[...] = jnp.where(even, mine_ref[0:4, :], mine_ref[4:8, :])


def finish_kernel(count_ref, mid_ref, got_a_ref, got_b_ref, own_ref, mine_ref, keep_ref, frac_ref, vel_ref, force_ref, energy_ref):
    even = lax.axis_index("gz") % 2 == 0
    got = (
        jnp.where(even, got_b_ref[...], got_a_ref[...]),
        jnp.where(even, got_a_ref[...], got_b_ref[...]),
    )
    slot_number = lax.broadcasted_iota(jnp.int32, (1, CAP), 1)
    for r in range(R):
        occupied = jnp.where(slot_number < count_ref[r], 1.0, 0.0)
        total = mid_ref[4 * (r + 1):4 * (r + 2), :] + own_ref[r * 4:r * 4 + 4, :] + got[r]
        force = occupied * total
        keep = keep_ref[r * 4:r * 4 + 4, :]
        mine = mine_ref[r * 4:r * 4 + 4, :]
        speed = occupied * (keep + 0.5 * TIME_STEP * force / keep[3:4])
        place = occupied * mine
        for c in range(3):
            force_ref[c, r:r + 1, :] = force[c:c + 1]
            vel_ref[c, r:r + 1, :] = speed[c:c + 1]
            frac_ref[c, r:r + 1, :] = place[c:c + 1]
        energy_ref[r:r + 1, :] = own_ref[r * 4 + 3:r * 4 + 4, :]


def prepare_kernel(codes_ref, emb_ref, w1_ref, w2_ref, wnt_ref, wc_ref, w2t_ref, wn_ref, embt_ref, off_ref, slot_ref, cell_ref, pick_ref):
    wc_ref[...] = jnp.zeros(wc_ref.shape, BF16)
    wc_ref[0:CH, 0:NB] = w1_ref[...].astype(F32).T.astype(BF16)
    emb = jnp.concatenate([emb_ref[...].astype(F32), jnp.zeros((6, CH), F32)], axis=0)
    embt = emb.T.astype(BF16)
    wc_ref[CH:, NB:NB + 16] = embt
    embt_ref[...] = embt
    w2t_ref[...] = w2_ref[...].astype(F32).T.astype(BF16)
    wn_ref[...] = wnt_ref[...].astype(F32).T.astype(BF16)
    row_cell = lax.broadcasted_iota(jnp.int32, (144, CAP), 0) // 4
    slots = lax.broadcasted_iota(jnp.int32, (CAP, CAP), 0)
    for r in range(R):
        code = codes_ref[pl.ds(r, K, stride=R), :]
        off = code // CAP
        slot = code % CAP
        off_ref[r] = off
        slot_ref[r] = slot
        cell = off // 3 * 4 + off % 3 + r
        for k in range(K):
            lanes = slice(k * W + r * CAP, k * W + (r + 1) * CAP)
            cell_ref[:, lanes] = jnp.where(jnp.broadcast_to(cell[k:k + 1], (144, CAP)) == row_cell, 1.0, 0.0).astype(BF16)
            pick_ref[:, lanes] = jnp.where(jnp.broadcast_to(slot[k:k + 1], (CAP, CAP)) == slots, 1.0, 0.0).astype(BF16)


def edges_kernel(
    count_ref, we_ref, plane_ref, got_a_ref, got_b_ref,
    w1_ref, w2_ref, wnt_ref, wc_ref, w2t_ref, wn_ref, embt_ref, off_ref, slot_ref, cell_ref, pick_ref,
    mid_ref, send_a_ref, send_b_ref, own_ref,
    pos_s, d_s, kd_s, ey_s, exu_s, ds_s, feat_s, q_s, m_s, gr_s, t_s, ts_s, g_s, a_s,
):
    even = lax.axis_index("gx") % 2 == 0
    pos_s[0:48] = jnp.where(even, got_b_ref[...], got_a_ref[...])
    pos_s[48:96] = plane_ref[...]
    pos_s[96:144] = jnp.where(even, got_a_ref[...], got_b_ref[...])

    acc = [jnp.zeros((8, CAP), F32) for _ in range(16)]
    offs = [[off_ref[r, h * 8:(h + 1) * 8, :] for h in range(2)] for r in range(R)]
    slots = [[slot_ref[r, h * 8:(h + 1) * 8, :] for h in range(2)] for r in range(R)]
    for col in range(9):
        for zz in range(4):
            rows = [rows8(pos_s[col * 16 + zz * 4 + q:col * 16 + zz * 4 + q + 1, :], CAP) for q in range(4)]
            for r in range(R):
                dz = zz - r
                if not 0 <= dz <= 2:
                    continue
                for h in range(2):
                    hit = offs[r][h] == col * 3 + dz
                    for q in range(4):
                        got = jnp.take_along_axis(rows[q], slots[r][h], axis=1, mode="promise_in_bounds")
                        at = (r * 2 + h) * 4 + q
                        acc[at] = jnp.where(hit, got, acc[at])
    for r in range(R):
        own = [pos_s[64 + (1 + r) * 4 + c:64 + (1 + r) * 4 + c + 1, :] for c in range(3)]
        for h in range(2):
            off = offs[r][h]
            shift = (off // 9 - 1, off // 3 % 3 - 1, off % 3 - 1)
            for c in range(3):
                value = shift[c].astype(F32) + acc[(r * 2 + h) * 4 + c] - rows8(own[c], CAP)
                d_s[r, c * K + h * 8:c * K + h * 8 + 8, :] = value
            kd_s[r, h * 8:h * 8 + 8, :] = acc[(r * 2 + h) * 4 + 3]

    centre = lax.broadcasted_iota(jnp.int32, (8, W), 0).astype(F32) / (NB - 1)
    kinds16 = lax.broadcasted_iota(jnp.int32, (16, W), 0).astype(F32)

    def radial_group(group, _):
        inputs = []
        for j in range(GROUP):
            k = group * GROUP + j
            x = wide(d_s, k, 8)
            y = wide(d_s, K + k, 8)
            z = wide(d_s, 2 * K + k, 8)
            xx, yy, zz = x * x, y * y, z * z
            s = xx + yy + zz
            m1 = jnp.maximum(1.0 - s, 0.0)
            env = m1 * m1 * m1
            u = s - centre
            ex = jnp.exp(-float((NB - 1) ** 2) * (u * u))
            at = k * 8
            exu_s[pl.ds(at, 8), :] = ex * (u * (-2.0 * float((NB - 1) ** 2)))
            ex3 = env * SQRT3
            terms = (
                env, env * x, env * y, env * z, ex3 * (x * y), ex3 * (y * z), ex3 * (z * x),
                (env * HALF_SQRT3) * (xx - yy), (env * 0.5) * (2.0 * zz - xx - yy),
            )
            for m in range(9):
                ey_s[m, pl.ds(at, 8), :] = terms[m]
            kind = wide(kd_s, k, 16)
            onehot = jnp.where(kind == kinds16, 1.0, 0.0)
            inputs.append(jnp.concatenate([ex, onehot], axis=0))
        rhs = jnp.concatenate(inputs, axis=1).astype(BF16)
        lanes = pl.ds(group * (GROUP * W), GROUP * W)
        first = jnp.dot(wc_ref[...], rhs, preferred_element_type=F32)
        pre = first[:CH]
        feat = first[CH:]
        sig = 0.5 * jnp.tanh(0.5 * pre) + 0.5
        hidden = (pre * sig).astype(BF16)
        ds_s[:, lanes] = sig * (1.0 + pre * (1.0 - sig))
        feat_s[:, lanes] = feat
        radial = jnp.dot(w2t_ref[...], hidden, preferred_element_type=F32)
        for deg in range(3):
            q_s[deg * CH:(deg + 1) * CH, lanes] = radial[deg * CH:(deg + 1) * CH] * feat
        return 0

    for group in range(K // GROUP):
        radial_group(group, 0)

    def message_block(cb, _):
        base = cb * 16
        for r in range(R):
            sums = [None] * 9
            for k in range(K):
                lo = k * W + r * CAP
                q = [q_s[pl.ds(deg * CH + base, 16), lo:lo + CAP] for deg in range(3)]
                for m in range(9):
                    weight = ey_s[m, k * 8:(k + 1) * 8, r * CAP:(r + 1) * CAP]
                    weight = jnp.concatenate([weight, weight], axis=0)
                    term = q[0 if m == 0 else 1 if m < 4 else 2] * weight
                    sums[m] = term if sums[m] is None else sums[m] + term
            for m in range(9):
                m_s[m, pl.ds(base, 16), r * CAP:(r + 1) * CAP] = sums[m]
        return 0

    for cb in range(CH // 16):
        message_block(cb, 0)

    own_kind = jnp.concatenate(
        [jnp.broadcast_to(pos_s[64 + (1 + r) * 4 + 3:64 + (1 + r) * 4 + 4, :], (16, CAP)) for r in range(R)], axis=1
    )
    own_feat = jnp.dot(
        embt_ref[...], jnp.where(own_kind == kinds16, 1.0, 0.0).astype(BF16), preferred_element_type=F32
    )
    slot_number = lax.broadcasted_iota(jnp.int32, (1, CAP), 1)
    occupied = jnp.concatenate(
        [jnp.where(slot_number < count_ref[r], 1.0, 0.0) for r in range(R)], axis=1
    )
    vec = m_s[1] * m_s[1] + m_s[2] * m_s[2] + m_s[3] * m_s[3]
    ten = m_s[4] * m_s[4] + m_s[5] * m_s[5] + m_s[6] * m_s[6] + m_s[7] * m_s[7] + m_s[8] * m_s[8]
    invariant = jnp.concatenate([m_s[0], vec, ten, own_feat], axis=0).astype(BF16)
    pre = jnp.dot(wnt_ref[...], invariant, preferred_element_type=F32)
    sig = 0.5 * jnp.tanh(0.5 * pre) + 0.5
    we = jnp.broadcast_to(we_ref[...], (8, CH)).T[:, 0:1]
    energy = jnp.sum(we * (pre * sig), axis=0, keepdims=True) * occupied
    gpre = we * occupied * (sig * (1.0 + pre * (1.0 - sig)))
    ginv = jnp.dot(wn_ref[0:3 * CH, :], gpre.astype(BF16), preferred_element_type=F32).astype(BF16).astype(F32)
    m_s[0] = ginv[:CH]
    gvec = 2.0 * ginv[CH:2 * CH]
    gten = 2.0 * ginv[2 * CH:]
    for m in range(1, 9):
        m_s[m] = m_s[m] * (gvec if m < 4 else gten)

    def carried_back(k, _):
        at = k * 8
        for r in range(R):
            cols = slice(r * CAP, (r + 1) * CAP)
            lanes = pl.ds(k * W + r * CAP, CAP)
            weight = []
            for m in range(9):
                w8 = ey_s[m, pl.ds(at, 8), cols]
                weight.append(jnp.concatenate([w8, w8], axis=0))
            sums = [None] * 9
            for cb in range(CH // 16):
                feat = feat_s[cb * 16:(cb + 1) * 16, lanes]
                q = [q_s[deg * CH + cb * 16:deg * CH + (cb + 1) * 16, lanes] for deg in range(3)]
                back = [None] * 3
                for m in range(9):
                    deg = 0 if m == 0 else 1 if m < 4 else 2
                    cot = m_s[m, cb * 16:(cb + 1) * 16, cols]
                    term = cot * q[deg]
                    sums[m] = term if sums[m] is None else sums[m] + term
                    term = cot * weight[m]
                    back[deg] = term if back[deg] is None else back[deg] + term
                for deg in range(3):
                    gr_s[deg * CH + cb * 16:deg * CH + (cb + 1) * 16, lanes] = (back[deg] * feat).astype(BF16)
            for m in range(9):
                t_s[r, m, pl.ds(at, 8), :] = sums[m][:8] + sums[m][8:]
        return 0

    for k in range(K):
        carried_back(k, 0)

    def radial_back(group, _):
        lanes = pl.ds(group * (GROUP * W), GROUP * W)
        ghid = jnp.dot(w2_ref[...], gr_s[:, lanes], preferred_element_type=F32)
        gpre = (ghid.astype(BF16).astype(F32) * ds_s[:, lanes]).astype(BF16)
        gbas = jnp.dot(w1_ref[...], gpre, preferred_element_type=F32).astype(BF16).astype(F32)
        for j in range(GROUP):
            at = (group * GROUP + j) * 8
            for r in range(R):
                lo = j * W + r * CAP
                ts_s[r, pl.ds(at, 8), :] = gbas[:, lo:lo + CAP] * exu_s[pl.ds(at, 8), r * CAP:(r + 1) * CAP]
        return 0

    for group in range(K // GROUP):
        radial_back(group, 0)

    def total(ref):
        out = ref[pl.ds(0, K, stride=8), :]
        for sub in range(1, 8):
            out = out + ref[pl.ds(sub, K, stride=8), :]
        return out

    for r in range(R):
        cols = slice(r * CAP, (r + 1) * CAP)
        x, y, z = d_s[r, 0:K, :], d_s[r, K:2 * K, :], d_s[r, 2 * K:3 * K, :]
        xx, yy, zz = x * x, y * y, z * z
        s = xx + yy + zz
        m1 = jnp.maximum(1.0 - s, 0.0)
        env = m1 * m1 * m1
        t = [total(t_s.at[r, m]) for m in range(9)]
        harm = (
            None, x, y, z, SQRT3 * (x * y), SQRT3 * (y * z), SQRT3 * (z * x),
            HALF_SQRT3 * (xx - yy), 0.5 * (2.0 * zz - xx - yy),
        )
        genv = t[0]
        for m in range(1, 9):
            genv = genv + harm[m] * t[m]
        gs2 = 2.0 * (total(ts_s.at[r]) - 3.0 * (m1 * m1) * genv)
        e = [env * v for v in t]
        gx = e[1] + SQRT3 * (y * e[4] + z * e[6]) + x * (SQRT3 * e[7] - e[8] + gs2)
        gy = e[2] + SQRT3 * (x * e[4] + z * e[5]) + y * (gs2 - SQRT3 * e[7] - e[8])
        gz = e[3] + SQRT3 * (y * e[5] + x * e[6]) + z * (2.0 * e[8] + gs2)
        for c, g in enumerate((gx, gy, gz)):
            g_s[r, c * K:(c + 1) * K, :] = g
            own_ref[r * 4 + c:r * 4 + c + 1, :] = jnp.sum(g, axis=0, keepdims=True)
        own_ref[r * 4 + 3:r * 4 + 4, :] = energy[:, cols]

    sub = lax.broadcasted_iota(jnp.int32, (16, CAP), 0)
    comp = sub % 4
    for k in range(K):
        for r in range(R):
            lanes = slice(k * W + r * CAP, k * W + (r + 1) * CAP)
            gx, gy, gz = (jnp.broadcast_to(g_s[r, c * K + k:c * K + k + 1, :], (16, CAP)) for c in range(3))
            mixed = jnp.where(comp == 0, gx, jnp.where(comp == 1, gy, jnp.where(comp == 2, gz, 0.0)))
            mixed = (-mixed).astype(BF16)
            for j in range(9):
                a_s[j * 16:(j + 1) * 16, lanes] = cell_ref[j * 16:(j + 1) * 16, lanes] * mixed
    out = lax.dot_general(a_s[...], pick_ref[...], (((1,), (1,)), ((), ())), preferred_element_type=F32)
    mid_ref[...] = out[48:96]
    send_a_ref[...] = jnp.where(even, out[96:144], out[0:48])
    send_b_ref[...] = jnp.where(even, out[0:48], out[96:144])


VMEM = pl.BlockSpec(memory_space=pltpu.VMEM)
SMEM = pl.BlockSpec(memory_space=pltpu.SMEM)


def call(kernel, name, args, outs, hbm_outs=False, smem=0, scratch=()):
    shape = jax.ShapeDtypeStruct if hbm_outs else pltpu.VMEM
    return pl.pallas_call(
        kernel,
        in_specs=[SMEM] * smem + [VMEM] * (len(args) - smem),
        out_specs=[VMEM] * len(outs),
        out_shape=[shape(*out) for out in outs],
        scratch_shapes=list(scratch),
        name=name,
    )(*args)


def begin(frac, velocity, force_old, species):
    outs = [((4, CAP), F32), ((4, CAP), F32), ((4 * R, CAP), F32), ((4 * R, CAP), F32)]
    return call(begin_kernel, "begin", (frac, velocity, force_old, species), outs)


def prepare(codes, embed, w1, w2, wnt):
    outs = [
        ((2 * CH, NB + 16), BF16), ((3 * CH, CH), BF16), ((4 * CH, CH), BF16), ((CH, 16), BF16),
        ((R, K, CAP), jnp.int32), ((R, K, CAP), jnp.int32), ((144, K * W), BF16), ((CAP, K * W), BF16),
    ]
    return call(prepare_kernel, "prepare", (codes, embed, w1, w2, wnt), outs)


def edges(count, we, plane, got_a, got_b, w1, w2, wnt, prepared):
    scratch = [
        pltpu.VMEM((144, CAP), F32),
        pltpu.VMEM((R, 3 * K, CAP), F32),
        pltpu.VMEM((R, K, CAP), F32),
        pltpu.VMEM((9, 8 * K, W), F32),
        pltpu.VMEM((8 * K, W), F32),
        pltpu.VMEM((CH, K * W), F32),
        pltpu.VMEM((CH, K * W), F32),
        pltpu.VMEM((3 * CH, K * W), F32),
        pltpu.VMEM((9, CH, W), F32),
        pltpu.VMEM((3 * CH, K * W), BF16),
        pltpu.VMEM((R, 9, 8 * K, CAP), F32),
        pltpu.VMEM((R, 8 * K, CAP), F32),
        pltpu.VMEM((R, 3 * K, CAP), F32),
        pltpu.VMEM((144, K * W), BF16),
    ]
    outs = [((48, CAP), F32), ((48, CAP), F32), ((48, CAP), F32), ((8, CAP), F32)]
    args = (count, we, plane, got_a, got_b, w1, w2, wnt, *prepared)
    return call(edges_kernel, "edges", args, outs, smem=1, scratch=scratch)


def finish(count, column, got_a, got_b, own, mine, keep):
    outs = [((3, R, CAP), F32)] * 3 + [((R, CAP), F32)]
    return call(finish_kernel, "finish", (count, column, got_a, got_b, own, mine, keep), outs, hbm_outs=True, smem=1)


def shards(
    frac, velocity, force_old, species, cell_count, neighbours, embed, w_radial_in, w_radial_out, w_node, w_energy
):
    even_y = lax.axis_index("gy") % 2 == 0
    even_z = lax.axis_index("gz") % 2 == 0
    vectors = (3, R, CAP)
    count = cell_count.reshape(R)
    wnt = w_node.T
    send_a, send_b, mine, keep = begin(
        frac.reshape(vectors), velocity.reshape(vectors), force_old.reshape(vectors), species.reshape(R, CAP)
    )
    prepared = prepare(neighbours.reshape(K * R, CAP), embed, w_radial_in, w_radial_out, wnt)

    got_a, got_b = swap(send_a, "gz", False), swap(send_b, "gz", True)
    column = jnp.concatenate(
        [jnp.where(even_z, got_b, got_a), mine, jnp.where(even_z, got_a, got_b)], axis=0
    )
    got_a, got_b = swap(column, "gy", False), swap(column, "gy", True)
    plane = jnp.concatenate(
        [jnp.where(even_y, got_b, got_a), column, jnp.where(even_y, got_a, got_b)], axis=0
    )
    got_a, got_b = swap(plane, "gx", False), swap(plane, "gx", True)

    plane, send_a, send_b, own = edges(
        count, w_energy.reshape(1, CH), plane, got_a, got_b, w_radial_in, w_radial_out, wnt, prepared
    )
    plane = plane + swap(send_a, "gx", False) + swap(send_b, "gx", True)
    lower, column, upper = plane[0:16], plane[16:32], plane[32:48]
    send_a, send_b = jnp.where(even_y, upper, lower), jnp.where(even_y, lower, upper)
    column = column + swap(send_a, "gy", False) + swap(send_b, "gy", True)
    send_a = jnp.where(even_z, column[12:16], column[0:4])
    send_b = jnp.where(even_z, column[0:4], column[12:16])
    got_a, got_b = swap(send_a, "gz", False), swap(send_b, "gz", True)
    next_frac, next_velocity, next_force, energy = finish(count, column, got_a, got_b, own, mine, keep)
    return (
        next_frac.reshape(frac.shape),
        next_velocity.reshape(frac.shape),
        next_force.reshape(frac.shape),
        energy.reshape(species.shape),
    )


def solution(mesh):
    cells = P(None, "gx", "gy", "gz", None)
    in_specs = (
        cells, cells, cells, P("gx", "gy", "gz", None), P("gx", "gy", "gz"), cells, P(), P(), P(), P(), P(),
    )
    out_specs = (cells, cells, cells, P("gx", "gy", "gz", None))
    return jax.shard_map(shards, mesh=mesh, in_specs=in_specs, out_specs=out_specs, check_vma=False)
```

```python
import jax
import jax.numpy as jnp
from jax import lax
from jax.experimental import pallas as pl
from jax.experimental.pallas import tpu as pltpu
from jax.sharding import PartitionSpec as P

MASSES = (1.008, 12.011, 14.007, 15.999, 32.06, 22.99, 35.45, 39.098, 24.305, 40.078)
SQRT3 = 1.7320508075688772
HALF_SQRT3 = 0.8660254037844386
TIME_STEP = 0.5

K = 16
CAP = 128
R = 2
W = R * CAP
CH = 64
NB = 8
GROUP = 4
F32 = jnp.float32
BF16 = jnp.bfloat16


def swap(array, axis, odd):
    n = lax.axis_size(axis)
    if odd:
        pairs = [(i, (i + 1) % n if i % 2 else (i - 1) % n) for i in range(n)]
    else:
        pairs = [(i, i ^ 1) for i in range(n)]
    return lax.ppermute(array, axis, pairs)


def rows8(row, width):
    return jnp.broadcast_to(row, (8, width))


def wide(ref, row, height):
    parts = [jnp.broadcast_to(ref[r, pl.ds(row, 1), :], (height, CAP)) for r in range(R)]
    return jnp.concatenate(parts, axis=1)


def begin_kernel(frac_ref, vel_ref, force_ref, kind_ref, send_a_ref, send_b_ref, mine_ref, keep_ref):
    kind = kind_ref[...]
    mass = jnp.zeros((R, CAP), F32)
    for number, value in enumerate(MASSES):
        mass = jnp.where(kind == number, jnp.float32(value) / jnp.float32(16.0), mass)
    for c in range(3):
        half = vel_ref[c] + 0.5 * TIME_STEP * force_ref[c] / mass
        moved = frac_ref[c] + TIME_STEP * half
        for r in range(R):
            mine_ref[r * 4 + c:r * 4 + c + 1, :] = moved[r:r + 1]
            keep_ref[r * 4 + c:r * 4 + c + 1, :] = half[r:r + 1]
    for r in range(R):
        mine_ref[r * 4 + 3:r * 4 + 4, :] = kind[r:r + 1].astype(F32)
        keep_ref[r * 4 + 3:r * 4 + 4, :] = mass[r:r + 1]
    even = lax.axis_index("gz") % 2 == 0
    send_a_ref[...] = jnp.where(even, mine_ref[4:8, :], mine_ref[0:4, :])
    send_b_ref[...] = jnp.where(even, mine_ref[0:4, :], mine_ref[4:8, :])


def finish_kernel(count_ref, mid_ref, got_a_ref, got_b_ref, own_ref, mine_ref, keep_ref, frac_ref, vel_ref, force_ref, energy_ref):
    even = lax.axis_index("gz") % 2 == 0
    got = (
        jnp.where(even, got_b_ref[...], got_a_ref[...]),
        jnp.where(even, got_a_ref[...], got_b_ref[...]),
    )
    slot_number = lax.broadcasted_iota(jnp.int32, (1, CAP), 1)
    for r in range(R):
        occupied = jnp.where(slot_number < count_ref[r], 1.0, 0.0)
        total = mid_ref[4 * (r + 1):4 * (r + 2), :] + own_ref[r * 4:r * 4 + 4, :] + got[r]
        force = occupied * total
        keep = keep_ref[r * 4:r * 4 + 4, :]
        mine = mine_ref[r * 4:r * 4 + 4, :]
        speed = occupied * (keep + 0.5 * TIME_STEP * force / keep[3:4])
        place = occupied * mine
        for c in range(3):
            force_ref[c, r:r + 1, :] = force[c:c + 1]
            vel_ref[c, r:r + 1, :] = speed[c:c + 1]
            frac_ref[c, r:r + 1, :] = place[c:c + 1]
        energy_ref[r:r + 1, :] = own_ref[r * 4 + 3:r * 4 + 4, :]


def prepare_kernel(codes_ref, emb_ref, w1_ref, w2_ref, wnt_ref, wc_ref, w2t_ref, wn_ref, embt_ref, off_ref, slot_ref, cell_ref, pick_ref):
    wc_ref[...] = jnp.zeros(wc_ref.shape, BF16)
    wc_ref[0:CH, 0:NB] = w1_ref[...].astype(F32).T.astype(BF16)
    emb = jnp.concatenate([emb_ref[...].astype(F32), jnp.zeros((6, CH), F32)], axis=0)
    embt = emb.T.astype(BF16)
    wc_ref[CH:, NB:NB + 16] = embt
    embt_ref[...] = embt
    w2t_ref[...] = w2_ref[...].astype(F32).T.astype(BF16)
    wn_ref[...] = wnt_ref[...].astype(F32).T.astype(BF16)
    row_cell = lax.broadcasted_iota(jnp.int32, (144, CAP), 0) // 4
    slots = lax.broadcasted_iota(jnp.int32, (CAP, CAP), 0)
    for r in range(R):
        code = codes_ref[pl.ds(r, K, stride=R), :]
        off = code // CAP
        slot = code % CAP
        off_ref[r] = off
        slot_ref[r] = slot
        cell = off // 3 * 4 + off % 3 + r
        for k in range(K):
            lanes = slice(k * W + r * CAP, k * W + (r + 1) * CAP)
            cell_ref[:, lanes] = jnp.where(jnp.broadcast_to(cell[k:k + 1], (144, CAP)) == row_cell, 1.0, 0.0).astype(BF16)
            pick_ref[:, lanes] = jnp.where(jnp.broadcast_to(slot[k:k + 1], (CAP, CAP)) == slots, 1.0, 0.0).astype(BF16)


def edges_kernel(
    count_ref, we_ref, w1_ref, w2_ref, wnt_ref,
    plane_ref, got_a_ref, got_b_ref, wc_ref, w2t_ref, wn_ref, embt_ref, off_ref, slot_ref, cell_ref, pick_ref,
    mid_ref, send_a_ref, send_b_ref, own_ref,
    pos_s, d_s, kd_s, ey_s, exu_s, ds_s, feat_s, q_s, m_s, gr_s, t_s, ts_s, g_s, a_s,
):
    even = lax.axis_index("gx") % 2 == 0
    pos_s[0:48] = jnp.where(even, got_b_ref[...], got_a_ref[...])
    pos_s[48:96] = plane_ref[...]
    pos_s[96:144] = jnp.where(even, got_a_ref[...], got_b_ref[...])

    acc = [jnp.zeros((8, CAP), F32) for _ in range(16)]
    offs = [[off_ref[r, h * 8:(h + 1) * 8, :] for h in range(2)] for r in range(R)]
    slots = [[slot_ref[r, h * 8:(h + 1) * 8, :] for h in range(2)] for r in range(R)]
    for col in range(9):
        for zz in range(4):
            rows = [rows8(pos_s[col * 16 + zz * 4 + q:col * 16 + zz * 4 + q + 1, :], CAP) for q in range(4)]
            for r in range(R):
                dz = zz - r
                if not 0 <= dz <= 2:
                    continue
                for h in range(2):
                    hit = offs[r][h] == col * 3 + dz
                    for q in range(4):
                        got = jnp.take_along_axis(rows[q], slots[r][h], axis=1, mode="promise_in_bounds")
                        at = (r * 2 + h) * 4 + q
                        acc[at] = jnp.where(hit, got, acc[at])
    for r in range(R):
        own = [pos_s[64 + (1 + r) * 4 + c:64 + (1 + r) * 4 + c + 1, :] for c in range(3)]
        for h in range(2):
            off = offs[r][h]
            shift = (off // 9 - 1, off // 3 % 3 - 1, off % 3 - 1)
            for c in range(3):
                value = shift[c].astype(F32) + acc[(r * 2 + h) * 4 + c] - rows8(own[c], CAP)
                d_s[r, c * K + h * 8:c * K + h * 8 + 8, :] = value
            kd_s[r, h * 8:h * 8 + 8, :] = acc[(r * 2 + h) * 4 + 3]

    centre = lax.broadcasted_iota(jnp.int32, (8, W), 0).astype(F32) / (NB - 1)
    kinds16 = lax.broadcasted_iota(jnp.int32, (16, W), 0).astype(F32)

    def radial_group(group, _):
        inputs = []
        for j in range(GROUP):
            k = group * GROUP + j
            x = wide(d_s, k, 8)
            y = wide(d_s, K + k, 8)
            z = wide(d_s, 2 * K + k, 8)
            xx, yy, zz = x * x, y * y, z * z
            s = xx + yy + zz
            m1 = jnp.maximum(1.0 - s, 0.0)
            env = m1 * m1 * m1
            u = s - centre
            ex = jnp.exp(-float((NB - 1) ** 2) * (u * u))
            at = k * 8
            exu_s[pl.ds(at, 8), :] = ex * (u * (-2.0 * float((NB - 1) ** 2)))
            ex3 = env * SQRT3
            terms = (
                env, env * x, env * y, env * z, ex3 * (x * y), ex3 * (y * z), ex3 * (z * x),
                (env * HALF_SQRT3) * (xx - yy), (env * 0.5) * (2.0 * zz - xx - yy),
            )
            for m in range(9):
                ey_s[m, pl.ds(at, 8), :] = terms[m]
            kind = wide(kd_s, k, 16)
            onehot = jnp.where(kind == kinds16, 1.0, 0.0)
            inputs.append(jnp.concatenate([ex, onehot], axis=0))
        rhs = jnp.concatenate(inputs, axis=1).astype(BF16)
        lanes = pl.ds(group * (GROUP * W), GROUP * W)
        first = jnp.dot(wc_ref[...], rhs, preferred_element_type=F32)
        pre = first[:CH]
        feat = first[CH:]
        sig = 0.5 * jnp.tanh(0.5 * pre) + 0.5
        hidden = (pre * sig).astype(BF16)
        ds_s[:, lanes] = sig * (1.0 + pre * (1.0 - sig))
        feat_s[:, lanes] = feat
        radial = jnp.dot(w2t_ref[...], hidden, preferred_element_type=F32)
        for deg in range(3):
            q_s[deg * CH:(deg + 1) * CH, lanes] = radial[deg * CH:(deg + 1) * CH] * feat
        return 0

    for group in range(K // GROUP):
        radial_group(group, 0)

    def message_block(cb, _):
        base = cb * 16
        for r in range(R):
            sums = [None] * 9
            for k in range(K):
                lo = k * W + r * CAP
                q = [q_s[pl.ds(deg * CH + base, 16), lo:lo + CAP] for deg in range(3)]
                for m in range(9):
                    weight = ey_s[m, k * 8:(k + 1) * 8, r * CAP:(r + 1) * CAP]
                    weight = jnp.concatenate([weight, weight], axis=0)
                    term = q[0 if m == 0 else 1 if m < 4 else 2] * weight
                    sums[m] = term if sums[m] is None else sums[m] + term
            for m in range(9):
                m_s[m, pl.ds(base, 16), r * CAP:(r + 1) * CAP] = sums[m]
        return 0

    for cb in range(CH // 16):
        message_block(cb, 0)

    own_kind = jnp.concatenate(
        [jnp.broadcast_to(pos_s[64 + (1 + r) * 4 + 3:64 + (1 + r) * 4 + 4, :], (16, CAP)) for r in range(R)], axis=1
    )
    own_feat = jnp.dot(
        embt_ref[...], jnp.where(own_kind == kinds16, 1.0, 0.0).astype(BF16), preferred_element_type=F32
    )
    slot_number = lax.broadcasted_iota(jnp.int32, (1, CAP), 1)
    occupied = jnp.concatenate(
        [jnp.where(slot_number < count_ref[r], 1.0, 0.0) for r in range(R)], axis=1
    )
    vec = m_s[1] * m_s[1] + m_s[2] * m_s[2] + m_s[3] * m_s[3]
    ten = m_s[4] * m_s[4] + m_s[5] * m_s[5] + m_s[6] * m_s[6] + m_s[7] * m_s[7] + m_s[8] * m_s[8]
    invariant = jnp.concatenate([m_s[0], vec, ten, own_feat], axis=0).astype(BF16)
    pre = jnp.dot(wnt_ref[...], invariant, preferred_element_type=F32)
    sig = 0.5 * jnp.tanh(0.5 * pre) + 0.5
    we = jnp.broadcast_to(we_ref[...], (8, CH)).T[:, 0:1]
    energy = jnp.sum(we * (pre * sig), axis=0, keepdims=True) * occupied
    gpre = we * occupied * (sig * (1.0 + pre * (1.0 - sig)))
    ginv = jnp.dot(wn_ref[0:3 * CH, :], gpre.astype(BF16), preferred_element_type=F32).astype(BF16).astype(F32)
    m_s[0] = ginv[:CH]
    gvec = 2.0 * ginv[CH:2 * CH]
    gten = 2.0 * ginv[2 * CH:]
    for m in range(1, 9):
        m_s[m] = m_s[m] * (gvec if m < 4 else gten)

    def carried_back(k, _):
        at = k * 8
        for r in range(R):
            cols = slice(r * CAP, (r + 1) * CAP)
            lanes = pl.ds(k * W + r * CAP, CAP)
            weight = []
            for m in range(9):
                w8 = ey_s[m, pl.ds(at, 8), cols]
                weight.append(jnp.concatenate([w8, w8], axis=0))
            sums = [None] * 9
            for cb in range(CH // 16):
                feat = feat_s[cb * 16:(cb + 1) * 16, lanes]
                q = [q_s[deg * CH + cb * 16:deg * CH + (cb + 1) * 16, lanes] for deg in range(3)]
                back = [None] * 3
                for m in range(9):
                    deg = 0 if m == 0 else 1 if m < 4 else 2
                    cot = m_s[m, cb * 16:(cb + 1) * 16, cols]
                    term = cot * q[deg]
                    sums[m] = term if sums[m] is None else sums[m] + term
                    term = cot * weight[m]
                    back[deg] = term if back[deg] is None else back[deg] + term
                for deg in range(3):
                    gr_s[deg * CH + cb * 16:deg * CH + (cb + 1) * 16, lanes] = (back[deg] * feat).astype(BF16)
            for m in range(9):
                t_s[r, m, pl.ds(at, 8), :] = sums[m][:8] + sums[m][8:]
        return 0

    for k in range(K):
        carried_back(k, 0)

    def radial_back(group, _):
        lanes = pl.ds(group * (GROUP * W), GROUP * W)
        ghid = jnp.dot(w2_ref[...], gr_s[:, lanes], preferred_element_type=F32)
        gpre = (ghid.astype(BF16).astype(F32) * ds_s[:, lanes]).astype(BF16)
        gbas = jnp.dot(w1_ref[...], gpre, preferred_element_type=F32).astype(BF16).astype(F32)
        for j in range(GROUP):
            at = (group * GROUP + j) * 8
            for r in range(R):
                lo = j * W + r * CAP
                ts_s[r, pl.ds(at, 8), :] = gbas[:, lo:lo + CAP] * exu_s[pl.ds(at, 8), r * CAP:(r + 1) * CAP]
        return 0

    for group in range(K // GROUP):
        radial_back(group, 0)

    def total(ref):
        out = ref[pl.ds(0, K, stride=8), :]
        for sub in range(1, 8):
            out = out + ref[pl.ds(sub, K, stride=8), :]
        return out

    for r in range(R):
        cols = slice(r * CAP, (r + 1) * CAP)
        x, y, z = d_s[r, 0:K, :], d_s[r, K:2 * K, :], d_s[r, 2 * K:3 * K, :]
        xx, yy, zz = x * x, y * y, z * z
        s = xx + yy + zz
        m1 = jnp.maximum(1.0 - s, 0.0)
        env = m1 * m1 * m1
        t = [total(t_s.at[r, m]) for m in range(9)]
        harm = (
            None, x, y, z, SQRT3 * (x * y), SQRT3 * (y * z), SQRT3 * (z * x),
            HALF_SQRT3 * (xx - yy), 0.5 * (2.0 * zz - xx - yy),
        )
        genv = t[0]
        for m in range(1, 9):
            genv = genv + harm[m] * t[m]
        gs2 = 2.0 * (total(ts_s.at[r]) - 3.0 * (m1 * m1) * genv)
        e = [env * v for v in t]
        gx = e[1] + SQRT3 * (y * e[4] + z * e[6]) + x * (SQRT3 * e[7] - e[8] + gs2)
        gy = e[2] + SQRT3 * (x * e[4] + z * e[5]) + y * (gs2 - SQRT3 * e[7] - e[8])
        gz = e[3] + SQRT3 * (y * e[5] + x * e[6]) + z * (2.0 * e[8] + gs2)
        for c, g in enumerate((gx, gy, gz)):
            g_s[r, c * K:(c + 1) * K, :] = g
            own_ref[r * 4 + c:r * 4 + c + 1, :] = jnp.sum(g, axis=0, keepdims=True)
        own_ref[r * 4 + 3:r * 4 + 4, :] = energy[:, cols]

    sub = lax.broadcasted_iota(jnp.int32, (16, CAP), 0)
    comp = sub % 4
    for k in range(K):
        for r in range(R):
            lanes = slice(k * W + r * CAP, k * W + (r + 1) * CAP)
            gx, gy, gz = (jnp.broadcast_to(g_s[r, c * K + k:c * K + k + 1, :], (16, CAP)) for c in range(3))
            mixed = jnp.where(comp == 0, gx, jnp.where(comp == 1, gy, jnp.where(comp == 2, gz, 0.0)))
            mixed = (-mixed).astype(BF16)
            for j in range(9):
                a_s[j * 16:(j + 1) * 16, lanes] = cell_ref[j * 16:(j + 1) * 16, lanes] * mixed
    out = lax.dot_general(a_s[...], pick_ref[...], (((1,), (1,)), ((), ())), preferred_element_type=F32)
    mid_ref[...] = out[48:96]
    send_a_ref[...] = jnp.where(even, out[96:144], out[0:48])
    send_b_ref[...] = jnp.where(even, out[0:48], out[96:144])


VMEM = pl.BlockSpec(memory_space=pltpu.VMEM)
SMEM = pl.BlockSpec(memory_space=pltpu.SMEM)


def call(kernel, name, args, outs, near, hbm_outs=False, smem=0, scratch=()):
    shape = jax.ShapeDtypeStruct if hbm_outs else pltpu.VMEM
    args = args[:near] + tuple(pltpu.with_memory_space_constraint(a, pltpu.VMEM) for a in args[near:])
    return pl.pallas_call(
        kernel,
        in_specs=[SMEM] * smem + [VMEM] * (len(args) - smem),
        out_specs=[VMEM] * len(outs),
        out_shape=[shape(*out) for out in outs],
        scratch_shapes=list(scratch),
        name=name,
    )(*args)


def begin(frac, velocity, force_old, species):
    outs = [((4, CAP), F32), ((4, CAP), F32), ((4 * R, CAP), F32), ((4 * R, CAP), F32)]
    return call(begin_kernel, "begin", (frac, velocity, force_old, species), outs, 4)


def prepare(codes, embed, w1, w2, wnt):
    outs = [
        ((2 * CH, NB + 16), BF16), ((3 * CH, CH), BF16), ((4 * CH, CH), BF16), ((CH, 16), BF16),
        ((R, K, CAP), jnp.int32), ((R, K, CAP), jnp.int32), ((144, K * W), BF16), ((CAP, K * W), BF16),
    ]
    return call(prepare_kernel, "prepare", (codes, embed, w1, w2, wnt), outs, 5)


def edges(count, we, plane, got_a, got_b, w1, w2, wnt, prepared):
    scratch = [
        pltpu.VMEM((144, CAP), F32),
        pltpu.VMEM((R, 3 * K, CAP), F32),
        pltpu.VMEM((R, K, CAP), F32),
        pltpu.VMEM((9, 8 * K, W), F32),
        pltpu.VMEM((8 * K, W), F32),
        pltpu.VMEM((CH, K * W), F32),
        pltpu.VMEM((CH, K * W), F32),
        pltpu.VMEM((3 * CH, K * W), F32),
        pltpu.VMEM((9, CH, W), F32),
        pltpu.VMEM((3 * CH, K * W), BF16),
        pltpu.VMEM((R, 9, 8 * K, CAP), F32),
        pltpu.VMEM((R, 8 * K, CAP), F32),
        pltpu.VMEM((R, 3 * K, CAP), F32),
        pltpu.VMEM((144, K * W), BF16),
    ]
    outs = [((48, CAP), F32), ((48, CAP), F32), ((48, CAP), F32), ((8, CAP), F32)]
    args = (count, we, w1, w2, wnt, plane, got_a, got_b, *prepared)
    return call(edges_kernel, "edges", args, outs, 5, smem=1, scratch=scratch)


def finish(count, column, got_a, got_b, own, mine, keep):
    outs = [((3, R, CAP), F32)] * 3 + [((R, CAP), F32)]
    return call(finish_kernel, "finish", (count, column, got_a, got_b, own, mine, keep), outs, 1, hbm_outs=True, smem=1)


def shards(
    frac, velocity, force_old, species, cell_count, neighbours, embed, w_radial_in, w_radial_out, w_node, w_energy
):
    even_y = lax.axis_index("gy") % 2 == 0
    even_z = lax.axis_index("gz") % 2 == 0
    vectors = (3, R, CAP)
    count = cell_count.reshape(R)
    wnt = w_node.T
    send_a, send_b, mine, keep = begin(
        frac.reshape(vectors), velocity.reshape(vectors), force_old.reshape(vectors), species.reshape(R, CAP)
    )
    prepared = prepare(neighbours.reshape(K * R, CAP), embed, w_radial_in, w_radial_out, wnt)

    got_a, got_b = swap(send_a, "gz", False), swap(send_b, "gz", True)
    column = jnp.concatenate(
        [jnp.where(even_z, got_b, got_a), mine, jnp.where(even_z, got_a, got_b)], axis=0
    )
    got_a, got_b = swap(column, "gy", False), swap(column, "gy", True)
    plane = jnp.concatenate(
        [jnp.where(even_y, got_b, got_a), column, jnp.where(even_y, got_a, got_b)], axis=0
    )
    got_a, got_b = swap(plane, "gx", False), swap(plane, "gx", True)

    plane, send_a, send_b, own = edges(
        count, w_energy.reshape(1, CH), plane, got_a, got_b, w_radial_in, w_radial_out, wnt, prepared
    )
    plane = plane + swap(send_a, "gx", False) + swap(send_b, "gx", True)
    lower, column, upper = plane[0:16], plane[16:32], plane[32:48]
    send_a, send_b = jnp.where(even_y, upper, lower), jnp.where(even_y, lower, upper)
    column = column + swap(send_a, "gy", False) + swap(send_b, "gy", True)
    send_a = jnp.where(even_z, column[12:16], column[0:4])
    send_b = jnp.where(even_z, column[0:4], column[12:16])
    got_a, got_b = swap(send_a, "gz", False), swap(send_b, "gz", True)
    next_frac, next_velocity, next_force, energy = finish(count, column, got_a, got_b, own, mine, keep)
    return (
        next_frac.reshape(frac.shape),
        next_velocity.reshape(frac.shape),
        next_force.reshape(frac.shape),
        energy.reshape(species.shape),
    )


def solution(mesh):
    cells = P(None, "gx", "gy", "gz", None)
    in_specs = (
        cells, cells, cells, P("gx", "gy", "gz", None), P("gx", "gy", "gz"), cells, P(), P(), P(), P(), P(),
    )
    out_specs = (cells, cells, cells, P("gx", "gy", "gz", None))
    return jax.shard_map(shards, mesh=mesh, in_specs=in_specs, out_specs=out_specs, check_vma=False)
```

```python
import jax
import jax.numpy as jnp
from jax import lax
from jax.experimental import pallas as pl
from jax.experimental.pallas import tpu as pltpu
from jax.sharding import PartitionSpec as P

MASSES = (1.008, 12.011, 14.007, 15.999, 32.06, 22.99, 35.45, 39.098, 24.305, 40.078)
SQRT3 = 1.7320508075688772
HALF_SQRT3 = 0.8660254037844386
TIME_STEP = 0.5

K = 16
CAP = 128
R = 2
W = R * CAP
CH = 64
NB = 8
GROUP = 8
F32 = jnp.float32
BF16 = jnp.bfloat16


def swap(array, axis, odd):
    n = lax.axis_size(axis)
    if odd:
        pairs = [(i, (i + 1) % n if i % 2 else (i - 1) % n) for i in range(n)]
    else:
        pairs = [(i, i ^ 1) for i in range(n)]
    return lax.ppermute(array, axis, pairs)


def rows8(row, width):
    return jnp.broadcast_to(row, (8, width))


def wide(ref, row, height):
    parts = [jnp.broadcast_to(ref[r, pl.ds(row, 1), :], (height, CAP)) for r in range(R)]
    return jnp.concatenate(parts, axis=1)


def begin_kernel(frac_ref, vel_ref, force_ref, kind_ref, send_a_ref, send_b_ref, mine_ref, keep_ref):
    kind = kind_ref[...]
    mass = jnp.zeros((R, CAP), F32)
    for number, value in enumerate(MASSES):
        mass = jnp.where(kind == number, jnp.float32(value) / jnp.float32(16.0), mass)
    for c in range(3):
        half = vel_ref[c] + 0.5 * TIME_STEP * force_ref[c] / mass
        moved = frac_ref[c] + TIME_STEP * half
        for r in range(R):
            mine_ref[r * 4 + c:r * 4 + c + 1, :] = moved[r:r + 1]
            keep_ref[r * 4 + c:r * 4 + c + 1, :] = half[r:r + 1]
    for r in range(R):
        mine_ref[r * 4 + 3:r * 4 + 4, :] = kind[r:r + 1].astype(F32)
        keep_ref[r * 4 + 3:r * 4 + 4, :] = mass[r:r + 1]
    even = lax.axis_index("gz") % 2 == 0
    send_a_ref[...] = jnp.where(even, mine_ref[4:8, :], mine_ref[0:4, :])
    send_b_ref[...] = jnp.where(even, mine_ref[0:4, :], mine_ref[4:8, :])


def early_kernel(mine_ref, keep_ref, own_ref, occ_ref, speed_ref, gain_ref, frac_ref, energy_ref):
    for r in range(R):
        occupied = occ_ref[:, r * CAP:(r + 1) * CAP]
        keep = keep_ref[r * 4:r * 4 + 4, :]
        gain = occupied * (0.5 * TIME_STEP) / keep[3:4]
        own = own_ref[r * 4:r * 4 + 4, :]
        place = occupied * mine_ref[r * 4:r * 4 + 4, :]
        speed_ref[r * 4:r * 4 + 4, :] = occupied * keep
        gain_ref[r * 4:r * 4 + 4, :] = jnp.concatenate([gain, occupied, gain, occupied], axis=0)
        for c in range(3):
            frac_ref[c, r:r + 1, :] = place[c:c + 1]
        energy_ref[r:r + 1, :] = own[3:4]


def finish_kernel(mid_ref, got_a_ref, got_b_ref, own_ref, speed_ref, gain_ref, vel_ref, force_ref):
    even = lax.axis_index("gz") % 2 == 0
    got = (
        jnp.where(even, got_b_ref[...], got_a_ref[...]),
        jnp.where(even, got_a_ref[...], got_b_ref[...]),
    )
    for r in range(R):
        gain = gain_ref[r * 4:r * 4 + 1, :]
        occupied = gain_ref[r * 4 + 1:r * 4 + 2, :]
        force = mid_ref[4 * (r + 1):4 * (r + 2), :] + own_ref[r * 4:r * 4 + 4, :] + got[r]
        speed = speed_ref[r * 4:r * 4 + 4, :] + gain * force
        force = occupied * force
        for c in range(3):
            force_ref[c, r:r + 1, :] = force[c:c + 1]
            vel_ref[c, r:r + 1, :] = speed[c:c + 1]


def prepare_kernel(
    count_ref, codes_ref, emb_ref, w1_ref, w2_ref, wnt_ref, we_ref,
    occ_ref, web_ref, w1c_ref, w2c_ref, wntc_ref, wc_ref, w2t_ref, wn_ref, embt_ref, off_ref, slot_ref, cell_ref, pick_ref,
):
    slot_number = lax.broadcasted_iota(jnp.int32, (1, CAP), 1)
    for r in range(R):
        occ_ref[:, r * CAP:(r + 1) * CAP] = jnp.where(slot_number < count_ref[r], 1.0, 0.0)
    web_ref[...] = jnp.broadcast_to(we_ref[...], (CAP, CH)).T
    w1c_ref[...] = w1_ref[...]
    w2c_ref[...] = w2_ref[...]
    wntc_ref[...] = wnt_ref[...]
    wc_ref[...] = jnp.zeros(wc_ref.shape, BF16)
    wc_ref[0:CH, 0:NB] = w1_ref[...].astype(F32).T.astype(BF16)
    emb = jnp.concatenate([emb_ref[...].astype(F32), jnp.zeros((6, CH), F32)], axis=0)
    embt = emb.T.astype(BF16)
    wc_ref[CH:, NB:NB + 16] = embt
    embt_ref[...] = embt
    w2t_ref[...] = w2_ref[...].astype(F32).T.astype(BF16)
    wn_ref[...] = wnt_ref[...].astype(F32).T.astype(BF16)
    row_cell = lax.broadcasted_iota(jnp.int32, (144, CAP), 0) // 4
    slots = lax.broadcasted_iota(jnp.int32, (CAP, CAP), 1).astype(F32)
    for r in range(R):
        code = codes_ref[pl.ds(r, K, stride=R), :]
        off = code // CAP
        slot = code % CAP
        off_ref[r] = off
        slot_ref[r] = slot
        cell = off // 3 * 4 + off % 3 + r
        slot_rows = jnp.concatenate([slot.astype(F32), jnp.zeros((CAP - K, CAP), F32)], axis=0).T
        for k in range(K):
            lanes = slice(k * W + r * CAP, k * W + (r + 1) * CAP)
            cell_ref[:, lanes] = jnp.where(jnp.broadcast_to(cell[k:k + 1], (144, CAP)) == row_cell, 1.0, 0.0).astype(BF16)
            pick_ref[lanes, :] = jnp.where(slot_rows[:, k:k + 1] == slots, 1.0, 0.0).astype(BF16)


def edges_kernel(
    plane_ref, got_a_ref, got_b_ref, occ_ref, web_ref, w1_ref, w2_ref, wnt_ref, wc_ref, w2t_ref, wn_ref, embt_ref, off_ref, slot_ref, cell_ref, pick_ref,
    mid_ref, send_a_ref, send_b_ref, own_ref,
    pos_s, d_s, kd_s, ey_s, eyb_s, exu_s, ds_s, feat_s, q_s, qb_s, m_s, mb_s, gr_s, t_s, ts_s, g_s, a_s,
):
    even = lax.axis_index("gx") % 2 == 0
    pos_s[0:48] = jnp.where(even, got_b_ref[...], got_a_ref[...])
    pos_s[48:96] = plane_ref[...]
    pos_s[96:144] = jnp.where(even, got_a_ref[...], got_b_ref[...])

    acc = [jnp.zeros((8, CAP), F32) for _ in range(16)]
    offs = [[off_ref[r, h * 8:(h + 1) * 8, :] for h in range(2)] for r in range(R)]
    slots = [[slot_ref[r, h * 8:(h + 1) * 8, :] for h in range(2)] for r in range(R)]
    for col in range(9):
        for zz in range(4):
            rows = [rows8(pos_s[col * 16 + zz * 4 + q:col * 16 + zz * 4 + q + 1, :], CAP) for q in range(4)]
            for r in range(R):
                dz = zz - r
                if not 0 <= dz <= 2:
                    continue
                for h in range(2):
                    hit = offs[r][h] == col * 3 + dz
                    for q in range(4):
                        got = jnp.take_along_axis(rows[q], slots[r][h], axis=1, mode="promise_in_bounds")
                        at = (r * 2 + h) * 4 + q
                        acc[at] = jnp.where(hit, got, acc[at])
    for r in range(R):
        own = [pos_s[64 + (1 + r) * 4 + c:64 + (1 + r) * 4 + c + 1, :] for c in range(3)]
        for h in range(2):
            off = offs[r][h]
            shift = (off // 9 - 1, off // 3 % 3 - 1, off % 3 - 1)
            for c in range(3):
                value = shift[c].astype(F32) + acc[(r * 2 + h) * 4 + c] - rows8(own[c], CAP)
                d_s[r, c * K + h * 8:c * K + h * 8 + 8, :] = value
            kd_s[r, h * 8:h * 8 + 8, :] = acc[(r * 2 + h) * 4 + 3]

    centre = lax.broadcasted_iota(jnp.int32, (8, W), 0).astype(F32) / (NB - 1)
    kinds16 = lax.broadcasted_iota(jnp.int32, (16, W), 0).astype(F32)

    def radial_group(group, _):
        inputs = []
        for j in range(GROUP):
            k = group * GROUP + j
            x = wide(d_s, k, 8)
            y = wide(d_s, K + k, 8)
            z = wide(d_s, 2 * K + k, 8)
            xx, yy, zz = x * x, y * y, z * z
            s = xx + yy + zz
            m1 = jnp.maximum(1.0 - s, 0.0)
            env = m1 * m1 * m1
            u = s - centre
            ex = jnp.exp(-float((NB - 1) ** 2) * (u * u))
            at = k * 8
            exu_s[pl.ds(at, 8), :] = ex * (u * (-2.0 * float((NB - 1) ** 2)))
            ex3 = env * SQRT3
            terms = (
                env, env * x, env * y, env * z, ex3 * (x * y), ex3 * (y * z), ex3 * (z * x),
                (env * HALF_SQRT3) * (xx - yy), (env * 0.5) * (2.0 * zz - xx - yy),
            )
            for m in range(9):
                ey_s[m, pl.ds(at, 8), :] = terms[m]
                eyb_s[m, k * 16:(k + 1) * 16, :] = jnp.concatenate([terms[m]] * 2, axis=0).astype(BF16)
            kind = wide(kd_s, k, 16)
            onehot = jnp.where(kind == kinds16, 1.0, 0.0)
            inputs.append(jnp.concatenate([ex, onehot], axis=0))
        rhs = jnp.concatenate(inputs, axis=1).astype(BF16)
        lanes = pl.ds(group * (GROUP * W), GROUP * W)
        first = jnp.dot(wc_ref[...], rhs, preferred_element_type=F32)
        pre = first[:CH]
        feat = first[CH:]
        sig = 0.5 * jnp.tanh(0.5 * pre) + 0.5
        hidden = (pre * sig).astype(BF16)
        ds_s[:, lanes] = sig * (1.0 + pre * (1.0 - sig))
        feat_s[:, lanes] = feat.astype(BF16)
        radial = jnp.dot(w2t_ref[...], hidden, preferred_element_type=F32)
        for deg in range(3):
            carried = radial[deg * CH:(deg + 1) * CH] * feat
            q_s[deg * CH:(deg + 1) * CH, lanes] = carried
            qb_s[deg * CH:(deg + 1) * CH, lanes] = carried.astype(BF16)
        return 0

    for group in range(K // GROUP):
        radial_group(group, 0)

    def message_block(cb, _):
        base = cb * 16
        for r in range(R):
            sums = [None] * 9
            for k in range(K):
                lo = k * W + r * CAP
                q = [q_s[pl.ds(deg * CH + base, 16), lo:lo + CAP] for deg in range(3)]
                for m in range(9):
                    weight = ey_s[m, k * 8:(k + 1) * 8, r * CAP:(r + 1) * CAP]
                    weight = jnp.concatenate([weight, weight], axis=0)
                    term = q[0 if m == 0 else 1 if m < 4 else 2] * weight
                    sums[m] = term if sums[m] is None else sums[m] + term
            for m in range(9):
                m_s[m, pl.ds(base, 16), r * CAP:(r + 1) * CAP] = sums[m]
        return 0

    for cb in range(CH // 16):
        message_block(cb, 0)

    own_kind = jnp.concatenate(
        [jnp.broadcast_to(pos_s[64 + (1 + r) * 4 + 3:64 + (1 + r) * 4 + 4, :], (16, CAP)) for r in range(R)], axis=1
    )
    own_feat = jnp.dot(
        embt_ref[...], jnp.where(own_kind == kinds16, 1.0, 0.0).astype(BF16), preferred_element_type=F32
    )
    occupied = occ_ref[...]
    vec = m_s[1] * m_s[1] + m_s[2] * m_s[2] + m_s[3] * m_s[3]
    ten = m_s[4] * m_s[4] + m_s[5] * m_s[5] + m_s[6] * m_s[6] + m_s[7] * m_s[7] + m_s[8] * m_s[8]
    invariant = jnp.concatenate([m_s[0], vec, ten, own_feat], axis=0).astype(BF16)
    pre = jnp.dot(wnt_ref[...], invariant, preferred_element_type=F32)
    sig = 0.5 * jnp.tanh(0.5 * pre) + 0.5
    we = jnp.concatenate([web_ref[...]] * R, axis=1)
    energy = jnp.sum(we * (pre * sig), axis=0, keepdims=True) * occupied
    gpre = we * occupied * (sig * (1.0 + pre * (1.0 - sig)))
    ginv = jnp.dot(wn_ref[0:3 * CH, :], gpre.astype(BF16), preferred_element_type=F32).astype(BF16).astype(F32)
    mb_s[0] = ginv[:CH].astype(BF16)
    gvec = 2.0 * ginv[CH:2 * CH]
    gten = 2.0 * ginv[2 * CH:]
    for m in range(1, 9):
        mb_s[m] = (m_s[m] * (gvec if m < 4 else gten)).astype(BF16)

    def carried_back(k, _):
        at = k * 8
        for r in range(R):
            cols = slice(r * CAP, (r + 1) * CAP)
            lanes = pl.ds(k * W + r * CAP, CAP)
            weight = [eyb_s[m, k * 16:(k + 1) * 16, cols] for m in range(9)]
            sums = [None] * 9
            for cb in range(CH // 16):
                feat = feat_s[cb * 16:(cb + 1) * 16, lanes]
                q = [qb_s[deg * CH + cb * 16:deg * CH + (cb + 1) * 16, lanes] for deg in range(3)]
                back = [None] * 3
                for m in range(9):
                    deg = 0 if m == 0 else 1 if m < 4 else 2
                    cot = mb_s[m, cb * 16:(cb + 1) * 16, cols]
                    term = cot * q[deg]
                    sums[m] = term if sums[m] is None else sums[m] + term
                    term = cot * weight[m]
                    back[deg] = term if back[deg] is None else back[deg] + term
                for deg in range(3):
                    gr_s[deg * CH + cb * 16:deg * CH + (cb + 1) * 16, lanes] = back[deg] * feat
            for m in range(9):
                both = sums[m].astype(F32)
                t_s[r, m, pl.ds(at, 8), :] = both[:8] + both[8:]
        return 0

    for k in range(K):
        carried_back(k, 0)

    def radial_back(group, _):
        lanes = pl.ds(group * (GROUP * W), GROUP * W)
        ghid = jnp.dot(w2_ref[...], gr_s[:, lanes], preferred_element_type=F32)
        gpre = (ghid.astype(BF16).astype(F32) * ds_s[:, lanes]).astype(BF16)
        gbas = jnp.dot(w1_ref[...], gpre, preferred_element_type=F32).astype(BF16).astype(F32)
        for j in range(GROUP):
            at = (group * GROUP + j) * 8
            for r in range(R):
                lo = j * W + r * CAP
                ts_s[r, pl.ds(at, 8), :] = gbas[:, lo:lo + CAP] * exu_s[pl.ds(at, 8), r * CAP:(r + 1) * CAP]
        return 0

    for group in range(K // GROUP):
        radial_back(group, 0)

    def total(ref):
        out = ref[pl.ds(0, K, stride=8), :]
        for sub in range(1, 8):
            out = out + ref[pl.ds(sub, K, stride=8), :]
        return out

    for r in range(R):
        cols = slice(r * CAP, (r + 1) * CAP)
        x, y, z = d_s[r, 0:K, :], d_s[r, K:2 * K, :], d_s[r, 2 * K:3 * K, :]
        xx, yy, zz = x * x, y * y, z * z
        s = xx + yy + zz
        m1 = jnp.maximum(1.0 - s, 0.0)
        env = m1 * m1 * m1
        t = [total(t_s.at[r, m]) for m in range(9)]
        harm = (
            None, x, y, z, SQRT3 * (x * y), SQRT3 * (y * z), SQRT3 * (z * x),
            HALF_SQRT3 * (xx - yy), 0.5 * (2.0 * zz - xx - yy),
        )
        genv = t[0]
        for m in range(1, 9):
            genv = genv + harm[m] * t[m]
        gs2 = 2.0 * (total(ts_s.at[r]) - 3.0 * (m1 * m1) * genv)
        e = [env * v for v in t]
        gx = e[1] + SQRT3 * (y * e[4] + z * e[6]) + x * (SQRT3 * e[7] - e[8] + gs2)
        gy = e[2] + SQRT3 * (x * e[4] + z * e[5]) + y * (gs2 - SQRT3 * e[7] - e[8])
        gz = e[3] + SQRT3 * (y * e[5] + x * e[6]) + z * (2.0 * e[8] + gs2)
        for c, g in enumerate((gx, gy, gz)):
            g_s[r, c * K:(c + 1) * K, :] = g
            own_ref[r * 4 + c:r * 4 + c + 1, :] = jnp.sum(g, axis=0, keepdims=True)
        own_ref[r * 4 + 3:r * 4 + 4, :] = energy[:, cols]

    sub = lax.broadcasted_iota(jnp.int32, (16, CAP), 0)
    comp = sub % 4
    for k in range(K):
        for r in range(R):
            lanes = slice(k * W + r * CAP, k * W + (r + 1) * CAP)
            gx, gy, gz = (jnp.broadcast_to(g_s[r, c * K + k:c * K + k + 1, :], (16, CAP)) for c in range(3))
            mixed = jnp.where(comp == 0, gx, jnp.where(comp == 1, gy, jnp.where(comp == 2, gz, 0.0)))
            mixed = (-mixed).astype(BF16)
            for j in range(9):
                a_s[j * 16:(j + 1) * 16, lanes] = cell_ref[j * 16:(j + 1) * 16, lanes] * mixed
    out = jnp.dot(a_s[...], pick_ref[...], preferred_element_type=F32)
    mid_ref[...] = out[48:96]
    send_a_ref[...] = jnp.where(even, out[96:144], out[0:48]).astype(BF16)
    send_b_ref[...] = jnp.where(even, out[0:48], out[96:144]).astype(BF16)


VMEM = pl.BlockSpec(memory_space=pltpu.VMEM)
SMEM = pl.BlockSpec(memory_space=pltpu.SMEM)


def call(kernel, name, args, outs, near, far=0, smem=0, scratch=()):
    args = args[:near] + tuple(pltpu.with_memory_space_constraint(a, pltpu.VMEM) for a in args[near:])
    return pl.pallas_call(
        kernel,
        in_specs=[SMEM] * smem + [VMEM] * (len(args) - smem),
        out_specs=[VMEM] * len(outs),
        out_shape=[(pltpu.VMEM if i < len(outs) - far else jax.ShapeDtypeStruct)(*out) for i, out in enumerate(outs)],
        scratch_shapes=list(scratch),
        name=name,
    )(*args)


def begin(frac, velocity, force_old, species):
    outs = [((4, CAP), F32), ((4, CAP), F32), ((4 * R, CAP), F32), ((4 * R, CAP), F32)]
    return call(begin_kernel, "begin", (frac, velocity, force_old, species), outs, 4)


def prepare(count, codes, embed, w1, w2, wnt, we):
    outs = [
        ((1, W), F32), ((CH, CAP), F32), ((NB, CH), BF16), ((CH, 3 * CH), BF16), ((CH, 4 * CH), BF16),
        ((2 * CH, NB + 16), BF16), ((3 * CH, CH), BF16), ((4 * CH, CH), BF16), ((CH, 16), BF16),
        ((R, K, CAP), jnp.int32), ((R, K, CAP), jnp.int32), ((144, K * W), BF16), ((K * W, CAP), BF16),
    ]
    return call(prepare_kernel, "prepare", (count, codes, embed, w1, w2, wnt, we), outs, 7, smem=1)


def edges(plane, got_a, got_b, prepared):
    scratch = [
        pltpu.VMEM((144, CAP), F32),
        pltpu.VMEM((R, 3 * K, CAP), F32),
        pltpu.VMEM((R, K, CAP), F32),
        pltpu.VMEM((9, 8 * K, W), F32),
        pltpu.VMEM((9, 16 * K, W), BF16),
        pltpu.VMEM((8 * K, W), F32),
        pltpu.VMEM((CH, K * W), F32),
        pltpu.VMEM((CH, K * W), BF16),
        pltpu.VMEM((3 * CH, K * W), F32),
        pltpu.VMEM((3 * CH, K * W), BF16),
        pltpu.VMEM((9, CH, W), F32),
        pltpu.VMEM((9, CH, W), BF16),
        pltpu.VMEM((3 * CH, K * W), BF16),
        pltpu.VMEM((R, 9, 8 * K, CAP), F32),
        pltpu.VMEM((R, 8 * K, CAP), F32),
        pltpu.VMEM((R, 3 * K, CAP), F32),
        pltpu.VMEM((144, K * W), BF16),
    ]
    outs = [((48, CAP), F32), ((48, CAP), BF16), ((48, CAP), BF16), ((8, CAP), F32)]
    return call(edges_kernel, "edges", (plane, got_a, got_b, *prepared), outs, 0, scratch=scratch)


def early(mine, keep, own, prepared):
    outs = [((4 * R, CAP), F32), ((4 * R, CAP), F32), ((3, R, CAP), F32), ((R, CAP), F32)]
    return call(early_kernel, "early", (mine, keep, own, prepared[0]), outs, 0, far=2)


def finish(column, got_a, got_b, own, speed, gain):
    outs = [((3, R, CAP), F32)] * 2
    return call(finish_kernel, "finish", (column, got_a, got_b, own, speed, gain), outs, 0, far=2)


def shards(
    frac, velocity, force_old, species, cell_count, neighbours, embed, w_radial_in, w_radial_out, w_node, w_energy
):
    even_y = lax.axis_index("gy") % 2 == 0
    even_z = lax.axis_index("gz") % 2 == 0
    vectors = (3, R, CAP)
    count = cell_count.reshape(R)
    wnt = w_node.T
    send_a, send_b, mine, keep = begin(
        frac.reshape(vectors), velocity.reshape(vectors), force_old.reshape(vectors), species.reshape(R, CAP)
    )
    prepared = prepare(
        count, neighbours.reshape(K * R, CAP), embed, w_radial_in, w_radial_out, wnt, w_energy.reshape(1, CH)
    )

    got_a, got_b = swap(send_a, "gz", False), swap(send_b, "gz", True)
    column = jnp.concatenate(
        [jnp.where(even_z, got_b, got_a), mine, jnp.where(even_z, got_a, got_b)], axis=0
    )
    got_a, got_b = swap(column, "gy", False), swap(column, "gy", True)
    plane = jnp.concatenate(
        [jnp.where(even_y, got_b, got_a), column, jnp.where(even_y, got_a, got_b)], axis=0
    )
    got_a, got_b = swap(plane, "gx", False), swap(plane, "gx", True)

    plane, send_a, send_b, own = edges(plane, got_a, got_b, prepared)
    speed, gain, next_frac, energy = early(mine, keep, own, prepared)
    plane = plane + swap(send_a, "gx", False).astype(F32) + swap(send_b, "gx", True).astype(F32)
    lower, column, upper = plane[0:16], plane[16:32], plane[32:48]
    send_a, send_b = jnp.where(even_y, upper, lower), jnp.where(even_y, lower, upper)
    column = column + swap(send_a, "gy", False) + swap(send_b, "gy", True)
    send_a = jnp.where(even_z, column[12:16], column[0:4])
    send_b = jnp.where(even_z, column[0:4], column[12:16])
    got_a, got_b = swap(send_a, "gz", False), swap(send_b, "gz", True)
    next_velocity, next_force = finish(column, got_a, got_b, own, speed, gain)
    return (
        next_frac.reshape(frac.shape),
        next_velocity.reshape(frac.shape),
        next_force.reshape(frac.shape),
        energy.reshape(species.shape),
    )


def solution(mesh):
    cells = P(None, "gx", "gy", "gz", None)
    in_specs = (
        cells, cells, cells, P("gx", "gy", "gz", None), P("gx", "gy", "gz"), cells, P(), P(), P(), P(), P(),
    )
    out_specs = (cells, cells, cells, P("gx", "gy", "gz", None))
    return jax.shard_map(shards, mesh=mesh, in_specs=in_specs, out_specs=out_specs, check_vma=False)
```

```python
import jax
import jax.numpy as jnp
from jax import lax
from jax.experimental import pallas as pl
from jax.experimental.pallas import tpu as pltpu
from jax.sharding import PartitionSpec as P

MASSES = (1.008, 12.011, 14.007, 15.999, 32.06, 22.99, 35.45, 39.098, 24.305, 40.078)
SQRT3 = 1.7320508075688772
HALF_SQRT3 = 0.8660254037844386
TIME_STEP = 0.5

K = 16
CAP = 128
R = 2
W = R * CAP
CH = 64
NB = 8
GROUP = 8
EDGES_LIMIT = 40 << 20
F32 = jnp.float32
BF16 = jnp.bfloat16


def swap(array, axis, odd):
    n = lax.axis_size(axis)
    if odd:
        pairs = [(i, (i + 1) % n if i % 2 else (i - 1) % n) for i in range(n)]
    else:
        pairs = [(i, i ^ 1) for i in range(n)]
    return lax.ppermute(array, axis, pairs)


def rows8(row, width):
    return jnp.broadcast_to(row, (8, width))


def wide(ref, row, height):
    parts = [jnp.broadcast_to(ref[r, pl.ds(row, 1), :], (height, CAP)) for r in range(R)]
    return jnp.concatenate(parts, axis=1)


def begin_kernel(frac_ref, vel_ref, force_ref, kind_ref, send_a_ref, send_b_ref, mine_ref, keep_ref):
    kind = kind_ref[...]
    mass = jnp.zeros((R, CAP), F32)
    for number, value in enumerate(MASSES):
        mass = jnp.where(kind == number, jnp.float32(value) / jnp.float32(16.0), mass)
    for c in range(3):
        half = vel_ref[c] + 0.5 * TIME_STEP * force_ref[c] / mass
        moved = frac_ref[c] + TIME_STEP * half
        for r in range(R):
            mine_ref[r * 4 + c:r * 4 + c + 1, :] = moved[r:r + 1]
            keep_ref[r * 4 + c:r * 4 + c + 1, :] = half[r:r + 1]
    for r in range(R):
        mine_ref[r * 4 + 3:r * 4 + 4, :] = kind[r:r + 1].astype(F32)
        keep_ref[r * 4 + 3:r * 4 + 4, :] = mass[r:r + 1]
    even = lax.axis_index("gz") % 2 == 0
    send_a_ref[...] = jnp.where(even, mine_ref[4:8, :], mine_ref[0:4, :])
    send_b_ref[...] = jnp.where(even, mine_ref[0:4, :], mine_ref[4:8, :])


def early_kernel(mine_ref, keep_ref, own_ref, occ_ref, speed_ref, gain_ref, frac_ref, energy_ref):
    for r in range(R):
        occupied = occ_ref[:, r * CAP:(r + 1) * CAP]
        keep = keep_ref[r * 4:r * 4 + 4, :]
        gain = occupied * (0.5 * TIME_STEP) / keep[3:4]
        own = own_ref[r * 4:r * 4 + 4, :]
        place = occupied * mine_ref[r * 4:r * 4 + 4, :]
        speed_ref[r * 4:r * 4 + 4, :] = occupied * keep
        gain_ref[r * 4:r * 4 + 4, :] = jnp.concatenate([gain, occupied, gain, occupied], axis=0)
        for c in range(3):
            frac_ref[c, r:r + 1, :] = place[c:c + 1]
        energy_ref[r:r + 1, :] = own[3:4]


def finish_kernel(mid_ref, got_a_ref, got_b_ref, own_ref, speed_ref, gain_ref, vel_ref, force_ref):
    even = lax.axis_index("gz") % 2 == 0
    got = (
        jnp.where(even, got_b_ref[...], got_a_ref[...]),
        jnp.where(even, got_a_ref[...], got_b_ref[...]),
    )
    for r in range(R):
        gain = gain_ref[r * 4:r * 4 + 1, :]
        occupied = gain_ref[r * 4 + 1:r * 4 + 2, :]
        force = mid_ref[4 * (r + 1):4 * (r + 2), :] + own_ref[r * 4:r * 4 + 4, :] + got[r]
        speed = speed_ref[r * 4:r * 4 + 4, :] + gain * force
        force = occupied * force
        for c in range(3):
            force_ref[c, r:r + 1, :] = force[c:c + 1]
            vel_ref[c, r:r + 1, :] = speed[c:c + 1]


def prepare_kernel(
    count_ref, codes_ref, emb_ref, w1_ref, w2_ref, wnt_ref, we_ref,
    occ_ref, web_ref, w1c_ref, w2c_ref, wntc_ref, wc_ref, w2t_ref, wn_ref, embt_ref, off_ref, slot_ref, cell_ref, pick_ref,
):
    slot_number = lax.broadcasted_iota(jnp.int32, (1, CAP), 1)
    for r in range(R):
        occ_ref[:, r * CAP:(r + 1) * CAP] = jnp.where(slot_number < count_ref[r], 1.0, 0.0)
    web_ref[...] = jnp.broadcast_to(we_ref[...], (CAP, CH)).T
    w1c_ref[...] = w1_ref[...]
    w2c_ref[...] = w2_ref[...]
    wntc_ref[...] = wnt_ref[...]
    wc_ref[...] = jnp.zeros(wc_ref.shape, BF16)
    wc_ref[0:CH, 0:NB] = w1_ref[...].astype(F32).T.astype(BF16)
    emb = jnp.concatenate([emb_ref[...].astype(F32), jnp.zeros((6, CH), F32)], axis=0)
    embt = emb.T.astype(BF16)
    wc_ref[CH:, NB:NB + 16] = embt
    embt_ref[...] = embt
    w2t_ref[...] = w2_ref[...].astype(F32).T.astype(BF16)
    wn_ref[...] = wnt_ref[...].astype(F32).T.astype(BF16)
    row_cell = lax.broadcasted_iota(jnp.int32, (144, CAP), 0) // 4
    slots = lax.broadcasted_iota(jnp.int32, (CAP, CAP), 1).astype(F32)
    for r in range(R):
        code = codes_ref[pl.ds(r, K, stride=R), :]
        off = code // CAP
        slot = code % CAP
        off_ref[r] = off
        slot_ref[r] = slot
        cell = (off // 3 % 3 * 3 + off // 9) * 4 + off % 3 + r
        slot_rows = jnp.concatenate([slot.astype(F32), jnp.zeros((CAP - K, CAP), F32)], axis=0).T
        for k in range(K):
            lanes = slice(k * W + r * CAP, k * W + (r + 1) * CAP)
            cell_ref[:, lanes] = jnp.where(jnp.broadcast_to(cell[k:k + 1], (144, CAP)) == row_cell, 1.0, 0.0).astype(BF16)
            pick_ref[lanes, :] = jnp.where(slot_rows[:, k:k + 1] == slots, 1.0, 0.0).astype(BF16)


def edges_kernel(
    plane_ref, got_a_ref, got_b_ref, occ_ref, web_ref, w1_ref, w2_ref, wnt_ref, wc_ref, w2t_ref, wn_ref, embt_ref, off_ref, slot_ref, cell_ref, pick_ref,
    send_a_ref, send_b_ref, g_s, energy_ref,
    pos_s, d_s, kd_s, ey_s, eyb_s, exu_s, ds_s, feat_s, q_s, qb_s, m_s, mb_s, gr_s, t_s, ts_s, a_s,
):
    even = lax.axis_index("gy") % 2 == 0
    pos_s[0:48] = jnp.where(even, got_b_ref[...], got_a_ref[...])
    pos_s[48:96] = plane_ref[...]
    pos_s[96:144] = jnp.where(even, got_a_ref[...], got_b_ref[...])

    acc = [jnp.zeros((8, CAP), F32) for _ in range(16)]
    offs = [[off_ref[r, h * 8:(h + 1) * 8, :] for h in range(2)] for r in range(R)]
    slots = [[slot_ref[r, h * 8:(h + 1) * 8, :] for h in range(2)] for r in range(R)]
    for col in range(9):
        place = col % 3 * 3 + col // 3
        for zz in range(4):
            rows = [rows8(pos_s[place * 16 + zz * 4 + q:place * 16 + zz * 4 + q + 1, :], CAP) for q in range(4)]
            for r in range(R):
                dz = zz - r
                if not 0 <= dz <= 2:
                    continue
                for h in range(2):
                    hit = offs[r][h] == col * 3 + dz
                    for q in range(4):
                        got = jnp.take_along_axis(rows[q], slots[r][h], axis=1, mode="promise_in_bounds")
                        at = (r * 2 + h) * 4 + q
                        acc[at] = jnp.where(hit, got, acc[at])
    for r in range(R):
        own = [pos_s[64 + (1 + r) * 4 + c:64 + (1 + r) * 4 + c + 1, :] for c in range(3)]
        for h in range(2):
            off = offs[r][h]
            shift = (off // 9 - 1, off // 3 % 3 - 1, off % 3 - 1)
            for c in range(3):
                value = shift[c].astype(F32) + acc[(r * 2 + h) * 4 + c] - rows8(own[c], CAP)
                d_s[r, c * K + h * 8:c * K + h * 8 + 8, :] = value
            kd_s[r, h * 8:h * 8 + 8, :] = acc[(r * 2 + h) * 4 + 3]

    centre = lax.broadcasted_iota(jnp.int32, (8, W), 0).astype(F32) / (NB - 1)
    kinds16 = lax.broadcasted_iota(jnp.int32, (16, W), 0).astype(F32)

    def radial_group(group, _):
        inputs = []
        for j in range(GROUP):
            k = group * GROUP + j
            x = wide(d_s, k, 8)
            y = wide(d_s, K + k, 8)
            z = wide(d_s, 2 * K + k, 8)
            xx, yy, zz = x * x, y * y, z * z
            s = xx + yy + zz
            m1 = jnp.maximum(1.0 - s, 0.0)
            env = m1 * m1 * m1
            u = s - centre
            ex = jnp.exp(-float((NB - 1) ** 2) * (u * u))
            at = k * 8
            exu_s[pl.ds(at, 8), :] = ex * (u * (-2.0 * float((NB - 1) ** 2)))
            ex3 = env * SQRT3
            terms = (
                env, env * x, env * y, env * z, ex3 * (x * y), ex3 * (y * z), ex3 * (z * x),
                (env * HALF_SQRT3) * (xx - yy), (env * 0.5) * (2.0 * zz - xx - yy),
            )
            for m in range(9):
                ey_s[m, pl.ds(at, 8), :] = terms[m]
                eyb_s[m, k * 16:(k + 1) * 16, :] = jnp.concatenate([terms[m]] * 2, axis=0).astype(BF16)
            kind = wide(kd_s, k, 16)
            onehot = jnp.where(kind == kinds16, 1.0, 0.0)
            inputs.append(jnp.concatenate([ex, onehot], axis=0))
        rhs = jnp.concatenate(inputs, axis=1).astype(BF16)
        lanes = pl.ds(group * (GROUP * W), GROUP * W)
        first = jnp.dot(wc_ref[...], rhs, preferred_element_type=F32)
        pre = first[:CH]
        feat = first[CH:]
        sig = 0.5 * jnp.tanh(0.5 * pre) + 0.5
        hidden = (pre * sig).astype(BF16)
        ds_s[:, lanes] = sig * (1.0 + pre * (1.0 - sig))
        feat_s[:, lanes] = feat.astype(BF16)
        radial = jnp.dot(w2t_ref[...], hidden, preferred_element_type=F32)
        for deg in range(3):
            carried = radial[deg * CH:(deg + 1) * CH] * feat
            q_s[deg * CH:(deg + 1) * CH, lanes] = carried
            qb_s[deg * CH:(deg + 1) * CH, lanes] = carried.astype(BF16)
        return 0

    for group in range(K // GROUP):
        radial_group(group, 0)

    def message_block(cb, _):
        base = cb * 16
        for r in range(R):
            sums = [None] * 9
            for k in range(K):
                lo = k * W + r * CAP
                q = [q_s[pl.ds(deg * CH + base, 16), lo:lo + CAP] for deg in range(3)]
                for m in range(9):
                    weight = ey_s[m, k * 8:(k + 1) * 8, r * CAP:(r + 1) * CAP]
                    weight = jnp.concatenate([weight, weight], axis=0)
                    term = q[0 if m == 0 else 1 if m < 4 else 2] * weight
                    sums[m] = term if sums[m] is None else sums[m] + term
            for m in range(9):
                m_s[m, pl.ds(base, 16), r * CAP:(r + 1) * CAP] = sums[m]
        return 0

    for cb in range(CH // 16):
        message_block(cb, 0)

    own_kind = jnp.concatenate(
        [jnp.broadcast_to(pos_s[64 + (1 + r) * 4 + 3:64 + (1 + r) * 4 + 4, :], (16, CAP)) for r in range(R)], axis=1
    )
    own_feat = jnp.dot(
        embt_ref[...], jnp.where(own_kind == kinds16, 1.0, 0.0).astype(BF16), preferred_element_type=F32
    )
    occupied = occ_ref[...]
    vec = m_s[1] * m_s[1] + m_s[2] * m_s[2] + m_s[3] * m_s[3]
    ten = m_s[4] * m_s[4] + m_s[5] * m_s[5] + m_s[6] * m_s[6] + m_s[7] * m_s[7] + m_s[8] * m_s[8]
    invariant = jnp.concatenate([m_s[0], vec, ten, own_feat], axis=0).astype(BF16)
    pre = jnp.dot(wnt_ref[...], invariant, preferred_element_type=F32)
    sig = 0.5 * jnp.tanh(0.5 * pre) + 0.5
    we = jnp.concatenate([web_ref[...]] * R, axis=1)
    energy = jnp.sum(we * (pre * sig), axis=0, keepdims=True) * occupied
    gpre = we * occupied * (sig * (1.0 + pre * (1.0 - sig)))
    ginv = jnp.dot(wn_ref[0:3 * CH, :], gpre.astype(BF16), preferred_element_type=F32).astype(BF16).astype(F32)
    mb_s[0] = ginv[:CH].astype(BF16)
    gvec = 2.0 * ginv[CH:2 * CH]
    gten = 2.0 * ginv[2 * CH:]
    for m in range(1, 9):
        mb_s[m] = (m_s[m] * (gvec if m < 4 else gten)).astype(BF16)

    def carried_back(k, _):
        at = k * 8
        for r in range(R):
            cols = slice(r * CAP, (r + 1) * CAP)
            lanes = pl.ds(k * W + r * CAP, CAP)
            weight = [eyb_s[m, k * 16:(k + 1) * 16, cols] for m in range(9)]
            sums = [None] * 9
            for cb in range(CH // 16):
                feat = feat_s[cb * 16:(cb + 1) * 16, lanes]
                q = [qb_s[deg * CH + cb * 16:deg * CH + (cb + 1) * 16, lanes] for deg in range(3)]
                back = [None] * 3
                for m in range(9):
                    deg = 0 if m == 0 else 1 if m < 4 else 2
                    cot = mb_s[m, cb * 16:(cb + 1) * 16, cols]
                    term = cot * q[deg]
                    sums[m] = term if sums[m] is None else sums[m] + term
                    term = cot * weight[m]
                    back[deg] = term if back[deg] is None else back[deg] + term
                for deg in range(3):
                    gr_s[deg * CH + cb * 16:deg * CH + (cb + 1) * 16, lanes] = back[deg] * feat
            for m in range(9):
                both = sums[m].astype(F32)
                t_s[r, m, pl.ds(at, 8), :] = both[:8] + both[8:]
        return 0

    for k in range(K):
        carried_back(k, 0)

    def radial_back(group, _):
        lanes = pl.ds(group * (GROUP * W), GROUP * W)
        ghid = jnp.dot(w2_ref[...], gr_s[:, lanes], preferred_element_type=F32)
        gpre = (ghid.astype(BF16).astype(F32) * ds_s[:, lanes]).astype(BF16)
        gbas = jnp.dot(w1_ref[...], gpre, preferred_element_type=F32).astype(BF16).astype(F32)
        for j in range(GROUP):
            at = (group * GROUP + j) * 8
            for r in range(R):
                lo = j * W + r * CAP
                ts_s[r, pl.ds(at, 8), :] = gbas[:, lo:lo + CAP] * exu_s[pl.ds(at, 8), r * CAP:(r + 1) * CAP]
        return 0

    for group in range(K // GROUP):
        radial_back(group, 0)

    def total(ref):
        out = ref[pl.ds(0, K, stride=8), :]
        for sub in range(1, 8):
            out = out + ref[pl.ds(sub, K, stride=8), :]
        return out

    for r in range(R):
        cols = slice(r * CAP, (r + 1) * CAP)
        x, y, z = d_s[r, 0:K, :], d_s[r, K:2 * K, :], d_s[r, 2 * K:3 * K, :]
        xx, yy, zz = x * x, y * y, z * z
        s = xx + yy + zz
        m1 = jnp.maximum(1.0 - s, 0.0)
        env = m1 * m1 * m1
        t = [total(t_s.at[r, m]) for m in range(9)]
        harm = (
            None, x, y, z, SQRT3 * (x * y), SQRT3 * (y * z), SQRT3 * (z * x),
            HALF_SQRT3 * (xx - yy), 0.5 * (2.0 * zz - xx - yy),
        )
        genv = t[0]
        for m in range(1, 9):
            genv = genv + harm[m] * t[m]
        gs2 = 2.0 * (total(ts_s.at[r]) - 3.0 * (m1 * m1) * genv)
        e = [env * v for v in t]
        gx = e[1] + SQRT3 * (y * e[4] + z * e[6]) + x * (SQRT3 * e[7] - e[8] + gs2)
        gy = e[2] + SQRT3 * (x * e[4] + z * e[5]) + y * (gs2 - SQRT3 * e[7] - e[8])
        gz = e[3] + SQRT3 * (y * e[5] + x * e[6]) + z * (2.0 * e[8] + gs2)
        for c, g in enumerate((gx, gy, gz)):
            g_s[r, c * K:(c + 1) * K, :] = g
    energy_ref[...] = energy

    scatter_inputs(g_s, cell_ref, a_s, ((0, 0), (96, 48)))
    out = jnp.dot(a_s[...], pick_ref[...], preferred_element_type=F32)
    send_a_ref[...] = jnp.where(even, out[48:96], out[0:48]).astype(BF16)
    send_b_ref[...] = jnp.where(even, out[0:48], out[48:96]).astype(BF16)


def scatter_inputs(g_ref, cell_ref, a_ref, blocks):
    comp = lax.broadcasted_iota(jnp.int32, (16, CAP), 0) % 4
    for k in range(K):
        for r in range(R):
            lanes = slice(k * W + r * CAP, k * W + (r + 1) * CAP)
            gx, gy, gz = (jnp.broadcast_to(g_ref[r, c * K + k:c * K + k + 1, :], (16, CAP)) for c in range(3))
            mixed = jnp.where(comp == 0, gx, jnp.where(comp == 1, gy, jnp.where(comp == 2, gz, 0.0)))
            mixed = (-mixed).astype(BF16)
            for take, put in blocks:
                for j in range(0, 48, 16):
                    a_ref[put + j:put + j + 16, lanes] = cell_ref[take + j:take + j + 16, lanes] * mixed


def near_kernel(g_ref, energy_ref, cell_ref, pick_ref, mid_ref, own_ref, a_s):
    scatter_inputs(g_ref, cell_ref, a_s, ((48, 0),))
    mid_ref[...] = jnp.dot(a_s[...], pick_ref[...], preferred_element_type=F32)
    for r in range(R):
        for c in range(3):
            own_ref[r * 4 + c:r * 4 + c + 1, :] = jnp.sum(g_ref[r, c * K:(c + 1) * K, :], axis=0, keepdims=True)
        own_ref[r * 4 + 3:r * 4 + 4, :] = energy_ref[:, r * CAP:(r + 1) * CAP]


VMEM = pl.BlockSpec(memory_space=pltpu.VMEM)
SMEM = pl.BlockSpec(memory_space=pltpu.SMEM)


def call(kernel, name, args, outs, near, far=0, smem=0, scratch=(), limit=None):
    args = args[:near] + tuple(pltpu.with_memory_space_constraint(a, pltpu.VMEM) for a in args[near:])
    return pl.pallas_call(
        kernel,
        in_specs=[SMEM] * smem + [VMEM] * (len(args) - smem),
        out_specs=[VMEM] * len(outs),
        out_shape=[(pltpu.VMEM if i < len(outs) - far else jax.ShapeDtypeStruct)(*out) for i, out in enumerate(outs)],
        scratch_shapes=list(scratch),
        compiler_params=pltpu.CompilerParams(vmem_limit_bytes=limit),
        name=name,
    )(*args)


def begin(frac, velocity, force_old, species):
    outs = [((4, CAP), F32), ((4, CAP), F32), ((4 * R, CAP), F32), ((4 * R, CAP), F32)]
    return call(begin_kernel, "begin", (frac, velocity, force_old, species), outs, 4)


def prepare(count, codes, embed, w1, w2, wnt, we):
    outs = [
        ((1, W), F32), ((CH, CAP), F32), ((NB, CH), BF16), ((CH, 3 * CH), BF16), ((CH, 4 * CH), BF16),
        ((2 * CH, NB + 16), BF16), ((3 * CH, CH), BF16), ((4 * CH, CH), BF16), ((CH, 16), BF16),
        ((R, K, CAP), jnp.int32), ((R, K, CAP), jnp.int32), ((144, K * W), BF16), ((K * W, CAP), BF16),
    ]
    return call(prepare_kernel, "prepare", (count, codes, embed, w1, w2, wnt, we), outs, 7, smem=1)


def edges(plane, got_a, got_b, prepared):
    scratch = [
        pltpu.VMEM((144, CAP), F32),
        pltpu.VMEM((R, 3 * K, CAP), F32),
        pltpu.VMEM((R, K, CAP), F32),
        pltpu.VMEM((9, 8 * K, W), F32),
        pltpu.VMEM((9, 16 * K, W), BF16),
        pltpu.VMEM((8 * K, W), F32),
        pltpu.VMEM((CH, K * W), F32),
        pltpu.VMEM((CH, K * W), BF16),
        pltpu.VMEM((3 * CH, K * W), F32),
        pltpu.VMEM((3 * CH, K * W), BF16),
        pltpu.VMEM((9, CH, W), F32),
        pltpu.VMEM((9, CH, W), BF16),
        pltpu.VMEM((3 * CH, K * W), BF16),
        pltpu.VMEM((R, 9, 8 * K, CAP), F32),
        pltpu.VMEM((R, 8 * K, CAP), F32),
        pltpu.VMEM((96, K * W), BF16),
    ]
    outs = [((48, CAP), BF16), ((48, CAP), BF16), ((R, 3 * K, CAP), F32), ((1, W), F32)]
    return call(edges_kernel, "edges", (plane, got_a, got_b, *prepared), outs, 0, scratch=scratch, limit=EDGES_LIMIT)


def near(gradient, energy, prepared):
    outs = [((48, CAP), F32), ((4 * R, CAP), F32)]
    scratch = [pltpu.VMEM((48, K * W), BF16)]
    return call(near_kernel, "near", (gradient, energy, *prepared[-2:]), outs, 0, scratch=scratch, limit=EDGES_LIMIT)


def early(mine, keep, own, prepared):
    outs = [((4 * R, CAP), F32), ((4 * R, CAP), F32), ((3, R, CAP), F32), ((R, CAP), F32)]
    return call(early_kernel, "early", (mine, keep, own, prepared[0]), outs, 0, far=2)


def finish(column, got_a, got_b, own, speed, gain):
    outs = [((3, R, CAP), F32)] * 2
    return call(finish_kernel, "finish", (column, got_a, got_b, own, speed, gain), outs, 0, far=2)


def shards(
    frac, velocity, force_old, species, cell_count, neighbours, embed, w_radial_in, w_radial_out, w_node, w_energy
):
    even_x = lax.axis_index("gx") % 2 == 0
    even_z = lax.axis_index("gz") % 2 == 0
    vectors = (3, R, CAP)
    count = cell_count.reshape(R)
    wnt = w_node.T
    send_a, send_b, mine, keep = begin(
        frac.reshape(vectors), velocity.reshape(vectors), force_old.reshape(vectors), species.reshape(R, CAP)
    )
    prepared = prepare(
        count, neighbours.reshape(K * R, CAP), embed, w_radial_in, w_radial_out, wnt, w_energy.reshape(1, CH)
    )

    got_a, got_b = swap(send_a, "gz", False), swap(send_b, "gz", True)
    column = jnp.concatenate(
        [jnp.where(even_z, got_b, got_a), mine, jnp.where(even_z, got_a, got_b)], axis=0
    )
    got_a, got_b = swap(column, "gx", False), swap(column, "gx", True)
    plane = jnp.concatenate(
        [jnp.where(even_x, got_b, got_a), column, jnp.where(even_x, got_a, got_b)], axis=0
    )
    got_a, got_b = swap(plane, "gy", False), swap(plane, "gy", True)

    send_a, send_b, gradient, energy = edges(plane, got_a, got_b, prepared)
    plane, own = near(gradient, energy, prepared)
    speed, gain, next_frac, energy = early(mine, keep, own, prepared)
    plane = plane + swap(send_a, "gy", False).astype(F32) + swap(send_b, "gy", True).astype(F32)
    lower, column, upper = plane[0:16], plane[16:32], plane[32:48]
    send_a, send_b = jnp.where(even_x, upper, lower), jnp.where(even_x, lower, upper)
    column = column + swap(send_a, "gx", False) + swap(send_b, "gx", True)
    send_a = jnp.where(even_z, column[12:16], column[0:4])
    send_b = jnp.where(even_z, column[0:4], column[12:16])
    got_a, got_b = swap(send_a, "gz", False), swap(send_b, "gz", True)
    next_velocity, next_force = finish(column, got_a, got_b, own, speed, gain)
    return (
        next_frac.reshape(frac.shape),
        next_velocity.reshape(frac.shape),
        next_force.reshape(frac.shape),
        energy.reshape(species.shape),
    )


def solution(mesh):
    cells = P(None, "gx", "gy", "gz", None)
    in_specs = (
        cells, cells, cells, P("gx", "gy", "gz", None), P("gx", "gy", "gz"), cells, P(), P(), P(), P(), P(),
    )
    out_specs = (cells, cells, cells, P("gx", "gy", "gz", None))
    return jax.shard_map(shards, mesh=mesh, in_specs=in_specs, out_specs=out_specs, check_vma=False)
```

```python
import jax
import jax.numpy as jnp
from jax import lax
from jax.experimental import pallas as pl
from jax.experimental.pallas import tpu as pltpu
from jax.sharding import PartitionSpec as P

MASSES = (1.008, 12.011, 14.007, 15.999, 32.06, 22.99, 35.45, 39.098, 24.305, 40.078)
SQRT3 = 1.7320508075688772
HALF_SQRT3 = 0.8660254037844386
TIME_STEP = 0.5

K = 16
CAP = 128
R = 2
W = R * CAP
CH = 64
NB = 8
GROUP = 8
EDGES_LIMIT = 40 << 20
F32 = jnp.float32
BF16 = jnp.bfloat16


def swap(array, axis, odd):
    n = lax.axis_size(axis)
    if odd:
        pairs = [(i, (i + 1) % n if i % 2 else (i - 1) % n) for i in range(n)]
    else:
        pairs = [(i, i ^ 1) for i in range(n)]
    return lax.ppermute(array, axis, pairs)


def rows8(row, width):
    return jnp.broadcast_to(row, (8, width))


def wide(ref, row, height):
    parts = [jnp.broadcast_to(ref[r, pl.ds(row, 1), :], (height, CAP)) for r in range(R)]
    return jnp.concatenate(parts, axis=1)


def begin_kernel(frac_ref, vel_ref, force_ref, kind_ref, send_a_ref, send_b_ref, mine_ref, keep_ref):
    kind = kind_ref[...]
    mass = jnp.zeros((R, CAP), F32)
    for number, value in enumerate(MASSES):
        mass = jnp.where(kind == number, jnp.float32(value) / jnp.float32(16.0), mass)
    for c in range(3):
        half = vel_ref[c] + 0.5 * TIME_STEP * force_ref[c] / mass
        moved = frac_ref[c] + TIME_STEP * half
        for r in range(R):
            mine_ref[r * 4 + c:r * 4 + c + 1, :] = moved[r:r + 1]
            keep_ref[r * 4 + c:r * 4 + c + 1, :] = half[r:r + 1]
    for r in range(R):
        mine_ref[r * 4 + 3:r * 4 + 4, :] = kind[r:r + 1].astype(F32)
        keep_ref[r * 4 + 3:r * 4 + 4, :] = mass[r:r + 1]
    even = lax.axis_index("gz") % 2 == 0
    send_a_ref[...] = jnp.where(even, mine_ref[4:8, :], mine_ref[0:4, :])
    send_b_ref[...] = jnp.where(even, mine_ref[0:4, :], mine_ref[4:8, :])


def early_kernel(mine_ref, keep_ref, own_ref, occ_ref, speed_ref, gain_ref, frac_ref, energy_ref):
    for r in range(R):
        occupied = occ_ref[:, r * CAP:(r + 1) * CAP]
        keep = keep_ref[r * 4:r * 4 + 4, :]
        gain = occupied * (0.5 * TIME_STEP) / keep[3:4]
        own = own_ref[r * 4:r * 4 + 4, :]
        place = occupied * mine_ref[r * 4:r * 4 + 4, :]
        speed_ref[r * 4:r * 4 + 4, :] = occupied * keep
        gain_ref[r * 4:r * 4 + 4, :] = jnp.concatenate([gain, occupied, gain, occupied], axis=0)
        for c in range(3):
            frac_ref[c, r:r + 1, :] = place[c:c + 1]
        energy_ref[r:r + 1, :] = own[3:4]


def finish_kernel(mid_ref, got_a_ref, got_b_ref, own_ref, speed_ref, gain_ref, vel_ref, force_ref):
    even = lax.axis_index("gz") % 2 == 0
    got = (
        jnp.where(even, got_b_ref[...], got_a_ref[...]),
        jnp.where(even, got_a_ref[...], got_b_ref[...]),
    )
    for r in range(R):
        gain = gain_ref[r * 4:r * 4 + 1, :]
        occupied = gain_ref[r * 4 + 1:r * 4 + 2, :]
        force = mid_ref[4 * (r + 1):4 * (r + 2), :] + own_ref[r * 4:r * 4 + 4, :] + got[r]
        speed = speed_ref[r * 4:r * 4 + 4, :] + gain * force
        force = occupied * force
        for c in range(3):
            force_ref[c, r:r + 1, :] = force[c:c + 1]
            vel_ref[c, r:r + 1, :] = speed[c:c + 1]


def prepare_kernel(
    count_ref, codes_ref, emb_ref, w1_ref, w2_ref, wnt_ref, we_ref,
    side_ref, occ_ref, web_ref, w1c_ref, w2c_ref, wntc_ref, wc_ref, w2t_ref, wn_ref, embt_ref, off_ref, slot_ref, cell_ref, pick_ref,
):
    side_ref[...] = jnp.where(lax.axis_index("gx") % 2 == 0, jnp.ones((16, CAP), F32), jnp.zeros((16, CAP), F32))
    slot_number = lax.broadcasted_iota(jnp.int32, (1, CAP), 1)
    for r in range(R):
        occ_ref[:, r * CAP:(r + 1) * CAP] = jnp.where(slot_number < count_ref[r], 1.0, 0.0)
    web_ref[...] = jnp.broadcast_to(we_ref[...], (CAP, CH)).T
    w1c_ref[...] = w1_ref[...]
    w2c_ref[...] = w2_ref[...]
    wntc_ref[...] = wnt_ref[...]
    wc_ref[...] = jnp.zeros(wc_ref.shape, BF16)
    wc_ref[0:CH, 0:NB] = w1_ref[...].astype(F32).T.astype(BF16)
    emb = jnp.concatenate([emb_ref[...].astype(F32), jnp.zeros((6, CH), F32)], axis=0)
    embt = emb.T.astype(BF16)
    wc_ref[CH:, NB:NB + 16] = embt
    embt_ref[...] = embt
    w2t_ref[...] = w2_ref[...].astype(F32).T.astype(BF16)
    wn_ref[...] = wnt_ref[...].astype(F32).T.astype(BF16)
    row_cell = lax.broadcasted_iota(jnp.int32, (144, CAP), 0) // 4
    slots = lax.broadcasted_iota(jnp.int32, (CAP, CAP), 1).astype(F32)
    for r in range(R):
        code = codes_ref[pl.ds(r, K, stride=R), :]
        off = code // CAP
        slot = code % CAP
        off_ref[r] = off
        slot_ref[r] = slot
        cell = (off // 3 % 3 * 3 + off // 9) * 4 + off % 3 + r
        slot_rows = jnp.concatenate([slot.astype(F32), jnp.zeros((CAP - K, CAP), F32)], axis=0).T
        for k in range(K):
            lanes = slice(k * W + r * CAP, k * W + (r + 1) * CAP)
            cell_ref[:, lanes] = jnp.where(jnp.broadcast_to(cell[k:k + 1], (144, CAP)) == row_cell, 1.0, 0.0).astype(BF16)
            pick_ref[lanes, :] = jnp.where(slot_rows[:, k:k + 1] == slots, 1.0, 0.0).astype(BF16)


def gather_plane(off_ref, slot_ref, table_ref, base, oy, acc):
    offs = [[off_ref[r, h * 8:(h + 1) * 8, :] for h in range(2)] for r in range(R)]
    slots = [[slot_ref[r, h * 8:(h + 1) * 8, :] for h in range(2)] for r in range(R)]
    acc = list(acc)
    for ox in range(3):
        for zz in range(4):
            at = base + ox * 16 + zz * 4
            rows = [rows8(table_ref[at + q:at + q + 1, :], CAP) for q in range(4)]
            for r in range(R):
                oz = zz - r
                if not 0 <= oz <= 2:
                    continue
                for h in range(2):
                    hit = offs[r][h] == ox * 9 + oy * 3 + oz
                    for q in range(4):
                        got = jnp.take_along_axis(rows[q], slots[r][h], axis=1, mode="promise_in_bounds")
                        n = (r * 2 + h) * 4 + q
                        acc[n] = jnp.where(hit, got, acc[n])
    return offs, acc


def middle_kernel(plane_ref, off_ref, slot_ref, gathered_ref):
    _, acc = gather_plane(off_ref, slot_ref, plane_ref, 0, 1, [jnp.zeros((8, CAP), F32)] * 16)
    for n in range(16):
        gathered_ref[n * 8:(n + 1) * 8, :] = acc[n]


def edges_kernel(
    plane_ref, got_a_ref, got_b_ref, gathered_ref, occ_ref, web_ref, w1_ref, w2_ref, wnt_ref, wc_ref, w2t_ref, wn_ref, embt_ref, off_ref, slot_ref, cell_ref, pick_ref,
    send_a_ref, send_b_ref, g_s, energy_ref,
    pos_s, d_s, kd_s, ey_s, eyb_s, exu_s, ds_s, feat_s, q_s, qb_s, m_s, mb_s, gr_s, t_s, ts_s, a_s,
):
    even = lax.axis_index("gy") % 2 == 0
    pos_s[0:48] = jnp.where(even, got_b_ref[...], got_a_ref[...])
    pos_s[48:96] = jnp.where(even, got_a_ref[...], got_b_ref[...])
    acc = [gathered_ref[at * 8:(at + 1) * 8, :] for at in range(16)]
    offs, acc = gather_plane(off_ref, slot_ref, pos_s, 0, 0, acc)
    offs, acc = gather_plane(off_ref, slot_ref, pos_s, 48, 2, acc)
    for r in range(R):
        own = [plane_ref[16 + (1 + r) * 4 + c:16 + (1 + r) * 4 + c + 1, :] for c in range(3)]
        for h in range(2):
            off = offs[r][h]
            shift = (off // 9 - 1, off // 3 % 3 - 1, off % 3 - 1)
            for c in range(3):
                value = shift[c].astype(F32) + acc[(r * 2 + h) * 4 + c] - rows8(own[c], CAP)
                d_s[r, c * K + h * 8:c * K + h * 8 + 8, :] = value
            kd_s[r, h * 8:h * 8 + 8, :] = acc[(r * 2 + h) * 4 + 3]

    centre = lax.broadcasted_iota(jnp.int32, (8, W), 0).astype(F32) / (NB - 1)
    kinds16 = lax.broadcasted_iota(jnp.int32, (16, W), 0).astype(F32)

    def radial_group(group, _):
        inputs = []
        for j in range(GROUP):
            k = group * GROUP + j
            x = wide(d_s, k, 8)
            y = wide(d_s, K + k, 8)
            z = wide(d_s, 2 * K + k, 8)
            xx, yy, zz = x * x, y * y, z * z
            s = xx + yy + zz
            m1 = jnp.maximum(1.0 - s, 0.0)
            env = m1 * m1 * m1
            u = s - centre
            ex = jnp.exp(-float((NB - 1) ** 2) * (u * u))
            at = k * 8
            exu_s[pl.ds(at, 8), :] = ex * (u * (-2.0 * float((NB - 1) ** 2)))
            ex3 = env * SQRT3
            terms = (
                env, env * x, env * y, env * z, ex3 * (x * y), ex3 * (y * z), ex3 * (z * x),
                (env * HALF_SQRT3) * (xx - yy), (env * 0.5) * (2.0 * zz - xx - yy),
            )
            for m in range(9):
                ey_s[m, pl.ds(at, 8), :] = terms[m]
                eyb_s[m, k * 16:(k + 1) * 16, :] = jnp.concatenate([terms[m]] * 2, axis=0).astype(BF16)
            kind = wide(kd_s, k, 16)
            onehot = jnp.where(kind == kinds16, 1.0, 0.0)
            inputs.append(jnp.concatenate([ex, onehot], axis=0))
        rhs = jnp.concatenate(inputs, axis=1).astype(BF16)
        lanes = pl.ds(group * (GROUP * W), GROUP * W)
        first = jnp.dot(wc_ref[...], rhs, preferred_element_type=F32)
        pre = first[:CH]
        feat = first[CH:]
        sig = 0.5 * jnp.tanh(0.5 * pre) + 0.5
        hidden = (pre * sig).astype(BF16)
        ds_s[:, lanes] = sig * (1.0 + pre * (1.0 - sig))
        feat_s[:, lanes] = feat.astype(BF16)
        radial = jnp.dot(w2t_ref[...], hidden, preferred_element_type=F32)
        for deg in range(3):
            carried = radial[deg * CH:(deg + 1) * CH] * feat
            q_s[deg * CH:(deg + 1) * CH, lanes] = carried
            qb_s[deg * CH:(deg + 1) * CH, lanes] = carried.astype(BF16)
        return 0

    for group in range(K // GROUP):
        radial_group(group, 0)

    def message_block(cb, _):
        base = cb * 16
        for r in range(R):
            sums = [None] * 9
            for k in range(K):
                lo = k * W + r * CAP
                q = [q_s[pl.ds(deg * CH + base, 16), lo:lo + CAP] for deg in range(3)]
                for m in range(9):
                    weight = ey_s[m, k * 8:(k + 1) * 8, r * CAP:(r + 1) * CAP]
                    weight = jnp.concatenate([weight, weight], axis=0)
                    term = q[0 if m == 0 else 1 if m < 4 else 2] * weight
                    sums[m] = term if sums[m] is None else sums[m] + term
            for m in range(9):
                m_s[m, pl.ds(base, 16), r * CAP:(r + 1) * CAP] = sums[m]
        return 0

    for cb in range(CH // 16):
        message_block(cb, 0)

    own_kind = jnp.concatenate(
        [jnp.broadcast_to(plane_ref[16 + (1 + r) * 4 + 3:16 + (1 + r) * 4 + 4, :], (16, CAP)) for r in range(R)], axis=1
    )
    own_feat = jnp.dot(
        embt_ref[...], jnp.where(own_kind == kinds16, 1.0, 0.0).astype(BF16), preferred_element_type=F32
    )
    occupied = occ_ref[...]
    vec = m_s[1] * m_s[1] + m_s[2] * m_s[2] + m_s[3] * m_s[3]
    ten = m_s[4] * m_s[4] + m_s[5] * m_s[5] + m_s[6] * m_s[6] + m_s[7] * m_s[7] + m_s[8] * m_s[8]
    invariant = jnp.concatenate([m_s[0], vec, ten, own_feat], axis=0).astype(BF16)
    pre = jnp.dot(wnt_ref[...], invariant, preferred_element_type=F32)
    sig = 0.5 * jnp.tanh(0.5 * pre) + 0.5
    we = jnp.concatenate([web_ref[...]] * R, axis=1)
    energy = jnp.sum(we * (pre * sig), axis=0, keepdims=True) * occupied
    gpre = we * occupied * (sig * (1.0 + pre * (1.0 - sig)))
    ginv = jnp.dot(wn_ref[0:3 * CH, :], gpre.astype(BF16), preferred_element_type=F32).astype(BF16).astype(F32)
    mb_s[0] = ginv[:CH].astype(BF16)
    gvec = 2.0 * ginv[CH:2 * CH]
    gten = 2.0 * ginv[2 * CH:]
    for m in range(1, 9):
        mb_s[m] = (m_s[m] * (gvec if m < 4 else gten)).astype(BF16)

    def carried_back(k, _):
        at = k * 8
        for r in range(R):
            cols = slice(r * CAP, (r + 1) * CAP)
            lanes = pl.ds(k * W + r * CAP, CAP)
            weight = [eyb_s[m, k * 16:(k + 1) * 16, cols] for m in range(9)]
            sums = [None] * 9
            for cb in range(CH // 16):
                feat = feat_s[cb * 16:(cb + 1) * 16, lanes]
                q = [qb_s[deg * CH + cb * 16:deg * CH + (cb + 1) * 16, lanes] for deg in range(3)]
                back = [None] * 3
                for m in range(9):
                    deg = 0 if m == 0 else 1 if m < 4 else 2
                    cot = mb_s[m, cb * 16:(cb + 1) * 16, cols]
                    term = cot * q[deg]
                    sums[m] = term if sums[m] is None else sums[m] + term
                    term = cot * weight[m]
                    back[deg] = term if back[deg] is None else back[deg] + term
                for deg in range(3):
                    gr_s[deg * CH + cb * 16:deg * CH + (cb + 1) * 16, lanes] = back[deg] * feat
            for m in range(9):
                both = sums[m].astype(F32)
                t_s[r, m, pl.ds(at, 8), :] = both[:8] + both[8:]
        return 0

    for k in range(K):
        carried_back(k, 0)

    def radial_back(group, _):
        lanes = pl.ds(group * (GROUP * W), GROUP * W)
        ghid = jnp.dot(w2_ref[...], gr_s[:, lanes], preferred_element_type=F32)
        gpre = (ghid.astype(BF16).astype(F32) * ds_s[:, lanes]).astype(BF16)
        gbas = jnp.dot(w1_ref[...], gpre, preferred_element_type=F32).astype(BF16).astype(F32)
        for j in range(GROUP):
            at = (group * GROUP + j) * 8
            for r in range(R):
                lo = j * W + r * CAP
                ts_s[r, pl.ds(at, 8), :] = gbas[:, lo:lo + CAP] * exu_s[pl.ds(at, 8), r * CAP:(r + 1) * CAP]
        return 0

    for group in range(K // GROUP):
        radial_back(group, 0)

    def total(ref):
        out = ref[pl.ds(0, K, stride=8), :]
        for sub in range(1, 8):
            out = out + ref[pl.ds(sub, K, stride=8), :]
        return out

    for r in range(R):
        cols = slice(r * CAP, (r + 1) * CAP)
        x, y, z = d_s[r, 0:K, :], d_s[r, K:2 * K, :], d_s[r, 2 * K:3 * K, :]
        xx, yy, zz = x * x, y * y, z * z
        s = xx + yy + zz
        m1 = jnp.maximum(1.0 - s, 0.0)
        env = m1 * m1 * m1
        t = [total(t_s.at[r, m]) for m in range(9)]
        harm = (
            None, x, y, z, SQRT3 * (x * y), SQRT3 * (y * z), SQRT3 * (z * x),
            HALF_SQRT3 * (xx - yy), 0.5 * (2.0 * zz - xx - yy),
        )
        genv = t[0]
        for m in range(1, 9):
            genv = genv + harm[m] * t[m]
        gs2 = 2.0 * (total(ts_s.at[r]) - 3.0 * (m1 * m1) * genv)
        e = [env * v for v in t]
        gx = e[1] + SQRT3 * (y * e[4] + z * e[6]) + x * (SQRT3 * e[7] - e[8] + gs2)
        gy = e[2] + SQRT3 * (x * e[4] + z * e[5]) + y * (gs2 - SQRT3 * e[7] - e[8])
        gz = e[3] + SQRT3 * (y * e[5] + x * e[6]) + z * (2.0 * e[8] + gs2)
        for c, g in enumerate((gx, gy, gz)):
            g_s[r, c * K:(c + 1) * K, :] = g
    energy_ref[...] = energy

    scatter_inputs(g_s, cell_ref, a_s, ((0, 0), (96, 48)))
    out = jnp.dot(a_s[...], pick_ref[...], preferred_element_type=F32)
    send_a_ref[...] = jnp.where(even, out[48:96], out[0:48]).astype(BF16)
    send_b_ref[...] = jnp.where(even, out[0:48], out[48:96]).astype(BF16)


def scatter_inputs(g_ref, cell_ref, a_ref, blocks):
    comp = lax.broadcasted_iota(jnp.int32, (16, CAP), 0) % 4
    for k in range(K):
        for r in range(R):
            lanes = slice(k * W + r * CAP, k * W + (r + 1) * CAP)
            gx, gy, gz = (jnp.broadcast_to(g_ref[r, c * K + k:c * K + k + 1, :], (16, CAP)) for c in range(3))
            mixed = jnp.where(comp == 0, gx, jnp.where(comp == 1, gy, jnp.where(comp == 2, gz, 0.0)))
            mixed = (-mixed).astype(BF16)
            for take, put in blocks:
                for j in range(0, 48, 16):
                    a_ref[put + j:put + j + 16, lanes] = cell_ref[take + j:take + j + 16, lanes] * mixed


def near_kernel(g_ref, energy_ref, cell_ref, pick_ref, mid_ref, own_ref, a_s):
    scatter_inputs(g_ref, cell_ref, a_s, ((48, 0),))
    mid_ref[...] = jnp.dot(a_s[...], pick_ref[...], preferred_element_type=F32)
    for r in range(R):
        for c in range(3):
            own_ref[r * 4 + c:r * 4 + c + 1, :] = jnp.sum(g_ref[r, c * K:(c + 1) * K, :], axis=0, keepdims=True)
        own_ref[r * 4 + 3:r * 4 + 4, :] = energy_ref[:, r * CAP:(r + 1) * CAP]


VMEM = pl.BlockSpec(memory_space=pltpu.VMEM)
SMEM = pl.BlockSpec(memory_space=pltpu.SMEM)


def call(kernel, name, args, outs, near, far=0, smem=0, scratch=(), limit=None):
    args = args[:near] + tuple(pltpu.with_memory_space_constraint(a, pltpu.VMEM) for a in args[near:])
    return pl.pallas_call(
        kernel,
        in_specs=[SMEM] * smem + [VMEM] * (len(args) - smem),
        out_specs=[VMEM] * len(outs),
        out_shape=[(pltpu.VMEM if i < len(outs) - far else jax.ShapeDtypeStruct)(*out) for i, out in enumerate(outs)],
        scratch_shapes=list(scratch),
        compiler_params=pltpu.CompilerParams(vmem_limit_bytes=limit),
        name=name,
    )(*args)


def begin(frac, velocity, force_old, species):
    outs = [((4, CAP), F32), ((4, CAP), F32), ((4 * R, CAP), F32), ((4 * R, CAP), F32)]
    return call(begin_kernel, "begin", (frac, velocity, force_old, species), outs, 4)


def prepare(count, codes, embed, w1, w2, wnt, we):
    outs = [
        ((16, CAP), F32), ((1, W), F32), ((CH, CAP), F32), ((NB, CH), BF16), ((CH, 3 * CH), BF16), ((CH, 4 * CH), BF16),
        ((2 * CH, NB + 16), BF16), ((3 * CH, CH), BF16), ((4 * CH, CH), BF16), ((CH, 16), BF16),
        ((R, K, CAP), jnp.int32), ((R, K, CAP), jnp.int32), ((144, K * W), BF16), ((K * W, CAP), BF16),
    ]
    return call(prepare_kernel, "prepare", (count, codes, embed, w1, w2, wnt, we), outs, 7, smem=1)


def middle(plane, prepared):
    outs = [((16 * 8, CAP), F32)]
    return call(middle_kernel, "middle", (plane, *prepared[-4:-2]), outs, 0, limit=EDGES_LIMIT)[0]


def edges(plane, got_a, got_b, gathered, prepared):
    scratch = [
        pltpu.VMEM((96, CAP), F32),
        pltpu.VMEM((R, 3 * K, CAP), F32),
        pltpu.VMEM((R, K, CAP), F32),
        pltpu.VMEM((9, 8 * K, W), F32),
        pltpu.VMEM((9, 16 * K, W), BF16),
        pltpu.VMEM((8 * K, W), F32),
        pltpu.VMEM((CH, K * W), F32),
        pltpu.VMEM((CH, K * W), BF16),
        pltpu.VMEM((3 * CH, K * W), F32),
        pltpu.VMEM((3 * CH, K * W), BF16),
        pltpu.VMEM((9, CH, W), F32),
        pltpu.VMEM((9, CH, W), BF16),
        pltpu.VMEM((3 * CH, K * W), BF16),
        pltpu.VMEM((R, 9, 8 * K, CAP), F32),
        pltpu.VMEM((R, 8 * K, CAP), F32),
        pltpu.VMEM((96, K * W), BF16),
    ]
    outs = [((48, CAP), BF16), ((48, CAP), BF16), ((R, 3 * K, CAP), F32), ((1, W), F32)]
    return call(edges_kernel, "edges", (plane, got_a, got_b, gathered, *prepared), outs, 0, scratch=scratch, limit=EDGES_LIMIT)


def near(gradient, energy, prepared):
    outs = [((48, CAP), F32), ((4 * R, CAP), F32)]
    scratch = [pltpu.VMEM((48, K * W), BF16)]
    return call(near_kernel, "near", (gradient, energy, *prepared[-2:]), outs, 0, scratch=scratch, limit=EDGES_LIMIT)


def early(mine, keep, own, prepared):
    outs = [((4 * R, CAP), F32), ((4 * R, CAP), F32), ((3, R, CAP), F32), ((R, CAP), F32)]
    return call(early_kernel, "early", (mine, keep, own, prepared[0]), outs, 0, far=2)


def finish(column, got_a, got_b, own, speed, gain):
    outs = [((3, R, CAP), F32)] * 2
    return call(finish_kernel, "finish", (column, got_a, got_b, own, speed, gain), outs, 0, far=2)


def shards(
    frac, velocity, force_old, species, cell_count, neighbours, embed, w_radial_in, w_radial_out, w_node, w_energy
):
    even_x = lax.axis_index("gx") % 2 == 0
    even_z = lax.axis_index("gz") % 2 == 0
    vectors = (3, R, CAP)
    count = cell_count.reshape(R)
    wnt = w_node.T
    send_a, send_b, mine, keep = begin(
        frac.reshape(vectors), velocity.reshape(vectors), force_old.reshape(vectors), species.reshape(R, CAP)
    )
    side, *prepared = prepare(
        count, neighbours.reshape(K * R, CAP), embed, w_radial_in, w_radial_out, wnt, w_energy.reshape(1, CH)
    )

    got_a, got_b = swap(send_a, "gz", False), swap(send_b, "gz", True)
    column = jnp.concatenate(
        [jnp.where(even_z, got_b, got_a), mine, jnp.where(even_z, got_a, got_b)], axis=0
    )
    got_a, got_b = swap(column, "gx", False), swap(column, "gx", True)
    plane = jnp.concatenate(
        [jnp.where(side > 0.5, got_b, got_a), column, jnp.where(side > 0.5, got_a, got_b)], axis=0
    )
    gathered = middle(plane, prepared)
    got_a, got_b = swap(plane, "gy", False), swap(plane, "gy", True)

    send_a, send_b, gradient, energy = edges(plane, got_a, got_b, gathered, prepared)
    plane, own = near(gradient, energy, prepared)
    speed, gain, next_frac, energy = early(mine, keep, own, prepared)
    plane = plane + swap(send_a, "gy", False).astype(F32) + swap(send_b, "gy", True).astype(F32)
    lower, column, upper = plane[0:16], plane[16:32], plane[32:48]
    send_a, send_b = jnp.where(even_x, upper, lower), jnp.where(even_x, lower, upper)
    column = column + swap(send_a, "gx", False) + swap(send_b, "gx", True)
    send_a = jnp.where(even_z, column[12:16], column[0:4])
    send_b = jnp.where(even_z, column[0:4], column[12:16])
    got_a, got_b = swap(send_a, "gz", False), swap(send_b, "gz", True)
    next_velocity, next_force = finish(column, got_a, got_b, own, speed, gain)
    return (
        next_frac.reshape(frac.shape),
        next_velocity.reshape(frac.shape),
        next_force.reshape(frac.shape),
        energy.reshape(species.shape),
    )


def solution(mesh):
    cells = P(None, "gx", "gy", "gz", None)
    in_specs = (
        cells, cells, cells, P("gx", "gy", "gz", None), P("gx", "gy", "gz"), cells, P(), P(), P(), P(), P(),
    )
    out_specs = (cells, cells, cells, P("gx", "gy", "gz", None))
    return jax.shard_map(shards, mesh=mesh, in_specs=in_specs, out_specs=out_specs, check_vma=False)
```

```python
import jax
import jax.numpy as jnp
from jax import lax
from jax.experimental import pallas as pl
from jax.experimental.pallas import tpu as pltpu
from jax.sharding import PartitionSpec as P

MASSES = (1.008, 12.011, 14.007, 15.999, 32.06, 22.99, 35.45, 39.098, 24.305, 40.078)
SQRT3 = 1.7320508075688772
HALF_SQRT3 = 0.8660254037844386
TIME_STEP = 0.5

K = 16
CAP = 128
R = 2
W = R * CAP
CH = 64
NB = 8
GROUP = 8
EDGES_LIMIT = 40 << 20
F32 = jnp.float32
BF16 = jnp.bfloat16


def swap(array, axis, odd):
    n = lax.axis_size(axis)
    if odd:
        pairs = [(i, (i + 1) % n if i % 2 else (i - 1) % n) for i in range(n)]
    else:
        pairs = [(i, i ^ 1) for i in range(n)]
    return lax.ppermute(array, axis, pairs)


def rows8(row, width):
    return jnp.broadcast_to(row, (8, width))


def wide(ref, row, height):
    parts = [jnp.broadcast_to(ref[r, pl.ds(row, 1), :], (height, CAP)) for r in range(R)]
    return jnp.concatenate(parts, axis=1)


def begin_kernel(frac_ref, vel_ref, force_ref, kind_ref, send_a_ref, send_b_ref, mine_ref, keep_ref):
    kind = kind_ref[...]
    mass = jnp.zeros((R, CAP), F32)
    for number, value in enumerate(MASSES):
        mass = jnp.where(kind == number, jnp.float32(value) / jnp.float32(16.0), mass)
    for c in range(3):
        half = vel_ref[c] + 0.5 * TIME_STEP * force_ref[c] / mass
        moved = frac_ref[c] + TIME_STEP * half
        for r in range(R):
            mine_ref[r * 4 + c:r * 4 + c + 1, :] = moved[r:r + 1]
            keep_ref[r * 4 + c:r * 4 + c + 1, :] = half[r:r + 1]
    for r in range(R):
        mine_ref[r * 4 + 3:r * 4 + 4, :] = kind[r:r + 1].astype(F32)
        keep_ref[r * 4 + 3:r * 4 + 4, :] = mass[r:r + 1]
    even = lax.axis_index("gz") % 2 == 0
    send_a_ref[...] = jnp.where(even, mine_ref[4:8, :], mine_ref[0:4, :])
    send_b_ref[...] = jnp.where(even, mine_ref[0:4, :], mine_ref[4:8, :])


def early_kernel(mine_ref, keep_ref, own_ref, occ_ref, speed_ref, gain_ref, frac_ref, energy_ref):
    for r in range(R):
        occupied = occ_ref[:, r * CAP:(r + 1) * CAP]
        keep = keep_ref[r * 4:r * 4 + 4, :]
        gain = occupied * (0.5 * TIME_STEP) / keep[3:4]
        own = own_ref[r * 4:r * 4 + 4, :]
        place = occupied * mine_ref[r * 4:r * 4 + 4, :]
        speed_ref[r * 4:r * 4 + 4, :] = occupied * keep
        gain_ref[r * 4:r * 4 + 4, :] = jnp.concatenate([gain, occupied, gain, occupied], axis=0)
        for c in range(3):
            frac_ref[c, r:r + 1, :] = place[c:c + 1]
        energy_ref[r:r + 1, :] = own[3:4]


def finish_kernel(mid_ref, got_a_ref, got_b_ref, own_ref, speed_ref, gain_ref, vel_ref, force_ref):
    even = lax.axis_index("gz") % 2 == 0
    got = (
        jnp.where(even, got_b_ref[...], got_a_ref[...]),
        jnp.where(even, got_a_ref[...], got_b_ref[...]),
    )
    for r in range(R):
        gain = gain_ref[r * 4:r * 4 + 1, :]
        occupied = gain_ref[r * 4 + 1:r * 4 + 2, :]
        force = mid_ref[4 * (r + 1):4 * (r + 2), :] + own_ref[r * 4:r * 4 + 4, :] + got[r]
        speed = speed_ref[r * 4:r * 4 + 4, :] + gain * force
        force = occupied * force
        for c in range(3):
            force_ref[c, r:r + 1, :] = force[c:c + 1]
            vel_ref[c, r:r + 1, :] = speed[c:c + 1]


def prepare_kernel(
    count_ref, codes_ref, emb_ref, w1_ref, w2_ref, wnt_ref, we_ref,
    side_ref, occ_ref, web_ref, w1c_ref, w2c_ref, wntc_ref, wc_ref, w2t_ref, wn_ref, embt_ref, off_ref, slot_ref, cell_ref, pick_ref,
):
    side_ref[...] = jnp.where(lax.axis_index("gx") % 2 == 0, jnp.ones((16, CAP), F32), jnp.zeros((16, CAP), F32))
    slot_number = lax.broadcasted_iota(jnp.int32, (1, CAP), 1)
    for r in range(R):
        occ_ref[:, r * CAP:(r + 1) * CAP] = jnp.where(slot_number < count_ref[r], 1.0, 0.0)
    web_ref[...] = jnp.broadcast_to(we_ref[...], (CAP, CH)).T
    w1c_ref[...] = w1_ref[...]
    w2c_ref[...] = w2_ref[...]
    wntc_ref[...] = wnt_ref[...]
    wc_ref[...] = jnp.zeros(wc_ref.shape, BF16)
    wc_ref[0:CH, 0:NB] = w1_ref[...].astype(F32).T.astype(BF16)
    emb = jnp.concatenate([emb_ref[...].astype(F32), jnp.zeros((6, CH), F32)], axis=0)
    embt = emb.T.astype(BF16)
    wc_ref[CH:, NB:NB + 16] = embt
    embt_ref[...] = embt
    w2t_ref[...] = w2_ref[...].astype(F32).T.astype(BF16)
    wn_ref[...] = wnt_ref[...].astype(F32).T.astype(BF16)
    row_cell = lax.broadcasted_iota(jnp.int32, (144, CAP), 0) // 4
    slots = lax.broadcasted_iota(jnp.int32, (CAP, CAP), 1).astype(F32)
    for r in range(R):
        code = codes_ref[pl.ds(r, K, stride=R), :]
        off = code // CAP
        slot = code % CAP
        off_ref[r] = off
        slot_ref[r] = slot
        cell = (off // 3 % 3 * 3 + off // 9) * 4 + off % 3 + r
        slot_rows = jnp.concatenate([slot.astype(F32), jnp.zeros((CAP - K, CAP), F32)], axis=0).T
        for k in range(K):
            lanes = slice(k * W + r * CAP, k * W + (r + 1) * CAP)
            cell_ref[:, lanes] = jnp.where(jnp.broadcast_to(cell[k:k + 1], (144, CAP)) == row_cell, 1.0, 0.0).astype(BF16)
            pick_ref[lanes, :] = jnp.where(slot_rows[:, k:k + 1] == slots, 1.0, 0.0).astype(BF16)


def gather_plane(off_ref, slot_ref, table_ref, base, oy, acc):
    offs = [[off_ref[r, h * 8:(h + 1) * 8, :] for h in range(2)] for r in range(R)]
    slots = [[slot_ref[r, h * 8:(h + 1) * 8, :] for h in range(2)] for r in range(R)]
    acc = list(acc)
    for ox in range(3):
        for zz in range(4):
            at = base + ox * 16 + zz * 4
            rows = [rows8(table_ref[at + q:at + q + 1, :], CAP) for q in range(4)]
            for r in range(R):
                oz = zz - r
                if not 0 <= oz <= 2:
                    continue
                for h in range(2):
                    hit = offs[r][h] == ox * 9 + oy * 3 + oz
                    for q in range(4):
                        got = jnp.take_along_axis(rows[q], slots[r][h], axis=1, mode="promise_in_bounds")
                        n = (r * 2 + h) * 4 + q
                        acc[n] = jnp.where(hit, got, acc[n])
    return offs, acc


def middle_kernel(plane_ref, off_ref, slot_ref, gathered_ref):
    _, acc = gather_plane(off_ref, slot_ref, plane_ref, 0, 1, [jnp.zeros((8, CAP), F32)] * 16)
    for n in range(16):
        gathered_ref[n * 8:(n + 1) * 8, :] = acc[n]


def edges_kernel(
    plane_ref, got_a_ref, got_b_ref, gathered_ref, occ_ref, web_ref, w1_ref, w2_ref, wnt_ref, wc_ref, w2t_ref, wn_ref, embt_ref, off_ref, slot_ref, cell_ref, pick_ref,
    send_a_ref, send_b_ref, g_s, energy_ref,
    pos_s, d_s, kd_s, ey_s, eyb_s, exu_s, ds_s, feat_s, q_s, qb_s, m_s, mb_s, gr_s, t_s, ts_s, a_s,
):
    even = lax.axis_index("gy") % 2 == 0
    pos_s[0:48] = jnp.where(even, got_b_ref[...], got_a_ref[...])
    pos_s[48:96] = jnp.where(even, got_a_ref[...], got_b_ref[...])
    acc = [gathered_ref[at * 8:(at + 1) * 8, :] for at in range(16)]
    offs, acc = gather_plane(off_ref, slot_ref, pos_s, 0, 0, acc)
    offs, acc = gather_plane(off_ref, slot_ref, pos_s, 48, 2, acc)
    for r in range(R):
        own = [plane_ref[16 + (1 + r) * 4 + c:16 + (1 + r) * 4 + c + 1, :] for c in range(3)]
        for h in range(2):
            off = offs[r][h]
            shift = (off // 9 - 1, off // 3 % 3 - 1, off % 3 - 1)
            for c in range(3):
                value = shift[c].astype(F32) + acc[(r * 2 + h) * 4 + c] - rows8(own[c], CAP)
                d_s[r, c * K + h * 8:c * K + h * 8 + 8, :] = value
            kd_s[r, h * 8:h * 8 + 8, :] = acc[(r * 2 + h) * 4 + 3]

    centre = lax.broadcasted_iota(jnp.int32, (8, W), 0).astype(F32) / (NB - 1)
    kinds16 = lax.broadcasted_iota(jnp.int32, (16, W), 0).astype(F32)

    def radial_group(group, _):
        inputs = []
        for j in range(GROUP):
            k = group * GROUP + j
            x = wide(d_s, k, 8)
            y = wide(d_s, K + k, 8)
            z = wide(d_s, 2 * K + k, 8)
            xx, yy, zz = x * x, y * y, z * z
            s = xx + yy + zz
            m1 = jnp.maximum(1.0 - s, 0.0)
            env = m1 * m1 * m1
            u = s - centre
            ex = jnp.exp(-float((NB - 1) ** 2) * (u * u))
            at = k * 8
            exu_s[pl.ds(at, 8), :] = ex * (u * (-2.0 * float((NB - 1) ** 2)))
            ex3 = env * SQRT3
            terms = (
                env, env * x, env * y, env * z, ex3 * (x * y), ex3 * (y * z), ex3 * (z * x),
                (env * HALF_SQRT3) * (xx - yy), (env * 0.5) * (2.0 * zz - xx - yy),
            )
            for m in range(9):
                ey_s[m, pl.ds(at, 8), :] = terms[m]
                eyb_s[m, k * 16:(k + 1) * 16, :] = jnp.concatenate([terms[m]] * 2, axis=0).astype(BF16)
            kind = wide(kd_s, k, 16)
            onehot = jnp.where(kind == kinds16, 1.0, 0.0)
            inputs.append(jnp.concatenate([ex, onehot], axis=0))
        rhs = jnp.concatenate(inputs, axis=1).astype(BF16)
        lanes = pl.ds(group * (GROUP * W), GROUP * W)
        first = jnp.dot(wc_ref[...], rhs, preferred_element_type=F32)
        pre = first[:CH]
        feat = first[CH:]
        sig = 0.5 * jnp.tanh(0.5 * pre) + 0.5
        hidden = (pre * sig).astype(BF16)
        ds_s[:, lanes] = sig * (1.0 + pre * (1.0 - sig))
        feat_s[:, lanes] = feat.astype(BF16)
        radial = jnp.dot(w2t_ref[...], hidden, preferred_element_type=F32)
        for deg in range(3):
            carried = radial[deg * CH:(deg + 1) * CH] * feat
            q_s[deg * CH:(deg + 1) * CH, lanes] = carried
            qb_s[deg * CH:(deg + 1) * CH, lanes] = carried.astype(BF16)
        return 0

    for group in range(K // GROUP):
        radial_group(group, 0)

    def message_block(cb, _):
        base = cb * 16
        for r in range(R):
            sums = [None] * 9
            for k in range(K):
                lo = k * W + r * CAP
                q = [q_s[pl.ds(deg * CH + base, 16), lo:lo + CAP] for deg in range(3)]
                for m in range(9):
                    weight = ey_s[m, k * 8:(k + 1) * 8, r * CAP:(r + 1) * CAP]
                    weight = jnp.concatenate([weight, weight], axis=0)
                    term = q[0 if m == 0 else 1 if m < 4 else 2] * weight
                    sums[m] = term if sums[m] is None else sums[m] + term
            for m in range(9):
                m_s[m, pl.ds(base, 16), r * CAP:(r + 1) * CAP] = sums[m]
        return 0

    for cb in range(CH // 16):
        message_block(cb, 0)

    own_kind = jnp.concatenate(
        [jnp.broadcast_to(plane_ref[16 + (1 + r) * 4 + 3:16 + (1 + r) * 4 + 4, :], (16, CAP)) for r in range(R)], axis=1
    )
    own_feat = jnp.dot(
        embt_ref[...], jnp.where(own_kind == kinds16, 1.0, 0.0).astype(BF16), preferred_element_type=F32
    )
    occupied = occ_ref[...]
    vec = m_s[1] * m_s[1] + m_s[2] * m_s[2] + m_s[3] * m_s[3]
    ten = m_s[4] * m_s[4] + m_s[5] * m_s[5] + m_s[6] * m_s[6] + m_s[7] * m_s[7] + m_s[8] * m_s[8]
    invariant = jnp.concatenate([m_s[0], vec, ten, own_feat], axis=0).astype(BF16)
    pre = jnp.dot(wnt_ref[...], invariant, preferred_element_type=F32)
    sig = 0.5 * jnp.tanh(0.5 * pre) + 0.5
    we = jnp.concatenate([web_ref[...]] * R, axis=1)
    energy = jnp.sum(we * (pre * sig), axis=0, keepdims=True) * occupied
    gpre = we * occupied * (sig * (1.0 + pre * (1.0 - sig)))
    ginv = jnp.dot(wn_ref[0:3 * CH, :], gpre.astype(BF16), preferred_element_type=F32).astype(BF16).astype(F32)
    mb_s[0] = ginv[:CH].astype(BF16)
    gvec = 2.0 * ginv[CH:2 * CH]
    gten = 2.0 * ginv[2 * CH:]
    for m in range(1, 9):
        mb_s[m] = (m_s[m] * (gvec if m < 4 else gten)).astype(BF16)

    def carried_back(k, _):
        at = k * 8
        for r in range(R):
            cols = slice(r * CAP, (r + 1) * CAP)
            lanes = pl.ds(k * W + r * CAP, CAP)
            weight = [eyb_s[m, k * 16:(k + 1) * 16, cols] for m in range(9)]
            sums = [None] * 9
            for cb in range(CH // 16):
                feat = feat_s[cb * 16:(cb + 1) * 16, lanes]
                q = [qb_s[deg * CH + cb * 16:deg * CH + (cb + 1) * 16, lanes] for deg in range(3)]
                back = [None] * 3
                for m in range(9):
                    deg = 0 if m == 0 else 1 if m < 4 else 2
                    cot = mb_s[m, cb * 16:(cb + 1) * 16, cols]
                    term = cot * q[deg]
                    sums[m] = term if sums[m] is None else sums[m] + term
                    term = cot * weight[m]
                    back[deg] = term if back[deg] is None else back[deg] + term
                for deg in range(3):
                    gr_s[deg * CH + cb * 16:deg * CH + (cb + 1) * 16, lanes] = back[deg] * feat
            for m in range(9):
                both = sums[m].astype(F32)
                t_s[r, m, pl.ds(at, 8), :] = both[:8] + both[8:]
        return 0

    for k in range(K):
        carried_back(k, 0)

    def radial_back(group, _):
        lanes = pl.ds(group * (GROUP * W), GROUP * W)
        ghid = jnp.dot(w2_ref[...], gr_s[:, lanes], preferred_element_type=F32)
        gpre = (ghid.astype(BF16).astype(F32) * ds_s[:, lanes]).astype(BF16)
        gbas = jnp.dot(w1_ref[...], gpre, preferred_element_type=F32).astype(BF16).astype(F32)
        for j in range(GROUP):
            at = (group * GROUP + j) * 8
            for r in range(R):
                lo = j * W + r * CAP
                ts_s[r, pl.ds(at, 8), :] = gbas[:, lo:lo + CAP] * exu_s[pl.ds(at, 8), r * CAP:(r + 1) * CAP]
        return 0

    for group in range(K // GROUP):
        radial_back(group, 0)

    def total(ref):
        out = ref[pl.ds(0, K, stride=8), :]
        for sub in range(1, 8):
            out = out + ref[pl.ds(sub, K, stride=8), :]
        return out

    for r in range(R):
        cols = slice(r * CAP, (r + 1) * CAP)
        x, y, z = d_s[r, 0:K, :], d_s[r, K:2 * K, :], d_s[r, 2 * K:3 * K, :]
        xx, yy, zz = x * x, y * y, z * z
        s = xx + yy + zz
        m1 = jnp.maximum(1.0 - s, 0.0)
        env = m1 * m1 * m1
        t = [total(t_s.at[r, m]) for m in range(9)]
        harm = (
            None, x, y, z, SQRT3 * (x * y), SQRT3 * (y * z), SQRT3 * (z * x),
            HALF_SQRT3 * (xx - yy), 0.5 * (2.0 * zz - xx - yy),
        )
        genv = t[0]
        for m in range(1, 9):
            genv = genv + harm[m] * t[m]
        gs2 = 2.0 * (total(ts_s.at[r]) - 3.0 * (m1 * m1) * genv)
        e = [env * v for v in t]
        gx = e[1] + SQRT3 * (y * e[4] + z * e[6]) + x * (SQRT3 * e[7] - e[8] + gs2)
        gy = e[2] + SQRT3 * (x * e[4] + z * e[5]) + y * (gs2 - SQRT3 * e[7] - e[8])
        gz = e[3] + SQRT3 * (y * e[5] + x * e[6]) + z * (2.0 * e[8] + gs2)
        for c, g in enumerate((gx, gy, gz)):
            g_s[r, c * K:(c + 1) * K, :] = g
    energy_ref[...] = energy

    scatter_inputs(g_s, cell_ref, a_s, ((0, 0), (96, 48)))
    out = jnp.dot(a_s[...], pick_ref[...], preferred_element_type=F32)
    send_a_ref[...] = jnp.where(even, out[48:96], out[0:48]).astype(BF16)
    send_b_ref[...] = jnp.where(even, out[0:48], out[48:96]).astype(BF16)


def scatter_inputs(g_ref, cell_ref, a_ref, blocks):
    comp = lax.broadcasted_iota(jnp.int32, (16, CAP), 0) % 4
    for k in range(K):
        for r in range(R):
            lanes = slice(k * W + r * CAP, k * W + (r + 1) * CAP)
            gx, gy, gz = (jnp.broadcast_to(g_ref[r, c * K + k:c * K + k + 1, :], (16, CAP)) for c in range(3))
            mixed = jnp.where(comp == 0, gx, jnp.where(comp == 1, gy, jnp.where(comp == 2, gz, 0.0)))
            mixed = (-mixed).astype(BF16)
            for take, put in blocks:
                for j in range(0, 48, 16):
                    a_ref[put + j:put + j + 16, lanes] = cell_ref[take + j:take + j + 16, lanes] * mixed


def near_kernel(g_ref, energy_ref, cell_ref, pick_ref, mid_ref, own_ref, a_s):
    scatter_inputs(g_ref, cell_ref, a_s, ((48, 0),))
    mid_ref[...] = jnp.dot(a_s[...], pick_ref[...], preferred_element_type=F32)
    for r in range(R):
        for c in range(3):
            own_ref[r * 4 + c:r * 4 + c + 1, :] = jnp.sum(g_ref[r, c * K:(c + 1) * K, :], axis=0, keepdims=True)
        own_ref[r * 4 + 3:r * 4 + 4, :] = energy_ref[:, r * CAP:(r + 1) * CAP]


VMEM = pl.BlockSpec(memory_space=pltpu.VMEM)
SMEM = pl.BlockSpec(memory_space=pltpu.SMEM)


def call(kernel, name, args, outs, near, far=0, smem=0, scratch=(), limit=None):
    args = args[:near] + tuple(pltpu.with_memory_space_constraint(a, pltpu.VMEM) for a in args[near:])
    return pl.pallas_call(
        kernel,
        in_specs=[SMEM] * smem + [VMEM] * (len(args) - smem),
        out_specs=[VMEM] * len(outs),
        out_shape=[(pltpu.VMEM if i < len(outs) - far else jax.ShapeDtypeStruct)(*out) for i, out in enumerate(outs)],
        scratch_shapes=list(scratch),
        compiler_params=pltpu.CompilerParams(vmem_limit_bytes=limit),
        name=name,
    )(*args)


def begin(frac, velocity, force_old, species):
    outs = [((4, CAP), F32), ((4, CAP), F32), ((4 * R, CAP), F32), ((4 * R, CAP), F32)]
    return call(begin_kernel, "begin", (frac, velocity, force_old, species), outs, 4)


def prepare(count, codes, embed, w1, w2, wnt, we):
    outs = [
        ((16, CAP), F32), ((1, W), F32), ((CH, CAP), F32), ((NB, CH), BF16), ((CH, 3 * CH), BF16), ((CH, 4 * CH), BF16),
        ((2 * CH, NB + 16), BF16), ((3 * CH, CH), BF16), ((4 * CH, CH), BF16), ((CH, 16), BF16),
        ((R, K, CAP), jnp.int32), ((R, K, CAP), jnp.int32), ((144, K * W), BF16), ((K * W, CAP), BF16),
    ]
    return call(prepare_kernel, "prepare", (count, codes, embed, w1, w2, wnt, we), outs, 7, smem=1)


def middle(plane, prepared):
    outs = [((16 * 8, CAP), F32)]
    return call(middle_kernel, "middle", (plane, *prepared[-4:-2]), outs, 0, limit=EDGES_LIMIT)[0]


def edges(plane, got_a, got_b, gathered, prepared):
    scratch = [
        pltpu.VMEM((96, CAP), F32),
        pltpu.VMEM((R, 3 * K, CAP), F32),
        pltpu.VMEM((R, K, CAP), F32),
        pltpu.VMEM((9, 8 * K, W), F32),
        pltpu.VMEM((9, 16 * K, W), BF16),
        pltpu.VMEM((8 * K, W), F32),
        pltpu.VMEM((CH, K * W), F32),
        pltpu.VMEM((CH, K * W), BF16),
        pltpu.VMEM((3 * CH, K * W), F32),
        pltpu.VMEM((3 * CH, K * W), BF16),
        pltpu.VMEM((9, CH, W), F32),
        pltpu.VMEM((9, CH, W), BF16),
        pltpu.VMEM((3 * CH, K * W), BF16),
        pltpu.VMEM((R, 9, 8 * K, CAP), F32),
        pltpu.VMEM((R, 8 * K, CAP), F32),
        pltpu.VMEM((96, K * W), BF16),
    ]
    outs = [((48, CAP), BF16), ((48, CAP), BF16), ((R, 3 * K, CAP), F32), ((1, W), F32)]
    return call(edges_kernel, "edges", (plane, got_a, got_b, gathered, *prepared), outs, 0, scratch=scratch, limit=EDGES_LIMIT)


def near(gradient, energy, prepared):
    outs = [((48, CAP), F32), ((4 * R, CAP), F32)]
    scratch = [pltpu.VMEM((48, K * W), BF16)]
    return call(near_kernel, "near", (gradient, energy, *prepared[-2:]), outs, 0, scratch=scratch, limit=EDGES_LIMIT)


def early(mine, keep, own, prepared):
    outs = [((4 * R, CAP), F32), ((4 * R, CAP), F32), ((3, R, CAP), F32), ((R, CAP), F32)]
    return call(early_kernel, "early", (mine, keep, own, prepared[0]), outs, 0, far=2)


def finish(column, got_a, got_b, own, speed, gain):
    outs = [((3, R, CAP), F32)] * 2
    return call(finish_kernel, "finish", (column, got_a, got_b, own, speed, gain), outs, 0, far=2)


def shards(
    frac, velocity, force_old, species, cell_count, neighbours, embed, w_radial_in, w_radial_out, w_node, w_energy
):
    even_x = lax.axis_index("gx") % 2 == 0
    even_z = lax.axis_index("gz") % 2 == 0
    vectors = (3, R, CAP)
    count = cell_count.reshape(R)
    wnt = w_node.T
    send_a, send_b, mine, keep = begin(
        frac.reshape(vectors), velocity.reshape(vectors), force_old.reshape(vectors), species.reshape(R, CAP)
    )
    side, *prepared = prepare(
        count, neighbours.reshape(K * R, CAP), embed, w_radial_in, w_radial_out, wnt, w_energy.reshape(1, CH)
    )

    got_a, got_b = swap(send_a, "gz", False), swap(send_b, "gz", True)
    column = jnp.concatenate(
        [jnp.where(even_z, got_b, got_a), mine, jnp.where(even_z, got_a, got_b)], axis=0
    )
    got_a, got_b = swap(column, "gx", False), swap(column, "gx", True)
    plane = jnp.concatenate(
        [jnp.where(side > 0.5, got_b, got_a), column, jnp.where(side > 0.5, got_a, got_b)], axis=0
    )
    gathered = middle(plane, prepared)
    got_a, got_b = swap(plane, "gy", False), swap(plane, "gy", True)

    send_a, send_b, gradient, energy = edges(plane, got_a, got_b, gathered, prepared)
    plane, own = near(gradient, energy, prepared)
    speed, gain, next_frac, energy = early(mine, keep, own, prepared)
    got_b, got_a = swap(send_b, "gy", True), swap(send_a, "gy", False)
    plane = plane + got_b.astype(F32)
    plane = lax.optimization_barrier(plane)
    plane = plane + got_a.astype(F32)
    lower, column, upper = plane[0:16], plane[16:32], plane[32:48]
    send_a, send_b = jnp.where(even_x, upper, lower), jnp.where(even_x, lower, upper)
    got_b, got_a = swap(send_b, "gx", True), swap(send_a, "gx", False)
    column = column + got_b
    column = lax.optimization_barrier(column)
    column = column + got_a
    send_a = jnp.where(even_z, column[12:16], column[0:4])
    send_b = jnp.where(even_z, column[0:4], column[12:16])
    got_a, got_b = swap(send_a, "gz", False), swap(send_b, "gz", True)
    next_velocity, next_force = finish(column, got_a, got_b, own, speed, gain)
    return (
        next_frac.reshape(frac.shape),
        next_velocity.reshape(frac.shape),
        next_force.reshape(frac.shape),
        energy.reshape(species.shape),
    )


def solution(mesh):
    cells = P(None, "gx", "gy", "gz", None)
    in_specs = (
        cells, cells, cells, P("gx", "gy", "gz", None), P("gx", "gy", "gz"), cells, P(), P(), P(), P(), P(),
    )
    out_specs = (cells, cells, cells, P("gx", "gy", "gz", None))
    return jax.shard_map(shards, mesh=mesh, in_specs=in_specs, out_specs=out_specs, check_vma=False)
```

```python
import jax
import jax.numpy as jnp
from jax import lax
from jax.experimental import pallas as pl
from jax.experimental.pallas import tpu as pltpu
from jax.sharding import PartitionSpec as P

MASSES = (1.008, 12.011, 14.007, 15.999, 32.06, 22.99, 35.45, 39.098, 24.305, 40.078)
SQRT3 = 1.7320508075688772
HALF_SQRT3 = 0.8660254037844386
TIME_STEP = 0.5

K = 16
CAP = 128
R = 2
W = R * CAP
CH = 64
NB = 8
GROUP = 8
EDGES_LIMIT = 40 << 20
F32 = jnp.float32
BF16 = jnp.bfloat16


def swap(array, axis, odd):
    n = lax.axis_size(axis)
    if odd:
        pairs = [(i, (i + 1) % n if i % 2 else (i - 1) % n) for i in range(n)]
    else:
        pairs = [(i, i ^ 1) for i in range(n)]
    return lax.ppermute(array, axis, pairs)


def rows8(row, width):
    return jnp.broadcast_to(row, (8, width))


def wide(ref, row, height):
    parts = [jnp.broadcast_to(ref[r, pl.ds(row, 1), :], (height, CAP)) for r in range(R)]
    return jnp.concatenate(parts, axis=1)


def begin_kernel(frac_ref, vel_ref, force_ref, kind_ref, send_a_ref, send_b_ref, mine_ref, keep_ref):
    kind = kind_ref[...]
    mass = jnp.zeros((R, CAP), F32)
    for number, value in enumerate(MASSES):
        mass = jnp.where(kind == number, jnp.float32(value) / jnp.float32(16.0), mass)
    for c in range(3):
        half = vel_ref[c] + 0.5 * TIME_STEP * force_ref[c] / mass
        moved = frac_ref[c] + TIME_STEP * half
        for r in range(R):
            mine_ref[r * 4 + c:r * 4 + c + 1, :] = moved[r:r + 1]
            keep_ref[r * 4 + c:r * 4 + c + 1, :] = half[r:r + 1]
    for r in range(R):
        mine_ref[r * 4 + 3:r * 4 + 4, :] = kind[r:r + 1].astype(F32)
        keep_ref[r * 4 + 3:r * 4 + 4, :] = mass[r:r + 1]
    even = lax.axis_index("gz") % 2 == 0
    send_a_ref[...] = jnp.where(even, mine_ref[4:8, :], mine_ref[0:4, :])
    send_b_ref[...] = jnp.where(even, mine_ref[0:4, :], mine_ref[4:8, :])


def early_kernel(mine_ref, keep_ref, own_ref, occ_ref, speed_ref, gain_ref, frac_ref, energy_ref):
    for r in range(R):
        occupied = occ_ref[:, r * CAP:(r + 1) * CAP]
        keep = keep_ref[r * 4:r * 4 + 4, :]
        gain = occupied * (0.5 * TIME_STEP) / keep[3:4]
        own = own_ref[r * 4:r * 4 + 4, :]
        place = occupied * mine_ref[r * 4:r * 4 + 4, :]
        speed_ref[r * 4:r * 4 + 4, :] = occupied * keep
        gain_ref[r * 4:r * 4 + 4, :] = jnp.concatenate([gain, occupied, gain, occupied], axis=0)
        for c in range(3):
            frac_ref[c, r:r + 1, :] = place[c:c + 1]
        energy_ref[r:r + 1, :] = own[3:4]


def finish_kernel(mid_ref, got_a_ref, got_b_ref, own_ref, speed_ref, gain_ref, vel_ref, force_ref):
    even = lax.axis_index("gz") % 2 == 0
    got = (
        jnp.where(even, got_b_ref[...], got_a_ref[...]),
        jnp.where(even, got_a_ref[...], got_b_ref[...]),
    )
    for r in range(R):
        gain = gain_ref[r * 4:r * 4 + 1, :]
        occupied = gain_ref[r * 4 + 1:r * 4 + 2, :]
        force = mid_ref[4 * (r + 1):4 * (r + 2), :] + own_ref[r * 4:r * 4 + 4, :] + got[r]
        speed = speed_ref[r * 4:r * 4 + 4, :] + gain * force
        force = occupied * force
        for c in range(3):
            force_ref[c, r:r + 1, :] = force[c:c + 1]
            vel_ref[c, r:r + 1, :] = speed[c:c + 1]


def prepare_kernel(
    count_ref, codes_ref, emb_ref, w1_ref, w2_ref, wnt_ref, we_ref,
    side_ref, occ_ref, web_ref, w1c_ref, w2c_ref, wntc_ref, wc_ref, w2t_ref, wn_ref, embt_ref, off_ref, slot_ref, cell_ref, pick_ref,
):
    side_ref[...] = jnp.where(lax.axis_index("gz") % 2 == 0, jnp.ones((4, CAP), F32), jnp.zeros((4, CAP), F32))
    slot_number = lax.broadcasted_iota(jnp.int32, (1, CAP), 1)
    for r in range(R):
        occ_ref[:, r * CAP:(r + 1) * CAP] = jnp.where(slot_number < count_ref[r], 1.0, 0.0)
    web_ref[...] = jnp.broadcast_to(we_ref[...], (CAP, CH)).T
    w1c_ref[...] = w1_ref[...]
    w2c_ref[...] = w2_ref[...]
    wntc_ref[...] = wnt_ref[...]
    wc_ref[...] = jnp.zeros(wc_ref.shape, BF16)
    wc_ref[0:CH, 0:NB] = w1_ref[...].astype(F32).T.astype(BF16)
    emb = jnp.concatenate([emb_ref[...].astype(F32), jnp.zeros((6, CH), F32)], axis=0)
    embt = emb.T.astype(BF16)
    wc_ref[CH:, NB:NB + 16] = embt
    embt_ref[...] = embt
    w2t_ref[...] = w2_ref[...].astype(F32).T.astype(BF16)
    wn_ref[...] = wnt_ref[...].astype(F32).T.astype(BF16)
    row_cell = lax.broadcasted_iota(jnp.int32, (144, CAP), 0) // 4
    slots = lax.broadcasted_iota(jnp.int32, (CAP, CAP), 1).astype(F32)
    for r in range(R):
        code = codes_ref[pl.ds(r, K, stride=R), :]
        off = code // CAP
        slot = code % CAP
        off_ref[r] = off
        slot_ref[r] = slot
        cell = (off // 3 % 3 * 3 + off // 9) * 4 + off % 3 + r
        slot_rows = jnp.concatenate([slot.astype(F32), jnp.zeros((CAP - K, CAP), F32)], axis=0).T
        for k in range(K):
            lanes = slice(k * W + r * CAP, k * W + (r + 1) * CAP)
            cell_ref[:, lanes] = jnp.where(jnp.broadcast_to(cell[k:k + 1], (144, CAP)) == row_cell, 1.0, 0.0).astype(BF16)
            pick_ref[lanes, :] = jnp.where(slot_rows[:, k:k + 1] == slots, 1.0, 0.0).astype(BF16)


def gather_plane(off_ref, slot_ref, table_ref, base, oy, acc):
    offs = [[off_ref[r, h * 8:(h + 1) * 8, :] for h in range(2)] for r in range(R)]
    slots = [[slot_ref[r, h * 8:(h + 1) * 8, :] for h in range(2)] for r in range(R)]
    acc = list(acc)
    for ox in range(3):
        for zz in range(4):
            at = base + ox * 16 + zz * 4
            rows = [rows8(table_ref[at + q:at + q + 1, :], CAP) for q in range(4)]
            for r in range(R):
                oz = zz - r
                if not 0 <= oz <= 2:
                    continue
                for h in range(2):
                    hit = offs[r][h] == ox * 9 + oy * 3 + oz
                    for q in range(4):
                        got = jnp.take_along_axis(rows[q], slots[r][h], axis=1, mode="promise_in_bounds")
                        n = (r * 2 + h) * 4 + q
                        acc[n] = jnp.where(hit, got, acc[n])
    return offs, acc


def middle_kernel(plane_ref, off_ref, slot_ref, gathered_ref):
    _, acc = gather_plane(off_ref, slot_ref, plane_ref, 0, 1, [jnp.zeros((8, CAP), F32)] * 16)
    for n in range(16):
        gathered_ref[n * 8:(n + 1) * 8, :] = acc[n]


def edges_kernel(
    plane_ref, got_a_ref, got_b_ref, gathered_ref, occ_ref, web_ref, w1_ref, w2_ref, wnt_ref, wc_ref, w2t_ref, wn_ref, embt_ref, off_ref, slot_ref, cell_ref, pick_ref,
    send_a_ref, send_b_ref, g_s, energy_ref,
    pos_s, d_s, kd_s, ey_s, eyb_s, exu_s, ds_s, feat_s, q_s, qb_s, m_s, mb_s, gr_s, t_s, ts_s, a_s,
):
    even = lax.axis_index("gy") % 2 == 0
    pos_s[0:48] = jnp.where(even, got_b_ref[...], got_a_ref[...])
    pos_s[48:96] = jnp.where(even, got_a_ref[...], got_b_ref[...])
    acc = [gathered_ref[at * 8:(at + 1) * 8, :] for at in range(16)]
    offs, acc = gather_plane(off_ref, slot_ref, pos_s, 0, 0, acc)
    offs, acc = gather_plane(off_ref, slot_ref, pos_s, 48, 2, acc)
    for r in range(R):
        own = [plane_ref[16 + (1 + r) * 4 + c:16 + (1 + r) * 4 + c + 1, :] for c in range(3)]
        for h in range(2):
            off = offs[r][h]
            shift = (off // 9 - 1, off // 3 % 3 - 1, off % 3 - 1)
            for c in range(3):
                value = shift[c].astype(F32) + acc[(r * 2 + h) * 4 + c] - rows8(own[c], CAP)
                d_s[r, c * K + h * 8:c * K + h * 8 + 8, :] = value
            kd_s[r, h * 8:h * 8 + 8, :] = acc[(r * 2 + h) * 4 + 3]

    centre = lax.broadcasted_iota(jnp.int32, (8, W), 0).astype(F32) / (NB - 1)
    kinds16 = lax.broadcasted_iota(jnp.int32, (16, W), 0).astype(F32)

    def radial_group(group, _):
        inputs = []
        for j in range(GROUP):
            k = group * GROUP + j
            x = wide(d_s, k, 8)
            y = wide(d_s, K + k, 8)
            z = wide(d_s, 2 * K + k, 8)
            xx, yy, zz = x * x, y * y, z * z
            s = xx + yy + zz
            m1 = jnp.maximum(1.0 - s, 0.0)
            env = m1 * m1 * m1
            u = s - centre
            ex = jnp.exp(-float((NB - 1) ** 2) * (u * u))
            at = k * 8
            exu_s[pl.ds(at, 8), :] = ex * (u * (-2.0 * float((NB - 1) ** 2)))
            ex3 = env * SQRT3
            terms = (
                env, env * x, env * y, env * z, ex3 * (x * y), ex3 * (y * z), ex3 * (z * x),
                (env * HALF_SQRT3) * (xx - yy), (env * 0.5) * (2.0 * zz - xx - yy),
            )
            for m in range(9):
                ey_s[m, pl.ds(at, 8), :] = terms[m]
                eyb_s[m, k * 16:(k + 1) * 16, :] = jnp.concatenate([terms[m]] * 2, axis=0).astype(BF16)
            kind = wide(kd_s, k, 16)
            onehot = jnp.where(kind == kinds16, 1.0, 0.0)
            inputs.append(jnp.concatenate([ex, onehot], axis=0))
        rhs = jnp.concatenate(inputs, axis=1).astype(BF16)
        lanes = pl.ds(group * (GROUP * W), GROUP * W)
        first = jnp.dot(wc_ref[...], rhs, preferred_element_type=F32)
        pre = first[:CH]
        feat = first[CH:]
        sig = 0.5 * jnp.tanh(0.5 * pre) + 0.5
        hidden = (pre * sig).astype(BF16)
        ds_s[:, lanes] = sig * (1.0 + pre * (1.0 - sig))
        feat_s[:, lanes] = feat.astype(BF16)
        radial = jnp.dot(w2t_ref[...], hidden, preferred_element_type=F32)
        for deg in range(3):
            carried = radial[deg * CH:(deg + 1) * CH] * feat
            q_s[deg * CH:(deg + 1) * CH, lanes] = carried
            qb_s[deg * CH:(deg + 1) * CH, lanes] = carried.astype(BF16)
        return 0

    for group in range(K // GROUP):
        radial_group(group, 0)

    def message_block(cb, _):
        base = cb * 16
        for r in range(R):
            sums = [None] * 9
            for k in range(K):
                lo = k * W + r * CAP
                q = [q_s[pl.ds(deg * CH + base, 16), lo:lo + CAP] for deg in range(3)]
                for m in range(9):
                    weight = ey_s[m, k * 8:(k + 1) * 8, r * CAP:(r + 1) * CAP]
                    weight = jnp.concatenate([weight, weight], axis=0)
                    term = q[0 if m == 0 else 1 if m < 4 else 2] * weight
                    sums[m] = term if sums[m] is None else sums[m] + term
            for m in range(9):
                m_s[m, pl.ds(base, 16), r * CAP:(r + 1) * CAP] = sums[m]
        return 0

    for cb in range(CH // 16):
        message_block(cb, 0)

    own_kind = jnp.concatenate(
        [jnp.broadcast_to(plane_ref[16 + (1 + r) * 4 + 3:16 + (1 + r) * 4 + 4, :], (16, CAP)) for r in range(R)], axis=1
    )
    own_feat = jnp.dot(
        embt_ref[...], jnp.where(own_kind == kinds16, 1.0, 0.0).astype(BF16), preferred_element_type=F32
    )
    occupied = occ_ref[...]
    vec = m_s[1] * m_s[1] + m_s[2] * m_s[2] + m_s[3] * m_s[3]
    ten = m_s[4] * m_s[4] + m_s[5] * m_s[5] + m_s[6] * m_s[6] + m_s[7] * m_s[7] + m_s[8] * m_s[8]
    invariant = jnp.concatenate([m_s[0], vec, ten, own_feat], axis=0).astype(BF16)
    pre = jnp.dot(wnt_ref[...], invariant, preferred_element_type=F32)
    sig = 0.5 * jnp.tanh(0.5 * pre) + 0.5
    we = jnp.concatenate([web_ref[...]] * R, axis=1)
    energy = jnp.sum(we * (pre * sig), axis=0, keepdims=True) * occupied
    gpre = we * occupied * (sig * (1.0 + pre * (1.0 - sig)))
    ginv = jnp.dot(wn_ref[0:3 * CH, :], gpre.astype(BF16), preferred_element_type=F32).astype(BF16).astype(F32)
    mb_s[0] = ginv[:CH].astype(BF16)
    gvec = 2.0 * ginv[CH:2 * CH]
    gten = 2.0 * ginv[2 * CH:]
    for m in range(1, 9):
        mb_s[m] = (m_s[m] * (gvec if m < 4 else gten)).astype(BF16)

    def carried_back(k, _):
        at = k * 8
        for r in range(R):
            cols = slice(r * CAP, (r + 1) * CAP)
            lanes = pl.ds(k * W + r * CAP, CAP)
            weight = [eyb_s[m, k * 16:(k + 1) * 16, cols] for m in range(9)]
            sums = [None] * 9
            for cb in range(CH // 16):
                feat = feat_s[cb * 16:(cb + 1) * 16, lanes]
                q = [qb_s[deg * CH + cb * 16:deg * CH + (cb + 1) * 16, lanes] for deg in range(3)]
                back = [None] * 3
                for m in range(9):
                    deg = 0 if m == 0 else 1 if m < 4 else 2
                    cot = mb_s[m, cb * 16:(cb + 1) * 16, cols]
                    term = cot * q[deg]
                    sums[m] = term if sums[m] is None else sums[m] + term
                    term = cot * weight[m]
                    back[deg] = term if back[deg] is None else back[deg] + term
                for deg in range(3):
                    gr_s[deg * CH + cb * 16:deg * CH + (cb + 1) * 16, lanes] = back[deg] * feat
            for m in range(9):
                both = sums[m].astype(F32)
                t_s[r, m, pl.ds(at, 8), :] = both[:8] + both[8:]
        return 0

    for k in range(K):
        carried_back(k, 0)

    def radial_back(group, _):
        lanes = pl.ds(group * (GROUP * W), GROUP * W)
        ghid = jnp.dot(w2_ref[...], gr_s[:, lanes], preferred_element_type=F32)
        gpre = (ghid.astype(BF16).astype(F32) * ds_s[:, lanes]).astype(BF16)
        gbas = jnp.dot(w1_ref[...], gpre, preferred_element_type=F32).astype(BF16).astype(F32)
        for j in range(GROUP):
            at = (group * GROUP + j) * 8
            for r in range(R):
                lo = j * W + r * CAP
                ts_s[r, pl.ds(at, 8), :] = gbas[:, lo:lo + CAP] * exu_s[pl.ds(at, 8), r * CAP:(r + 1) * CAP]
        return 0

    for group in range(K // GROUP):
        radial_back(group, 0)

    def total(ref):
        out = ref[pl.ds(0, K, stride=8), :]
        for sub in range(1, 8):
            out = out + ref[pl.ds(sub, K, stride=8), :]
        return out

    for r in range(R):
        cols = slice(r * CAP, (r + 1) * CAP)
        x, y, z = d_s[r, 0:K, :], d_s[r, K:2 * K, :], d_s[r, 2 * K:3 * K, :]
        xx, yy, zz = x * x, y * y, z * z
        s = xx + yy + zz
        m1 = jnp.maximum(1.0 - s, 0.0)
        env = m1 * m1 * m1
        t = [total(t_s.at[r, m]) for m in range(9)]
        harm = (
            None, x, y, z, SQRT3 * (x * y), SQRT3 * (y * z), SQRT3 * (z * x),
            HALF_SQRT3 * (xx - yy), 0.5 * (2.0 * zz - xx - yy),
        )
        genv = t[0]
        for m in range(1, 9):
            genv = genv + harm[m] * t[m]
        gs2 = 2.0 * (total(ts_s.at[r]) - 3.0 * (m1 * m1) * genv)
        e = [env * v for v in t]
        gx = e[1] + SQRT3 * (y * e[4] + z * e[6]) + x * (SQRT3 * e[7] - e[8] + gs2)
        gy = e[2] + SQRT3 * (x * e[4] + z * e[5]) + y * (gs2 - SQRT3 * e[7] - e[8])
        gz = e[3] + SQRT3 * (y * e[5] + x * e[6]) + z * (2.0 * e[8] + gs2)
        for c, g in enumerate((gx, gy, gz)):
            g_s[r, c * K:(c + 1) * K, :] = g
    energy_ref[...] = energy

    scatter_inputs(g_s, cell_ref, a_s, ((0, 0), (96, 48)))
    out = jnp.dot(a_s[...], pick_ref[...], preferred_element_type=F32)
    send_a_ref[...] = jnp.where(even, out[48:96], out[0:48]).astype(BF16)
    send_b_ref[...] = jnp.where(even, out[0:48], out[48:96]).astype(BF16)


def scatter_inputs(g_ref, cell_ref, a_ref, blocks):
    comp = lax.broadcasted_iota(jnp.int32, (16, CAP), 0) % 4
    for k in range(K):
        for r in range(R):
            lanes = slice(k * W + r * CAP, k * W + (r + 1) * CAP)
            gx, gy, gz = (jnp.broadcast_to(g_ref[r, c * K + k:c * K + k + 1, :], (16, CAP)) for c in range(3))
            mixed = jnp.where(comp == 0, gx, jnp.where(comp == 1, gy, jnp.where(comp == 2, gz, 0.0)))
            mixed = (-mixed).astype(BF16)
            for take, put in blocks:
                for j in range(0, 48, 16):
                    a_ref[put + j:put + j + 16, lanes] = cell_ref[take + j:take + j + 16, lanes] * mixed


def near_kernel(g_ref, energy_ref, cell_ref, pick_ref, mid_ref, own_ref, a_s):
    scatter_inputs(g_ref, cell_ref, a_s, ((48, 0),))
    mid_ref[...] = jnp.dot(a_s[...], pick_ref[...], preferred_element_type=F32)
    for r in range(R):
        for c in range(3):
            own_ref[r * 4 + c:r * 4 + c + 1, :] = jnp.sum(g_ref[r, c * K:(c + 1) * K, :], axis=0, keepdims=True)
        own_ref[r * 4 + 3:r * 4 + 4, :] = energy_ref[:, r * CAP:(r + 1) * CAP]


VMEM = pl.BlockSpec(memory_space=pltpu.VMEM)
SMEM = pl.BlockSpec(memory_space=pltpu.SMEM)


def call(kernel, name, args, outs, near, far=0, smem=0, scratch=(), limit=None):
    args = args[:near] + tuple(pltpu.with_memory_space_constraint(a, pltpu.VMEM) for a in args[near:])
    return pl.pallas_call(
        kernel,
        in_specs=[SMEM] * smem + [VMEM] * (len(args) - smem),
        out_specs=[VMEM] * len(outs),
        out_shape=[(pltpu.VMEM if i < len(outs) - far else jax.ShapeDtypeStruct)(*out) for i, out in enumerate(outs)],
        scratch_shapes=list(scratch),
        compiler_params=pltpu.CompilerParams(vmem_limit_bytes=limit),
        name=name,
    )(*args)


def begin(frac, velocity, force_old, species):
    outs = [((4, CAP), F32), ((4, CAP), F32), ((4 * R, CAP), F32), ((4 * R, CAP), F32)]
    return call(begin_kernel, "begin", (frac, velocity, force_old, species), outs, 4)


def prepare(count, codes, embed, w1, w2, wnt, we):
    outs = [
        ((4, CAP), F32), ((1, W), F32), ((CH, CAP), F32), ((NB, CH), BF16), ((CH, 3 * CH), BF16), ((CH, 4 * CH), BF16),
        ((2 * CH, NB + 16), BF16), ((3 * CH, CH), BF16), ((4 * CH, CH), BF16), ((CH, 16), BF16),
        ((R, K, CAP), jnp.int32), ((R, K, CAP), jnp.int32), ((144, K * W), BF16), ((K * W, CAP), BF16),
    ]
    return call(prepare_kernel, "prepare", (count, codes, embed, w1, w2, wnt, we), outs, 7, smem=1)


def middle(plane, prepared):
    outs = [((16 * 8, CAP), F32)]
    return call(middle_kernel, "middle", (plane, *prepared[-4:-2]), outs, 0, limit=EDGES_LIMIT)[0]


def edges(plane, got_a, got_b, gathered, prepared):
    scratch = [
        pltpu.VMEM((96, CAP), F32),
        pltpu.VMEM((R, 3 * K, CAP), F32),
        pltpu.VMEM((R, K, CAP), F32),
        pltpu.VMEM((9, 8 * K, W), F32),
        pltpu.VMEM((9, 16 * K, W), BF16),
        pltpu.VMEM((8 * K, W), F32),
        pltpu.VMEM((CH, K * W), F32),
        pltpu.VMEM((CH, K * W), BF16),
        pltpu.VMEM((3 * CH, K * W), F32),
        pltpu.VMEM((3 * CH, K * W), BF16),
        pltpu.VMEM((9, CH, W), F32),
        pltpu.VMEM((9, CH, W), BF16),
        pltpu.VMEM((3 * CH, K * W), BF16),
        pltpu.VMEM((R, 9, 8 * K, CAP), F32),
        pltpu.VMEM((R, 8 * K, CAP), F32),
        pltpu.VMEM((96, K * W), BF16),
    ]
    outs = [((48, CAP), BF16), ((48, CAP), BF16), ((R, 3 * K, CAP), F32), ((1, W), F32)]
    return call(edges_kernel, "edges", (plane, got_a, got_b, gathered, *prepared), outs, 0, scratch=scratch, limit=EDGES_LIMIT)


def near(gradient, energy, prepared):
    outs = [((48, CAP), F32), ((4 * R, CAP), F32)]
    scratch = [pltpu.VMEM((48, K * W), BF16)]
    return call(near_kernel, "near", (gradient, energy, *prepared[-2:]), outs, 0, scratch=scratch, limit=EDGES_LIMIT)


def early(mine, keep, own, prepared):
    outs = [((4 * R, CAP), F32), ((4 * R, CAP), F32), ((3, R, CAP), F32), ((R, CAP), F32)]
    return call(early_kernel, "early", (mine, keep, own, prepared[0]), outs, 0, far=2)


def finish(column, got_a, got_b, own, speed, gain):
    outs = [((3, R, CAP), F32)] * 2
    return call(finish_kernel, "finish", (column, got_a, got_b, own, speed, gain), outs, 0, far=2)


def shards(
    frac, velocity, force_old, species, cell_count, neighbours, embed, w_radial_in, w_radial_out, w_node, w_energy
):
    even_x = lax.axis_index("gx") % 2 == 0
    even_z = lax.axis_index("gz") % 2 == 0
    vectors = (3, R, CAP)
    count = cell_count.reshape(R)
    wnt = w_node.T
    send_a, send_b, mine, keep = begin(
        frac.reshape(vectors), velocity.reshape(vectors), force_old.reshape(vectors), species.reshape(R, CAP)
    )
    side, *prepared = prepare(
        count, neighbours.reshape(K * R, CAP), embed, w_radial_in, w_radial_out, wnt, w_energy.reshape(1, CH)
    )

    got_a, got_b = swap(send_a, "gz", False), swap(send_b, "gz", True)
    column = jnp.concatenate(
        [jnp.where(side > 0.5, got_b, got_a), mine, jnp.where(side > 0.5, got_a, got_b)], axis=0
    )
    got_a, got_b = swap(column, "gx", False), swap(column, "gx", True)
    low, high = lax.optimization_barrier((jnp.where(even_x, got_b, 0.0), jnp.where(even_x, 0.0, got_b)))
    plane = jnp.concatenate(
        [jnp.where(even_x, low, got_a), column, jnp.where(even_x, got_a, high)], axis=0
    )
    gathered = middle(plane, prepared)
    got_a, got_b = swap(plane, "gy", False), swap(plane, "gy", True)

    send_a, send_b, gradient, energy = edges(plane, got_a, got_b, gathered, prepared)
    plane, own = near(gradient, energy, prepared)
    speed, gain, next_frac, energy = early(mine, keep, own, prepared)
    got_b, got_a = swap(send_b, "gy", True), swap(send_a, "gy", False)
    plane = plane + got_b.astype(F32)
    plane = lax.optimization_barrier(plane)
    plane = plane + got_a.astype(F32)
    lower, column, upper = plane[0:16], plane[16:32], plane[32:48]
    send_a, send_b = jnp.where(even_x, upper, lower), jnp.where(even_x, lower, upper)
    got_b, got_a = swap(send_b, "gx", True), swap(send_a, "gx", False)
    column = column + got_b
    column = lax.optimization_barrier(column)
    column = column + got_a
    send_a = jnp.where(even_z, column[12:16], column[0:4])
    send_b = jnp.where(even_z, column[0:4], column[12:16])
    got_a, got_b = swap(send_a, "gz", False), swap(send_b, "gz", True)
    next_velocity, next_force = finish(column, got_a, got_b, own, speed, gain)
    return (
        next_frac.reshape(frac.shape),
        next_velocity.reshape(frac.shape),
        next_force.reshape(frac.shape),
        energy.reshape(species.shape),
    )


def solution(mesh):
    cells = P(None, "gx", "gy", "gz", None)
    in_specs = (
        cells, cells, cells, P("gx", "gy", "gz", None), P("gx", "gy", "gz"), cells, P(), P(), P(), P(), P(),
    )
    out_specs = (cells, cells, cells, P("gx", "gy", "gz", None))
    return jax.shard_map(shards, mesh=mesh, in_specs=in_specs, out_specs=out_specs, check_vma=False)
```
